32 devices in a mesh: groups: 2 (over y), space: 16 (over z, x, core).
Axes of the slice: x: 2, y: 2, z: 4, core: 2. Of those that a mesh axis runs over, the one named last changes fastest.
Arguments:
- features: bfloat16 [64, 128, 2048], P(None, 'space', 'groups'), parts along dimension 2, may hold values from -6 to 6
- cotangent: bfloat16 [64, 128, 2048], P(None, 'space', 'groups'), parts along dimension 2, may hold values from -6 to 6
- kernels: bfloat16 [2, 2, 64, 576], replicated, may hold values from -0.25 to 0.25
Outputs:
- section_output: bfloat16 [64, 128, 2048], P(None, 'space', 'groups'), parts along dimension 2
- input_grad: bfloat16 [64, 128, 2048], P(None, 'space', 'groups'), parts along dimension 2
- kernel_grad: float32 [4, 2, 64, 576], P('groups'), parts along dimension 0
The draws below stay inside these ranges and needn't reach their ends.
There are 2 independent parts, one for each index of `groups`. The reference program is written for one: setup_inputs(seed, part) draws one part's arguments, and reference() takes and returns one part's arrays. A program takes and returns all parts, laid end to end along the dimension named above; an argument that names none is the same for every part. Nothing has to cross between parts.
All inputs are finite; a program needn't handle non-finite values.
Results may differ from the reference program's by a relative error of at most 0.0085.
The reference program's roundings to bfloat16 on the way count: a program that leaves them out, or rounds other values in their place, can miss the bound.
Values may be sent and summed in bfloat16 or wider, within the bound.
No kernel may reach another device: no remote copies, remote signals or barrier semaphores. Data moves between devices by JAX's collectives and lax.ppermute only.
A program may use at most 128 MiB of HBM per device.

```python
import math
import jax
import jax.numpy as jnp

CHAN = 64
SECTIONS = 2
WIDTH = 1024
HEIGHT = 128


def block_levels(stream_key, dims, cuts, smallest, high):
    gain, own = 1.0, jax.random.fold_in(stream_key, 6)
    for axis_at, parts in cuts:
        draws = jnp.exp(jax.random.uniform(jax.random.fold_in(own, axis_at), (parts,), jnp.float32, smallest / len(cuts), high / len(cuts)))
        gain = gain * jnp.repeat(draws, dims[axis_at] // parts).reshape([-1 if axis == axis_at else 1 for axis in range(len(dims))])
    return gain


def gaussian(own_key, dims, spread, bound, split=(), held_as=jnp.bfloat16):
    drawn = spread * jax.random.normal(own_key, dims, jnp.float32)
    if split:
        drawn = drawn * block_levels(own_key, dims, split, -0.22, 0.18)
    return jnp.clip(drawn, -bound, bound).astype(held_as)


def setup_inputs(seed: int = 0, part: int = 0) -> dict:
    splits = jax.random.split(jax.random.key(seed), 4)
    part_keys = jax.random.split(jax.random.fold_in(splits[3], part), 4)
    features = gaussian(part_keys[0], (CHAN, HEIGHT, WIDTH), 1.0, 6.0, ((1, 16),))
    cotangent = gaussian(part_keys[1], (CHAN, HEIGHT, WIDTH), 1.0, 6.0, ((1, 16),))
    kernels = gaussian(splits[2], (SECTIONS, 2, CHAN, 9 * CHAN), (9 * CHAN) ** -0.5, 0.25)
    return {"features": features, "cotangent": cotangent, "kernels": kernels}


def shifted_columns(field, offset):
    zeros = jnp.zeros(field.shape[:-1] + (1,), field.dtype)
    if offset == 1:
        return jnp.concatenate([field[..., 1:], zeros], axis=-1)
    if offset == -1:
        return jnp.concatenate([zeros, field[..., :-1]], axis=-1)
    return field

def three_columns(field):
    return jnp.concatenate([shifted_columns(field, -1), field, shifted_columns(field, 1)], axis=0)

def convolve(padded, matrix, count):
    chan = padded.shape[0]
    total = None
    for row in range(3):
        stacked = three_columns(padded[:, row:row + count]).astype(jnp.float32)
        block = matrix[:, row * 3 * chan:(row + 1) * 3 * chan].astype(jnp.float32)
        term = jnp.einsum('ok,khw->ohw', block, stacked)
        total = term if total is None else total + term
    return total

def weight_grad(upper, padded):
    count = upper.shape[1]
    pieces = []
    for row in range(3):
        stacked = three_columns(padded[:, row:row + count]).astype(jnp.float32)
        pieces.append(jnp.einsum('ohw,khw->ok', upper.astype(jnp.float32), stacked))
    return jnp.concatenate(pieces, axis=1)

def flipped(matrix):
    chan = matrix.shape[0]
    inner = matrix.reshape(chan, 3, 3, chan)[:, ::-1, ::-1, :]
    return inner.transpose(3, 1, 2, 0).reshape(chan, 9 * chan)

def pad_rows(field):
    return jnp.pad(field, ((0, 0), (1, 1), (0, 0)))

def reference(features, cotangent, kernels):
    height = features.shape[1]
    width = features.shape[2]
    scale = 1.0 / math.sqrt(height * width)
    current = features
    saved = []
    for section in range(SECTIONS):
        in_pad = pad_rows(current)
        hidden = jnp.maximum(convolve(in_pad, kernels[section, 0], height), 0.0).astype(jnp.bfloat16)
        hid_pad = pad_rows(hidden)
        current = (current.astype(jnp.float32) + convolve(hid_pad, kernels[section, 1], height)).astype(jnp.bfloat16)
        saved.append((in_pad, hid_pad))
    grad = cotangent
    section_grads = [None] * SECTIONS
    for section in range(SECTIONS - 1, -1, -1):
        in_pad, hid_pad = saved[section]
        positive = hid_pad[:, 1:-1] > 0
        dmid = jnp.where(positive, convolve(pad_rows(grad), flipped(kernels[section, 1]), height), 0.0).astype(jnp.bfloat16)
        second = scale * weight_grad(grad, hid_pad)
        first = scale * weight_grad(dmid, in_pad)
        grad = (grad.astype(jnp.float32) + convolve(pad_rows(dmid), flipped(kernels[section, 0]), height)).astype(jnp.bfloat16)
        section_grads[section] = jnp.stack([first, second])
    return (current, grad, jnp.stack(section_grads))
```

```python
import functools
import math

import jax
import jax.numpy as jnp
from jax import lax
from jax.experimental import pallas as pl
from jax.experimental.pallas import tpu as pltpu
from jax.sharding import PartitionSpec as P

CHAN = 64
STACK = 3 * CHAN
F32 = jnp.float32
BF16 = jnp.bfloat16
VMEM = pl.BlockSpec(memory_space=pltpu.VMEM)


def call(body, inputs, outs, scratch, flops, nbytes, name):
    return pl.pallas_call(
        body,
        out_shape=outs,
        out_specs=jax.tree.map(lambda _: VMEM, outs),
        in_specs=[VMEM] * inputs,
        scratch_shapes=scratch,
        compiler_params=pltpu.CompilerParams(vmem_limit_bytes=60 << 20),
        cost_estimate=pl.CostEstimate(flops=flops, bytes_accessed=nbytes, transcendentals=0),
        name=name,
    )


def aligned(index, size):
    return pl.ds(pl.multiple_of(index, CHAN), size)


def stacked(field):
    width = field.shape[1]
    lane = lax.broadcasted_iota(jnp.int32, field.shape, 1)
    zero = jnp.zeros_like(field)
    left = jnp.where(lane == 0, zero, pltpu.roll(field, 1, 1))
    right = jnp.where(lane == width - 1, zero, pltpu.roll(field, width - 1, 1))
    return jnp.concatenate([left, field, right], axis=0)


def put(ref, row, field):
    ref[aligned(row * STACK, STACK), :] = stacked(field)


def middle(ref, row):
    return ref[aligned(row * STACK + CHAN, CHAN), :]


def one(ref, row):
    return ref[aligned(row * CHAN, CHAN), :]


def conv_rows(weight_ref, source, count, finish):
    def body(pair, _):
        row = 2 * pair
        total = jnp.dot(
            weight_ref[...],
            source[aligned(row * STACK, 4 * STACK), :],
            preferred_element_type=F32,
        )
        finish(row, total[:CHAN])
        finish(row + 1, total[CHAN:])
        return 0

    lax.fori_loop(0, count // 2, body, 0)


def grad_rows(upper, upper_row, lower, lower_row, count, out_ref):
    def body(row, _):
        left = upper[aligned((row + upper_row) * STACK, STACK), :]
        right = lower[aligned((row + lower_row) * CHAN, STACK), :]
        out_ref[...] += lax.dot_general(
            left, right, (((1,), (1,)), ((), ())), preferred_element_type=F32
        )
        return 0

    out_ref[...] = jnp.zeros_like(out_ref)
    lax.fori_loop(0, count, body, 0)


def rows_first_kernel(rows, x_ref, g_ref, xt_ref, gt_ref, wide):
    for source, target in ((x_ref, xt_ref), (g_ref, gt_ref)):
        value = source[...].astype(F32)
        wide[...] = jnp.swapaxes(value, 0, 1)
        target[...] = wide[...].reshape(target.shape).astype(BF16)


def stack_rows(pieces, target):
    at = 0
    for ref, count in pieces:

        def body(row, _, ref=ref, at=at):
            put(target, row + at, one(ref, row))
            return 0

        lax.fori_loop(0, count, body, 0)
        at += count


def forward_kernel(
    rows, height, x_ref, xlo_ref, xhi_ref, g_ref, glo_ref, ghi_ref, w00, w01, w10, f11, f10,
    hid0_ref, x1_ref, hid1_ref, g1_ref, grad_ref, x3, h3, y3, k3, g3, d3,
):
    first = lax.axis_index("space") * rows

    def inside(row):
        return jnp.logical_and(first + row >= 0, first + row < height)

    stack_rows([(xlo_ref, 4), (x_ref, rows), (xhi_ref, 4)], x3)
    stack_rows([(glo_ref, 2), (g_ref, rows), (ghi_ref, 2)], g3)

    def hidden0(row, total):
        keep = inside(row - 3)
        value = jnp.where(keep, jnp.maximum(total, 0.0), 0.0).astype(BF16)
        put(h3, row, value)

    conv_rows(w00, x3, rows + 6, hidden0)

    def copy0(row, _):
        hid0_ref[aligned(row * CHAN, CHAN), :] = middle(h3, row + 2)
        return 0

    lax.fori_loop(0, rows + 2, copy0, 0)

    def next_x(row, total):
        keep = inside(row - 2)
        value = jnp.where(keep, middle(x3, row + 2).astype(F32) + total, 0.0).astype(BF16)
        put(y3, row, value)

    conv_rows(w01, h3, rows + 4, next_x)

    def copy1(row, _):
        x1_ref[aligned(row * CHAN, CHAN), :] = middle(y3, row + 1)
        return 0

    lax.fori_loop(0, rows + 2, copy1, 0)

    def hidden1(row, total):
        keep = inside(row - 1)
        value = jnp.where(keep, jnp.maximum(total, 0.0), 0.0).astype(BF16)
        hid1_ref[aligned(row * CHAN, CHAN), :] = value

    conv_rows(w10, y3, rows + 2, hidden1)

    def dhidden1(row, total):
        value = jnp.where(one(hid1_ref, row) > 0, total, 0.0).astype(BF16)
        put(d3, row, value)

    conv_rows(f11, g3, rows + 2, dhidden1)

    def next_g(row, total):
        g1_ref[aligned(row * CHAN, CHAN), :] = (one(g_ref, row).astype(F32) + total).astype(BF16)

    conv_rows(f10, d3, rows, next_g)
    grad_rows(d3, 1, x1_ref, 0, rows, grad_ref)


def channels_first(rows, wide, target):
    target[...] = jnp.swapaxes(wide[...], 0, 1).astype(BF16)


def output_kernel(rows, hid1_ref, x1_ref, g_ref, w11, out_ref, grad_ref, k3, g3, wide):
    stack_rows([(g_ref, rows)], g3)
    grad_rows(g3, 0, hid1_ref, 0, rows, grad_ref)
    stack_rows([(hid1_ref, rows + 2)], k3)

    def last_x(row, total):
        wide[row] = one(x1_ref, row + 1).astype(F32) + total

    conv_rows(w11, k3, rows, last_x)
    channels_first(rows, wide, out_ref)


def backward_kernel(
    rows, scale, g1_ref, glo_ref, ghi_ref, hid0_ref, x_ref, xlo_ref, xhi_ref, f01, grad11, grad10,
    dh0_ref, send_ref, g3, d3, xs, grad01, grad00,
):
    stack_rows([(glo_ref, 2), (g1_ref, rows), (ghi_ref, 2)], g3)

    def dhidden0(row, total):
        value = jnp.where(one(hid0_ref, row) > 0, total, 0.0).astype(BF16)
        dh0_ref[aligned(row * CHAN, CHAN), :] = value
        put(d3, row, value)

    conv_rows(f01, g3, rows + 2, dhidden0)
    xs[pl.ds(0, CHAN), :] = one(xlo_ref, 3)
    xs[pl.ds(CHAN, rows * CHAN), :] = x_ref[...]
    xs[pl.ds((rows + 1) * CHAN, CHAN), :] = one(xhi_ref, 0)
    grad_rows(g3, 2, hid0_ref, 0, rows, grad01)
    grad_rows(d3, 1, xs, 0, rows, grad00)
    for section, pair in enumerate(((grad00, grad01), (grad10, grad11))):
        for which, ref in enumerate(pair):
            for a in range(3):
                for b in range(3):
                    block = ref[(2 - b) * CHAN : (3 - b) * CHAN, a * CHAN : (a + 1) * CHAN]
                    at = which * 9 * CHAN + (3 * a + b) * CHAN
                    send_ref[section * CHAN : (section + 1) * CHAN, at : at + CHAN] = block * scale


def input_grad_kernel(rows, dh0_ref, g1_ref, f00, out_ref, d3, wide):
    stack_rows([(dh0_ref, rows + 2)], d3)

    def last_g(row, total):
        wide[row] = one(g1_ref, row).astype(F32) + total

    conv_rows(f00, d3, rows, last_g)
    channels_first(rows, wide, out_ref)


def flipped(matrix):
    inner = matrix.reshape(CHAN, 3, 3, CHAN)[:, ::-1, ::-1, :]
    return inner.transpose(3, 1, 2, 0).reshape(CHAN, 9 * CHAN)


def two_rows(matrix):
    zeros = jnp.zeros((CHAN, STACK), matrix.dtype)
    upper = jnp.concatenate([matrix, zeros], axis=1)
    lower = jnp.concatenate([zeros, matrix], axis=1)
    return jnp.concatenate([upper, lower], axis=0)


def exchange(value, mask, count):
    return lax.ppermute(value, "space", [(d, d ^ mask) for d in range(count)])


def sum_over_space(part):
    count = lax.axis_size("space")
    place = lax.axis_index("space")
    masks = []
    while (1 << len(masks)) < count and len(masks) < 2:
        masks.append(1 << len(masks))
    for mask in masks:
        half = part.shape[0] // 2
        low, high = part[:half], part[half:]
        bit = (place & mask) != 0
        keep = jnp.where(bit, high, low)
        send = jnp.where(bit, low, high).astype(BF16)
        part = keep + exchange(send, mask, count).astype(F32)
    step = 1 << len(masks)
    while step < count:
        send = part.astype(BF16)
        own = send.astype(F32)
        near = exchange(send, step, count).astype(F32)
        if 2 * step < count:
            far = exchange(send, 2 * step, count).astype(F32)
            both = exchange(send, 3 * step, count).astype(F32)
            part = (own + near) + (far + both)
            step *= 4
        else:
            part = own + near
            step *= 2
    done = part.astype(BF16)
    for mask in reversed(masks):
        bit = (place & mask) != 0
        other = exchange(done, mask, count)
        done = jnp.where(
            bit, jnp.concatenate([other, done]), jnp.concatenate([done, other])
        )
    return done.astype(F32)


def local(features, cotangent, kernels):
    rows, width = features.shape[1], features.shape[2]
    count = lax.axis_size("space")
    height = rows * count
    scale = 1.0 / math.sqrt(height * width)
    down = [(i, i + 1) for i in range(count - 1)]
    up = [(i + 1, i) for i in range(count - 1)]

    def shape(n, dtype=BF16):
        return jax.ShapeDtypeStruct((n * CHAN, width), dtype)

    def vmem(n):
        return pltpu.VMEM((n * STACK, width), BF16)

    row_flops = 2 * CHAN * 9 * CHAN * width
    grad = jax.ShapeDtypeStruct((STACK, STACK), F32)
    tile = jax.ShapeDtypeStruct((CHAN, rows, width), BF16)
    wide = pltpu.VMEM((rows, CHAN, width), F32)
    row_bytes = CHAN * width * 2

    x, g = call(
        functools.partial(rows_first_kernel, rows), 2, (shape(rows), shape(rows)), [wide],
        0, 4 * rows * row_bytes, "rows_first",
    )(features, cotangent)
    xlo = lax.ppermute(x[(rows - 4) * CHAN :], "space", down)
    xhi = lax.ppermute(x[: 4 * CHAN], "space", up)
    glo = lax.ppermute(g[(rows - 2) * CHAN :], "space", down)
    ghi = lax.ppermute(g[: 2 * CHAN], "space", up)
    w00, w01, w10, w11 = (two_rows(kernels[s, j]) for s in range(2) for j in range(2))
    f00, f01, f10, f11 = (two_rows(flipped(kernels[s, j])) for s in range(2) for j in range(2))
    hid0, x1, hid1, g1, grad10 = call(
        functools.partial(forward_kernel, rows, height), 11,
        (shape(rows + 2), shape(rows + 2), shape(rows + 2), shape(rows), grad),
        [vmem(rows + 8), vmem(rows + 6), vmem(rows + 4), vmem(2), vmem(rows + 4), vmem(rows + 2)],
        8 * rows * row_flops, 8 * rows * row_bytes, "forward",
    )(x, xlo, xhi, g, glo, ghi, w00, w01, w10, f11, f10)
    g1lo = lax.ppermute(g1[(rows - 2) * CHAN :], "space", down)
    g1hi = lax.ppermute(g1[: 2 * CHAN], "space", up)
    section_output, grad11 = call(
        functools.partial(output_kernel, rows), 4, (tile, grad), [vmem(rows + 2), vmem(rows), wide],
        2 * rows * row_flops, 4 * rows * row_bytes, "output",
    )(hid1, x1, g, w11)
    dh0, send = call(
        functools.partial(backward_kernel, rows, scale), 10,
        (shape(rows + 2), jax.ShapeDtypeStruct((2 * CHAN, 18 * CHAN), F32)),
        [vmem(rows + 4), vmem(rows + 2), pltpu.VMEM(((rows + 2) * CHAN, width), BF16),
         pltpu.VMEM((STACK, STACK), F32), pltpu.VMEM((STACK, STACK), F32)],
        4 * rows * row_flops, 5 * rows * row_bytes, "backward",
    )(g1, g1lo, g1hi, hid0, x, xlo, xhi, f01, grad11, grad10)
    input_grad = call(
        functools.partial(input_grad_kernel, rows), 3, tile, [vmem(rows + 2), wide],
        rows * row_flops, 3 * rows * row_bytes, "input_grad",
    )(dh0, g1, f00)
    total = sum_over_space(send)
    kernel_grad = total.reshape(2, CHAN, 2, 9 * CHAN).transpose(0, 2, 1, 3)
    return (section_output, input_grad, kernel_grad)


def solution(mesh):
    return jax.shard_map(
        local,
        mesh=mesh,
        in_specs=(P(None, "space", "groups"), P(None, "space", "groups"), P()),
        out_specs=(
            P(None, "space", "groups"),
            P(None, "space", "groups"),
            P("groups", None, None, None),
        ),
        check_vma=False,
    )
```

```python
import functools
import math

import jax
import jax.numpy as jnp
from jax import lax
from jax.experimental import pallas as pl
from jax.experimental.pallas import tpu as pltpu
from jax.sharding import PartitionSpec as P

CHAN = 64
STACK = 3 * CHAN
F32 = jnp.float32
BF16 = jnp.bfloat16
VMEM = pl.BlockSpec(memory_space=pltpu.VMEM)


def call(body, operands, outs, scratch, flops, name):
    nbytes = sum(v.size * v.dtype.itemsize for v in (*operands, *outs))
    held = sum(math.prod(v.shape) * jnp.dtype(v.dtype).itemsize for v in scratch)
    return pl.pallas_call(
        body,
        out_shape=outs,
        in_specs=[VMEM] * len(operands),
        out_specs=[VMEM] * len(outs),
        scratch_shapes=scratch,
        compiler_params=pltpu.CompilerParams(vmem_limit_bytes=nbytes + held + (6 << 20)),
        cost_estimate=pl.CostEstimate(flops=flops, bytes_accessed=nbytes, transcendentals=0),
        name=name,
    )(*operands)


def stacked(field):
    width = field.shape[1]
    lane = lax.broadcasted_iota(jnp.int32, field.shape, 1)
    zero = jnp.zeros_like(field)
    left = jnp.where(lane == 0, zero, pltpu.roll(field, 1, 1))
    right = jnp.where(lane == width - 1, zero, pltpu.roll(field, width - 1, 1))
    return jnp.concatenate([left, field, right], axis=0)


def put(ref, row, field):
    ref[row * STACK : (row + 1) * STACK, :] = stacked(field)


def middle(ref, row):
    return ref[row * STACK + CHAN : row * STACK + 2 * CHAN, :]


def one(ref, row):
    return ref[row * CHAN : (row + 1) * CHAN, :]


def stack_rows(pieces, target):
    at = 0
    for ref, count in pieces:
        for row in range(count):
            put(target, at, one(ref, row))
            at += 1


def two_rows(matrix_ref, target):
    target[...] = jnp.zeros_like(target)
    target[:CHAN, : 3 * STACK] = matrix_ref[...]
    target[CHAN:, STACK:] = matrix_ref[...]


def conv_rows(weight_ref, source, count, finish):
    for row in range(0, count, 2):
        total = jnp.dot(
            weight_ref[...],
            source[row * STACK : (row + 4) * STACK, :],
            preferred_element_type=F32,
        )
        finish(row, total[:CHAN])
        finish(row + 1, total[CHAN:])


def grad_rows(upper, upper_row, lower, lower_row, count):
    total = None
    for row in range(0, count, 2):
        left = upper[(row + upper_row) * STACK : (row + upper_row + 2) * STACK, :]
        right = lower[(row + lower_row) * CHAN : (row + lower_row + 4) * CHAN, :]
        term = lax.dot_general(
            left, right, (((1,), (1,)), ((), ())), preferred_element_type=F32
        )
        total = term if total is None else total + term
    return total[:STACK, :STACK] + total[STACK:, CHAN:]


def rows_first(tile_ref, wide, target):
    wide[...] = jnp.swapaxes(tile_ref[...].astype(F32), 0, 1)
    target[...] = wide[...].reshape(target.shape).astype(BF16)


def channels_first(wide, target):
    target[...] = jnp.swapaxes(wide[...], 0, 1).astype(BF16)


def entry_kernel(edge, tile_ref, rows_ref, top_ref, bottom_ref, wide):
    rows_first(tile_ref, wide, rows_ref)
    count = rows_ref.shape[0]
    top_ref[...] = rows_ref[: edge * CHAN, :]
    bottom_ref[...] = rows_ref[count - edge * CHAN :, :]


def forward_kernel(
    rows, height, x_ref, lo_ref, hi_ref, k00, k01, k10, hid0_ref, x1_ref, hid1_ref,
    x3, h3, y3, w00, w01, w10,
):
    first = lax.axis_index("space") * rows

    def inside(row, value):
        if 0 <= row < rows:
            return value
        keep = jnp.logical_and(first + row >= 0, first + row < height)
        return jnp.where(keep, value, 0.0)

    for matrix, target in ((k00, w00), (k01, w01), (k10, w10)):
        two_rows(matrix, target)
    stack_rows([(lo_ref, 4), (x_ref, rows), (hi_ref, 4)], x3)

    def hidden0(row, total):
        value = inside(row - 3, jnp.maximum(total, 0.0)).astype(BF16)
        put(h3, row, value)
        if 2 <= row < rows + 4:
            hid0_ref[(row - 2) * CHAN : (row - 1) * CHAN, :] = value

    conv_rows(w00, x3, rows + 6, hidden0)

    def next_x(row, total):
        value = inside(row - 2, middle(x3, row + 2).astype(F32) + total).astype(BF16)
        put(y3, row, value)
        if 1 <= row < rows + 3:
            x1_ref[(row - 1) * CHAN : row * CHAN, :] = value

    conv_rows(w01, h3, rows + 4, next_x)

    def hidden1(row, total):
        value = inside(row - 1, jnp.maximum(total, 0.0)).astype(BF16)
        hid1_ref[row * CHAN : (row + 1) * CHAN, :] = value

    conv_rows(w10, y3, rows + 2, hidden1)


def backward1_kernel(
    rows, g_ref, lo_ref, hi_ref, hid1_ref, f11, f10, g1_ref, top_ref, bottom_ref, dh1_ref,
    g3, d3, w11, w10,
):
    two_rows(f11, w11)
    two_rows(f10, w10)
    stack_rows([(lo_ref, 2), (g_ref, rows), (hi_ref, 2)], g3)

    def dhidden1(row, total):
        value = jnp.where(one(hid1_ref, row) > 0, total, 0.0).astype(BF16)
        put(d3, row, value)
        if 1 <= row < rows + 1:
            dh1_ref[(row - 1) * CHAN : row * CHAN, :] = value

    conv_rows(w11, g3, rows + 2, dhidden1)

    def next_g(row, total):
        value = (one(g_ref, row).astype(F32) + total).astype(BF16)
        g1_ref[row * CHAN : (row + 1) * CHAN, :] = value
        if row < 2:
            top_ref[row * CHAN : (row + 1) * CHAN, :] = value
        if row >= rows - 2:
            at = row - (rows - 2)
            bottom_ref[at * CHAN : (at + 1) * CHAN, :] = value

    conv_rows(w10, d3, rows, next_g)


def grads1_kernel(rows, g_ref, hid1_ref, dh1_ref, x1_ref, grad10, grad11, s3):
    stack_rows([(g_ref, rows)], s3)
    grad11[...] = grad_rows(s3, 0, hid1_ref, 0, rows)
    stack_rows([(dh1_ref, rows)], s3)
    grad10[...] = grad_rows(s3, 0, x1_ref, 0, rows)


def output_kernel(rows, hid1_ref, x1_ref, k11, out_ref, k3, w11, wide):
    two_rows(k11, w11)
    stack_rows([(hid1_ref, rows + 2)], k3)

    def last_x(row, total):
        wide[row] = one(x1_ref, row + 1).astype(F32) + total

    conv_rows(w11, k3, rows, last_x)
    channels_first(wide, out_ref)


def backward0_kernel(
    rows, scale, g1_ref, lo_ref, hi_ref, hid0_ref, x_ref, xlo_ref, xhi_ref, f01, grad10, grad11,
    dh0_ref, keep_ref, send_ref, g3, d3, xs, w01, both,
):
    two_rows(f01, w01)
    stack_rows([(lo_ref, 2), (g1_ref, rows), (hi_ref, 2)], g3)

    def dhidden0(row, total):
        value = jnp.where(one(hid0_ref, row) > 0, total, 0.0).astype(BF16)
        dh0_ref[row * CHAN : (row + 1) * CHAN, :] = value
        put(d3, row, value)

    conv_rows(w01, g3, rows + 2, dhidden0)
    xs[:CHAN, :] = one(xlo_ref, 3)
    xs[CHAN : (rows + 1) * CHAN, :] = x_ref[...]
    xs[(rows + 1) * CHAN :, :] = one(xhi_ref, 0)
    grad01 = grad_rows(g3, 2, hid0_ref, 0, rows)
    grad00 = grad_rows(d3, 1, xs, 0, rows)
    pairs = ((grad00, grad01), (grad10[...], grad11[...]))
    for section, pair in enumerate(pairs):
        for which, value in enumerate(pair):
            for a in range(3):
                for b in range(3):
                    block = value[(2 - b) * CHAN : (3 - b) * CHAN, a * CHAN : (a + 1) * CHAN]
                    at = which * 9 * CHAN + (3 * a + b) * CHAN
                    both[section, :, at : at + CHAN] = block * scale
    mine = lax.rem(lax.axis_index("space"), 2)
    keep_ref[...] = both[mine]
    send_ref[...] = both[1 - mine].astype(BF16)


def input_grad_kernel(rows, dh0_ref, g1_ref, f00, out_ref, d3, w00, wide):
    two_rows(f00, w00)
    stack_rows([(dh0_ref, rows + 2)], d3)

    def last_g(row, total):
        wide[row] = one(g1_ref, row).astype(F32) + total

    conv_rows(w00, d3, rows, last_g)
    channels_first(wide, out_ref)


def flipped(matrix):
    inner = matrix.reshape(CHAN, 3, 3, CHAN)[:, ::-1, ::-1, :]
    return inner.transpose(3, 1, 2, 0).reshape(CHAN, 9 * CHAN)


def exchange(value, mask, count):
    return lax.ppermute(value, "space", [(d, d ^ mask) for d in range(count)])


def local(features, cotangent, kernels):
    rows, width = features.shape[1], features.shape[2]
    count = lax.axis_size("space")
    height = rows * count
    scale = 1.0 / math.sqrt(height * width)
    place = lax.axis_index("space")
    down = [(i, i + 1) for i in range(count - 1)]
    up = [(i + 1, i) for i in range(count - 1)]

    def shape(n, dtype=BF16):
        return jax.ShapeDtypeStruct((n * CHAN, width), dtype)

    def vmem(n):
        return pltpu.VMEM((n * STACK, width), BF16)

    def ends(top, bottom):
        return lax.ppermute(bottom, "space", down), lax.ppermute(top, "space", up)

    weight = pltpu.VMEM((2 * CHAN, 4 * STACK), BF16)
    row_flops = 2 * CHAN * 9 * CHAN * width * 4
    grad = jax.ShapeDtypeStruct((STACK, STACK), F32)
    tile = jax.ShapeDtypeStruct((CHAN, rows, width), BF16)
    wide = pltpu.VMEM((rows, CHAN, width), F32)
    half = (CHAN, 18 * CHAN)

    x, x_top, x_bottom = call(
        functools.partial(entry_kernel, 4), (features,), (shape(rows), shape(4), shape(4)),
        [wide], 0, "x_rows",
    )
    xlo, xhi = ends(x_top, x_bottom)
    later, _ = lax.optimization_barrier((cotangent, x_top))
    g, g_top, g_bottom = call(
        functools.partial(entry_kernel, 2), (later,), (shape(rows), shape(2), shape(2)),
        [wide], 0, "g_rows",
    )
    glo, ghi = ends(g_top, g_bottom)
    k00, k01, k10, k11 = (kernels[s, j] for s in range(2) for j in range(2))
    f00, f01, f10, f11 = (flipped(kernels[s, j]) for s in range(2) for j in range(2))
    hid0, x1, hid1 = call(
        functools.partial(forward_kernel, rows, height), (x, xlo, xhi, k00, k01, k10),
        (shape(rows + 2),) * 3, [vmem(rows + 8), vmem(rows + 6), vmem(rows + 4)] + [weight] * 3,
        36 * row_flops, "forward",
    )
    g1, g1_top, g1_bottom, dh1 = call(
        functools.partial(backward1_kernel, rows), (g, glo, ghi, hid1, f11, f10),
        (shape(rows), shape(2), shape(2), shape(rows)),
        [vmem(rows + 4), vmem(rows + 2)] + [weight] * 2, 18 * row_flops, "backward1",
    )
    g1lo, g1hi = ends(g1_top, g1_bottom)
    grad10, grad11 = call(
        functools.partial(grads1_kernel, rows), (g, hid1, dh1, x1), (grad, grad), [vmem(rows)],
        16 * row_flops, "grads1",
    )
    dh0, part, send = call(
        functools.partial(backward0_kernel, rows, scale),
        (g1, g1lo, g1hi, hid0, x, xlo, xhi, f01, grad10, grad11),
        (shape(rows + 2), jax.ShapeDtypeStruct(half, F32), jax.ShapeDtypeStruct(half, BF16)),
        [vmem(rows + 4), vmem(rows + 2), pltpu.VMEM(((rows + 2) * CHAN, width), BF16), weight,
         pltpu.VMEM((2, *half), F32)],
        26 * row_flops, "backward0",
    )

    part = part + exchange(send, 1, count).astype(F32)
    low, high = part[: CHAN // 2], part[CHAN // 2 :]
    bit = (place & 2) != 0
    send = jnp.where(bit, low, high).astype(BF16)
    part = jnp.where(bit, high, low)
    arrived = exchange(send, 2, count)
    hid1_later, _ = lax.optimization_barrier((hid1, send))
    (section_output,) = call(
        functools.partial(output_kernel, rows), (hid1_later, x1, k11), (tile,),
        [vmem(rows + 2), weight, wide], 8 * row_flops, "output",
    )
    arrived, section_output = lax.optimization_barrier((arrived, section_output))
    part = part + arrived.astype(F32)
    step = 4
    input_grad = None
    while step < count:
        send = part.astype(BF16)
        masks = [step, 2 * step, 3 * step] if 2 * step < count else [step]
        arrived = [exchange(send, mask, count) for mask in masks]
        if input_grad is None:
            dh0_later, _ = lax.optimization_barrier((dh0, send))
            (input_grad,) = call(
                functools.partial(input_grad_kernel, rows), (dh0_later, g1, f00), (tile,),
                [vmem(rows + 2), weight, wide], 8 * row_flops, "input_grad",
            )
            arrived, input_grad = lax.optimization_barrier((arrived, input_grad))
        own = send.astype(F32)
        arrived = [value.astype(F32) for value in arrived]
        part = own + arrived[0]
        if len(masks) == 3:
            part = part + (arrived[1] + arrived[2])
        step *= len(masks) + 1
    done = part.astype(BF16)
    for mask in (2, 1):
        bit = (place & mask) != 0
        other = exchange(done, mask, count)
        done = jnp.where(
            bit, jnp.concatenate([other, done]), jnp.concatenate([done, other])
        )
    kernel_grad = done.astype(F32).reshape(2, CHAN, 2, 9 * CHAN).transpose(0, 2, 1, 3)
    return (section_output, input_grad, kernel_grad)


def solution(mesh):
    return jax.shard_map(
        local,
        mesh=mesh,
        in_specs=(P(None, "space", "groups"), P(None, "space", "groups"), P()),
        out_specs=(
            P(None, "space", "groups"),
            P(None, "space", "groups"),
            P("groups", None, None, None),
        ),
        check_vma=False,
    )
```

```python
import functools
import math

import jax
import jax.numpy as jnp
from jax import lax
from jax.experimental import pallas as pl
from jax.experimental.pallas import tpu as pltpu
from jax.sharding import PartitionSpec as P

CHAN = 64
STACK = 3 * CHAN
F32 = jnp.float32
BF16 = jnp.bfloat16
VMEM = pl.BlockSpec(memory_space=pltpu.VMEM)
ANY = pl.BlockSpec(memory_space=pl.ANY)
HBM = pl.BlockSpec(memory_space=pltpu.HBM)
PIECES = 4


def call(body, operands, outs, scratch, flops, name, after=(), place=VMEM):
    nbytes = sum(v.size * v.dtype.itemsize for v in (*operands, *outs))
    held = sum(math.prod(v.shape) * v.dtype.itemsize for v in scratch if v.dtype in (F32, BF16))

    def kernel(*refs):
        body(*refs[len(after) :])

    return pl.pallas_call(
        kernel,
        out_shape=outs,
        in_specs=[ANY] * len(after) + [place] * len(operands),
        out_specs=[VMEM] * len(outs),
        scratch_shapes=scratch,
        compiler_params=pltpu.CompilerParams(vmem_limit_bytes=nbytes + held + (6 << 20)),
        cost_estimate=pl.CostEstimate(flops=flops, bytes_accessed=nbytes, transcendentals=0),
        name=name,
    )(*after, *operands)


def stacked(field):
    width = field.shape[1]
    lane = lax.broadcasted_iota(jnp.int32, field.shape, 1)
    zero = jnp.zeros_like(field)
    left = jnp.where(lane == 0, zero, pltpu.roll(field, 1, 1))
    right = jnp.where(lane == width - 1, zero, pltpu.roll(field, width - 1, 1))
    return jnp.concatenate([left, field, right], axis=0)


def put(ref, row, field):
    ref[row * STACK : (row + 1) * STACK, :] = stacked(field)


def middle(ref, row):
    return ref[row * STACK + CHAN : row * STACK + 2 * CHAN, :]


def one(ref, row):
    return ref[row * CHAN : (row + 1) * CHAN, :]


def stack_rows(ref, count, target, at):
    for row in range(count):
        put(target, row + at, one(ref, row))


def two_rows(target, index, column, value):
    width = value.shape[1]
    target[index, :CHAN, column : column + width] = value
    target[index, CHAN:, STACK + column : STACK + column + width] = value


def weights_kernel(kernels_ref, target):
    target[...] = jnp.zeros_like(target)
    line = lax.broadcasted_iota(jnp.int32, (CHAN, CHAN), 0)
    same = line == lax.broadcasted_iota(jnp.int32, (CHAN, CHAN), 1)
    unit = jnp.where(same, 1.0, 0.0).astype(BF16)
    for section in range(2):
        for which in range(2):
            index = 2 * (2 * section + which)
            two_rows(target, index, 0, kernels_ref[section, which])
            for tap in range(9):
                at = (8 - tap) * CHAN
                block = kernels_ref[section, which, :, at : at + CHAN]
                turned = lax.dot_general(
                    unit, block, (((1,), (1,)), ((), ())), preferred_element_type=F32
                )
                two_rows(target, index + 1, tap * CHAN, turned.astype(BF16))


def conv_rows(weight, source, count, finish):
    for row in range(0, count, 2):
        total = jnp.dot(
            weight,
            source[row * STACK : (row + 4) * STACK, :],
            preferred_element_type=F32,
        )
        finish(row, total[:CHAN])
        finish(row + 1, total[CHAN:])


def grad_rows(upper, upper_row, lower, lower_row, count):
    total = None
    for row in range(0, count, 2):
        left = upper[(row + upper_row) * STACK : (row + upper_row + 2) * STACK, :]
        right = lower[(row + lower_row) * CHAN : (row + lower_row + 4) * CHAN, :]
        term = lax.dot_general(
            left, right, (((1,), (1,)), ((), ())), preferred_element_type=F32
        )
        total = term if total is None else total + term
    return total[:STACK, :STACK] + total[STACK:, CHAN:]


def channels_first(wide, target):
    target[...] = jnp.swapaxes(wide[...], 0, 1).astype(BF16)


def odd_place():
    return lax.rem(lax.axis_index("space"), 2) == 1


def put_at(ref, row, field):
    ref[pl.ds(pl.multiple_of(row * STACK, CHAN), STACK), :] = stacked(field)


def halo_rows(near_ref, far_ref, count, rows, target):
    odd = odd_place()
    above, below = 0, rows + count
    near_at = jnp.where(odd, above, below)
    far_at = jnp.where(odd, below, above)
    for row in range(count):
        put_at(target, near_at + row, one(near_ref, row))
        put_at(target, far_at + row, one(far_ref, row))


def send_edges(rows_ref, edge, near_ref, far_ref):
    odd = odd_place()
    last = rows_ref.shape[0] - edge * CHAN
    near_at = jnp.where(odd, 0, last)
    far_at = jnp.where(odd, last, 0)
    near_ref[...] = rows_ref[pl.ds(pl.multiple_of(near_at, CHAN), edge * CHAN), :]
    far_ref[...] = rows_ref[pl.ds(pl.multiple_of(far_at, CHAN), edge * CHAN), :]


def entry_kernel(edge, tile_ref, rows_ref, near_ref, far_ref, held, arrived):
    piece = CHAN // PIECES
    copies = [
        pltpu.make_async_copy(
            tile_ref.at[i * piece : (i + 1) * piece],
            held.at[i * piece : (i + 1) * piece],
            arrived.at[i],
        )
        for i in range(PIECES)
    ]
    for copy in copies:
        copy.start()
    for i, copy in enumerate(copies):
        copy.wait()
        part = held[i * piece : (i + 1) * piece].astype(F32)
        turned = jnp.swapaxes(part, 0, 1).astype(BF16)
        for row in range(turned.shape[0]):
            at = row * CHAN + i * piece
            rows_ref[at : at + piece, :] = turned[row]
    send_edges(rows_ref, edge, near_ref, far_ref)


def channels_first(wide, target):
    target[...] = jnp.swapaxes(wide[...], 0, 1).astype(BF16)


def forward_kernel(
    rows, height, x_ref, near_ref, far_ref, w_ref, hid0_ref, x1_ref, hid1_ref, x3, h3, y3,
):
    first = lax.axis_index("space") * rows

    def inside(row, value):
        if 0 <= row < rows:
            return value
        keep = jnp.logical_and(first + row >= 0, first + row < height)
        return jnp.where(keep, value, 0.0)

    stack_rows(x_ref, rows, x3, 4)
    halo_rows(near_ref, far_ref, 4, rows, x3)

    def hidden0(row, total):
        value = inside(row - 3, jnp.maximum(total, 0.0)).astype(BF16)
        put(h3, row, value)
        if 2 <= row < rows + 4:
            hid0_ref[(row - 2) * CHAN : (row - 1) * CHAN, :] = value

    conv_rows(w_ref[0], x3, rows + 6, hidden0)

    def next_x(row, total):
        value = inside(row - 2, middle(x3, row + 2).astype(F32) + total).astype(BF16)
        put(y3, row, value)
        if 1 <= row < rows + 3:
            x1_ref[(row - 1) * CHAN : row * CHAN, :] = value

    conv_rows(w_ref[2], h3, rows + 4, next_x)

    def hidden1(row, total):
        value = inside(row - 1, jnp.maximum(total, 0.0)).astype(BF16)
        hid1_ref[row * CHAN : (row + 1) * CHAN, :] = value

    conv_rows(w_ref[4], y3, rows + 2, hidden1)


def backward1_kernel(
    rows, g_ref, near_ref, far_ref, hid1_ref, w_ref, g1_ref, next_near, next_far, dh1_ref, g3, d3,
):
    stack_rows(g_ref, rows, g3, 2)
    halo_rows(near_ref, far_ref, 2, rows, g3)

    def dhidden1(row, total):
        value = jnp.where(one(hid1_ref, row) > 0, total, 0.0).astype(BF16)
        put(d3, row, value)
        if 1 <= row < rows + 1:
            dh1_ref[(row - 1) * CHAN : row * CHAN, :] = value

    conv_rows(w_ref[7], g3, rows + 2, dhidden1)

    def next_g(row, total):
        value = (one(g_ref, row).astype(F32) + total).astype(BF16)
        g1_ref[row * CHAN : (row + 1) * CHAN, :] = value

    conv_rows(w_ref[5], d3, rows, next_g)
    send_edges(g1_ref, 2, next_near, next_far)


def grads1_kernel(rows, g_ref, hid1_ref, dh1_ref, x1_ref, grad10, grad11, s3):
    stack_rows(g_ref, rows, s3, 0)
    grad11[...] = grad_rows(s3, 0, hid1_ref, 0, rows)
    stack_rows(dh1_ref, rows, s3, 0)
    grad10[...] = grad_rows(s3, 0, x1_ref, 0, rows)


def output_kernel(rows, hid1_ref, x1_ref, w_ref, out_ref, token, k3, wide):
    token[...] = jnp.zeros_like(token)
    stack_rows(hid1_ref, rows + 2, k3, 0)

    def last_x(row, total):
        wide[row] = one(x1_ref, row + 1).astype(F32) + total

    conv_rows(w_ref[6], k3, rows, last_x)
    channels_first(wide, out_ref)


def backward0_kernel(
    rows, scale, g1_ref, near_ref, far_ref, hid0_ref, x_ref, xnear_ref, xfar_ref, w_ref, grad10, grad11,
    dh0_ref, keep_ref, send_ref, g3, d3, xs, both,
):
    stack_rows(g1_ref, rows, g3, 2)
    halo_rows(near_ref, far_ref, 2, rows, g3)

    def dhidden0(row, total):
        value = jnp.where(one(hid0_ref, row) > 0, total, 0.0).astype(BF16)
        dh0_ref[row * CHAN : (row + 1) * CHAN, :] = value
        put(d3, row, value)

    conv_rows(w_ref[3], g3, rows + 2, dhidden0)
    odd = odd_place()
    xs[CHAN : (rows + 1) * CHAN, :] = x_ref[...]
    near_at, far_at = jnp.where(odd, 0, rows + 1), jnp.where(odd, rows + 1, 0)
    near_row, far_row = jnp.where(odd, 3, 0), jnp.where(odd, 0, 3)
    for ref, at, row in ((xnear_ref, near_at, near_row), (xfar_ref, far_at, far_row)):
        source = pl.ds(pl.multiple_of(row * CHAN, CHAN), CHAN)
        xs[pl.ds(pl.multiple_of(at * CHAN, CHAN), CHAN), :] = ref[source, :]
    grad01 = grad_rows(g3, 2, hid0_ref, 0, rows)
    grad00 = grad_rows(d3, 1, xs, 0, rows)
    pairs = ((grad00, grad01), (grad10[...], grad11[...]))
    for section, pair in enumerate(pairs):
        for which, value in enumerate(pair):
            for a in range(3):
                for b in range(3):
                    block = value[(2 - b) * CHAN : (3 - b) * CHAN, a * CHAN : (a + 1) * CHAN]
                    at = which * 9 * CHAN + (3 * a + b) * CHAN
                    both[section, :, at : at + CHAN] = block * scale
    mine = lax.rem(lax.axis_index("space"), 2)
    keep_ref[...] = both[mine]
    send_ref[...] = both[1 - mine].astype(BF16)


def input_grad_kernel(rows, dh0_ref, g1_ref, w_ref, out_ref, token, d3, wide):
    token[...] = jnp.zeros_like(token)
    stack_rows(dh0_ref, rows + 2, d3, 0)

    def last_g(row, total):
        wide[row] = one(g1_ref, row).astype(F32) + total

    conv_rows(w_ref[1], d3, rows, last_g)
    channels_first(wide, out_ref)


def gathered_kernel(own_ref, other_ref, out_ref):
    mine = lax.rem(lax.axis_index("space"), 2)
    for section, ref in ((mine, own_ref), (1 - mine, other_ref)):
        for which in range(2):
            piece = ref[:, which * 9 * CHAN : (which + 1) * 9 * CHAN]
            out_ref[section, which] = piece.astype(F32)


def exchange(value, mask, count):
    return lax.ppermute(value, "space", [(d, d ^ mask) for d in range(count)])


def local(features, cotangent, kernels):
    rows, width = features.shape[1], features.shape[2]
    count = lax.axis_size("space")
    height = rows * count
    scale = 1.0 / math.sqrt(height * width)
    place = lax.axis_index("space")
    beyond = [(i, i + 1) for i in range(1, count - 1, 2)]
    beyond += [(target, source) for source, target in beyond]

    def shape(n, dtype=BF16):
        return jax.ShapeDtypeStruct((n * CHAN, width), dtype)

    def vmem(n):
        return pltpu.VMEM((n * STACK, width), BF16)

    def neighbours(near, far):
        return exchange(near, 1, count), lax.ppermute(far, "space", beyond)

    row_flops = 2 * CHAN * 9 * CHAN * width * 4
    grad = jax.ShapeDtypeStruct((STACK, STACK), F32)
    tile = jax.ShapeDtypeStruct((CHAN, rows, width), BF16)
    token = jax.ShapeDtypeStruct((8, 128), F32)
    wide = pltpu.VMEM((rows, CHAN, width), F32)
    half = (CHAN, 18 * CHAN)
    entry = [pltpu.VMEM((CHAN, rows, width), BF16), pltpu.SemaphoreType.DMA((PIECES,))]

    x, x_near, x_far = call(
        functools.partial(entry_kernel, 4), (features,), (shape(rows), shape(4), shape(4)),
        entry, 0, "x_rows", place=HBM,
    )
    xnear, xfar = neighbours(x_near, x_far)
    g, g_near, g_far = call(
        functools.partial(entry_kernel, 2), (cotangent,), (shape(rows), shape(2), shape(2)),
        entry, 0, "g_rows", after=(x_near,), place=HBM,
    )
    gnear, gfar = neighbours(g_near, g_far)
    (weights,) = call(
        weights_kernel, (kernels,), (jax.ShapeDtypeStruct((8, 2 * CHAN, 4 * STACK), BF16),), [],
        row_flops, "weights", after=(g_near,),
    )
    hid0, x1, hid1 = call(
        functools.partial(forward_kernel, rows, height), (x, xnear, xfar, weights),
        (shape(rows + 2),) * 3, [vmem(rows + 8), vmem(rows + 6), vmem(rows + 4)],
        36 * row_flops, "forward",
    )
    g1, g1_near, g1_far, dh1 = call(
        functools.partial(backward1_kernel, rows), (g, gnear, gfar, hid1, weights),
        (shape(rows), shape(2), shape(2), shape(rows)),
        [vmem(rows + 4), vmem(rows + 2)], 18 * row_flops, "backward1",
    )
    g1near, g1far = neighbours(g1_near, g1_far)
    grad10, grad11 = call(
        functools.partial(grads1_kernel, rows), (g, hid1, dh1, x1), (grad, grad), [vmem(rows)],
        16 * row_flops, "grads1",
    )
    dh0, part, send = call(
        functools.partial(backward0_kernel, rows, scale),
        (g1, g1near, g1far, hid0, x, xnear, xfar, weights, grad10, grad11),
        (shape(rows + 2), jax.ShapeDtypeStruct(half, F32), jax.ShapeDtypeStruct(half, BF16)),
        [vmem(rows + 4), vmem(rows + 2), pltpu.VMEM(((rows + 2) * CHAN, width), BF16),
         pltpu.VMEM((2, *half), F32)],
        26 * row_flops, "backward0",
    )

    part = part + exchange(send, 1, count).astype(F32)
    low, high = part[: CHAN // 2], part[CHAN // 2 :]
    bit = (place & 2) != 0
    send = jnp.where(bit, low, high).astype(BF16)
    part = jnp.where(bit, high, low)
    arrived = exchange(send, 2, count)
    section_output, mark = call(
        functools.partial(output_kernel, rows), (hid1, x1, weights), (tile, token),
        [vmem(rows + 2), wide], 8 * row_flops, "output", after=(send, dh0, g1),
    )
    part = part + (arrived.astype(F32) + mark[0, 0])
    step = 4
    input_grad = None
    while step < count:
        send = part.astype(BF16)
        masks = [step, 2 * step, 3 * step] if 2 * step < count else [step]
        arrived = [exchange(send, mask, count) for mask in masks]
        if input_grad is None:
            input_grad, mark = call(
                functools.partial(input_grad_kernel, rows), (dh0, g1, weights), (tile, token),
                [vmem(rows + 2), wide], 8 * row_flops, "input_grad", after=(send,),
            )
        own = send.astype(F32) + mark[0, 0]
        arrived = [value.astype(F32) for value in arrived]
        part = own + arrived[0]
        if len(masks) == 3:
            part = part + (arrived[1] + arrived[2])
        step *= len(masks) + 1
    done = part.astype(BF16)
    bit = (place & 2) != 0
    other = exchange(done, 2, count)
    done = jnp.where(bit, jnp.concatenate([other, done]), jnp.concatenate([done, other]))
    (kernel_grad,) = call(
        gathered_kernel, (done, exchange(done, 1, count)),
        (jax.ShapeDtypeStruct((2, 2, CHAN, 9 * CHAN), F32),), [], 0, "gathered",
    )
    return (section_output, input_grad, kernel_grad)


def solution(mesh):
    return jax.shard_map(
        local,
        mesh=mesh,
        in_specs=(P(None, "space", "groups"), P(None, "space", "groups"), P()),
        out_specs=(
            P(None, "space", "groups"),
            P(None, "space", "groups"),
            P("groups", None, None, None),
        ),
        check_vma=False,
    )
```

```python
import functools
import math

import jax
import jax.numpy as jnp
from jax import lax
from jax.experimental import pallas as pl
from jax.experimental.pallas import tpu as pltpu
from jax.sharding import PartitionSpec as P

CHAN = 64
STACK = 3 * CHAN
F32 = jnp.float32
BF16 = jnp.bfloat16
VMEM = pl.BlockSpec(memory_space=pltpu.VMEM)
ANY = pl.BlockSpec(memory_space=pl.ANY)
HBM = pl.BlockSpec(memory_space=pltpu.HBM)
PIECES = 4


def call(body, operands, outs, scratch, flops, name, after=(), place=VMEM):
    nbytes = sum(v.size * v.dtype.itemsize for v in (*operands, *outs))
    held = sum(math.prod(v.shape) * v.dtype.itemsize for v in scratch if v.dtype in (F32, BF16))

    def kernel(*refs):
        body(*refs[len(after) :])

    return pl.pallas_call(
        kernel,
        out_shape=outs,
        in_specs=[ANY] * len(after) + [place] * len(operands),
        out_specs=[VMEM] * len(outs),
        scratch_shapes=scratch,
        compiler_params=pltpu.CompilerParams(vmem_limit_bytes=nbytes + held + (6 << 20)),
        cost_estimate=pl.CostEstimate(flops=flops, bytes_accessed=nbytes, transcendentals=0),
        name=name,
    )(*after, *operands)


def stacked(field):
    width = field.shape[1]
    lane = lax.broadcasted_iota(jnp.int32, field.shape, 1)
    zero = jnp.zeros_like(field)
    left = jnp.where(lane == 0, zero, pltpu.roll(field, 1, 1))
    right = jnp.where(lane == width - 1, zero, pltpu.roll(field, width - 1, 1))
    return jnp.concatenate([left, field, right], axis=0)


def put(ref, row, field):
    ref[row * STACK : (row + 1) * STACK, :] = stacked(field)


def middle(ref, row):
    return ref[row * STACK + CHAN : row * STACK + 2 * CHAN, :]


def one(ref, row):
    return ref[row * CHAN : (row + 1) * CHAN, :]


def stack_rows(ref, rows, target, at):
    for row in rows:
        put(target, row + at, one(ref, row))


def copy_rows(ref, count, target, at):
    target[at * CHAN : (at + count) * CHAN, :] = ref[: count * CHAN, :]


def two_rows(target, index, column, value):
    width = value.shape[1]
    target[index, :CHAN, column : column + width] = value
    target[index, CHAN:, STACK + column : STACK + column + width] = value


def weights_kernel(kernels_ref, target):
    target[...] = jnp.zeros_like(target)
    line = lax.broadcasted_iota(jnp.int32, (CHAN, CHAN), 0)
    same = line == lax.broadcasted_iota(jnp.int32, (CHAN, CHAN), 1)
    unit = jnp.where(same, 1.0, 0.0).astype(BF16)
    for section in range(2):
        for which in range(2):
            index = 2 * (2 * section + which)
            two_rows(target, index, 0, kernels_ref[section, which])
            for tap in range(9):
                at = (8 - tap) * CHAN
                block = kernels_ref[section, which, :, at : at + CHAN]
                turned = lax.dot_general(
                    unit, block, (((1,), (1,)), ((), ())), preferred_element_type=F32
                )
                two_rows(target, index + 1, tap * CHAN, turned.astype(BF16))


def conv_rows(weight, source, first, count, finish):
    for row in range(first, first + count, 2):
        total = jnp.dot(
            weight,
            source[row * STACK : (row + 4) * STACK, :],
            preferred_element_type=F32,
        )
        finish(row, total[:CHAN])
        finish(row + 1, total[CHAN:])


def grad_rows(upper, upper_row, lower, lower_row, count):
    total = None
    for row in range(0, count, 2):
        left = upper[(row + upper_row) * STACK : (row + upper_row + 2) * STACK, :]
        right = lower[(row + lower_row) * CHAN : (row + lower_row + 4) * CHAN, :]
        term = lax.dot_general(
            left, right, (((1,), (1,)), ((), ())), preferred_element_type=F32
        )
        total = term if total is None else total + term
    return total[:STACK, :STACK] + total[STACK:, CHAN:]


def channels_first(wide, target):
    target[...] = jnp.swapaxes(wide[...], 0, 1).astype(BF16)


def odd_place():
    return lax.rem(lax.axis_index("space"), 2) == 1


def put_at(ref, row, field):
    ref[pl.ds(pl.multiple_of(row * STACK, CHAN), STACK), :] = stacked(field)


def halo_rows(near_ref, far_ref, count, rows, target):
    odd = odd_place()
    above, below = 0, rows + count
    near_at = jnp.where(odd, above, below)
    far_at = jnp.where(odd, below, above)
    for row in range(count):
        put_at(target, near_at + row, one(near_ref, row))
        put_at(target, far_at + row, one(far_ref, row))


def send_edges(rows_ref, edge, near_ref, far_ref):
    odd = odd_place()
    last = rows_ref.shape[0] - edge * CHAN
    near_at = jnp.where(odd, 0, last)
    far_at = jnp.where(odd, last, 0)
    near_ref[...] = rows_ref[pl.ds(pl.multiple_of(near_at, CHAN), edge * CHAN), :]
    far_ref[...] = rows_ref[pl.ds(pl.multiple_of(far_at, CHAN), edge * CHAN), :]


def entry_kernel(edge, tile_ref, rows_ref, near_ref, far_ref, held, arrived):
    piece = CHAN // PIECES
    copies = [
        pltpu.make_async_copy(
            tile_ref.at[i * piece : (i + 1) * piece],
            held.at[i * piece : (i + 1) * piece],
            arrived.at[i],
        )
        for i in range(PIECES)
    ]
    for copy in copies:
        copy.start()
    for i, copy in enumerate(copies):
        copy.wait()
        part = held[i * piece : (i + 1) * piece].astype(F32)
        turned = jnp.swapaxes(part, 0, 1).astype(BF16)
        for row in range(turned.shape[0]):
            at = row * CHAN + i * piece
            rows_ref[at : at + piece, :] = turned[row]
    send_edges(rows_ref, edge, near_ref, far_ref)


def channels_first(wide, target):
    target[...] = jnp.swapaxes(wide[...], 0, 1).astype(BF16)


def inner_kernel(rows, x_ref, w_ref, hid0_ref, x1_ref, hid1_ref, x3, h3, y3):
    stack_rows(x_ref, range(rows), x3, 0)

    def hidden0(row, total):
        value = jnp.maximum(total, 0.0).astype(BF16)
        put(h3, row, value)
        hid0_ref[row * CHAN : (row + 1) * CHAN, :] = value

    conv_rows(w_ref[0], x3, 0, rows - 2, hidden0)

    def next_x(row, total):
        value = (one(x_ref, row + 2).astype(F32) + total).astype(BF16)
        put(y3, row, value)
        x1_ref[row * CHAN : (row + 1) * CHAN, :] = value

    conv_rows(w_ref[2], h3, 0, rows - 4, next_x)

    def hidden1(row, total):
        hid1_ref[row * CHAN : (row + 1) * CHAN, :] = jnp.maximum(total, 0.0).astype(BF16)

    conv_rows(w_ref[4], y3, 0, rows - 6, hidden1)


def forward_kernel(
    rows, height, x_ref, near_ref, far_ref, w_ref, hid0_in, x1_in, hid1_in,
    hid0_ref, x1_ref, hid1_ref, x3, h3, y3,
):
    first = lax.axis_index("space") * rows

    def inside(row, value):
        if 0 <= row < rows:
            return value
        keep = jnp.logical_and(first + row >= 0, first + row < height)
        return jnp.where(keep, value, 0.0)

    halo_rows(near_ref, far_ref, 4, rows, x3)
    stack_rows(x_ref, (0, 1, rows - 2, rows - 1), x3, 4)
    stack_rows(hid0_in, (0, 1, rows - 4, rows - 3), h3, 4)
    stack_rows(x1_in, (0, 1, rows - 6, rows - 5), y3, 4)
    copy_rows(hid0_in, rows - 2, hid0_ref, 2)
    copy_rows(x1_in, rows - 4, x1_ref, 3)
    copy_rows(hid1_in, rows - 6, hid1_ref, 4)

    def hidden0(row, total):
        value = inside(row - 3, jnp.maximum(total, 0.0)).astype(BF16)
        put(h3, row, value)
        if 2 <= row < rows + 4:
            hid0_ref[(row - 2) * CHAN : (row - 1) * CHAN, :] = value

    def next_x(row, total):
        value = inside(row - 2, middle(x3, row + 2).astype(F32) + total).astype(BF16)
        put(y3, row, value)
        if 1 <= row < rows + 3:
            x1_ref[(row - 1) * CHAN : row * CHAN, :] = value

    def hidden1(row, total):
        value = inside(row - 1, jnp.maximum(total, 0.0)).astype(BF16)
        hid1_ref[row * CHAN : (row + 1) * CHAN, :] = value

    for at in (0, rows + 2):
        conv_rows(w_ref[0], x3, at, 4, hidden0)
    for at in (0, rows):
        conv_rows(w_ref[2], h3, at, 4, next_x)
    for at in (0, rows - 2):
        conv_rows(w_ref[4], y3, at, 4, hidden1)


def backward1_kernel(
    rows, g_ref, near_ref, far_ref, hid1_ref, w_ref, g1_ref, next_near, next_far, dh1_ref, g3, d3,
):
    stack_rows(g_ref, range(rows), g3, 2)
    halo_rows(near_ref, far_ref, 2, rows, g3)

    def dhidden1(row, total):
        value = jnp.where(one(hid1_ref, row) > 0, total, 0.0).astype(BF16)
        put(d3, row, value)
        if 1 <= row < rows + 1:
            dh1_ref[(row - 1) * CHAN : row * CHAN, :] = value

    conv_rows(w_ref[7], g3, 0, rows + 2, dhidden1)

    def next_g(row, total):
        value = (one(g_ref, row).astype(F32) + total).astype(BF16)
        g1_ref[row * CHAN : (row + 1) * CHAN, :] = value

    conv_rows(w_ref[5], d3, 0, rows, next_g)
    send_edges(g1_ref, 2, next_near, next_far)


def grads1_kernel(
    rows, g_ref, hid1_ref, dh1_ref, x1_ref, g1_ref, hid0_ref, grad01, grad10, grad11, s3, t3, u3
):
    stack_rows(g_ref, range(rows), s3, 0)
    grad11[...] = grad_rows(s3, 0, hid1_ref, 0, rows)
    stack_rows(dh1_ref, range(rows), t3, 0)
    grad10[...] = grad_rows(t3, 0, x1_ref, 0, rows)
    stack_rows(g1_ref, range(rows), u3, 0)
    grad01[...] = grad_rows(u3, 0, hid0_ref, 0, rows)


def output_kernel(rows, hid1_ref, x1_ref, w_ref, out_ref, k3, wide):
    stack_rows(hid1_ref, range(rows + 2), k3, 0)

    def last_x(row, total):
        wide[row] = one(x1_ref, row + 1).astype(F32) + total

    conv_rows(w_ref[6], k3, 0, rows, last_x)
    channels_first(wide, out_ref)


def backward0_kernel(
    rows, scale, g1_ref, near_ref, far_ref, hid0_ref, x_ref, xnear_ref, xfar_ref, w_ref, grad01, grad10, grad11,
    dh0_ref, keep_ref, send_ref, g3, d3, xs, both,
):
    stack_rows(g1_ref, range(rows), g3, 2)
    halo_rows(near_ref, far_ref, 2, rows, g3)

    def dhidden0(row, total):
        value = jnp.where(one(hid0_ref, row) > 0, total, 0.0).astype(BF16)
        dh0_ref[row * CHAN : (row + 1) * CHAN, :] = value
        put(d3, row, value)

    conv_rows(w_ref[3], g3, 0, rows + 2, dhidden0)
    odd = odd_place()
    xs[CHAN : (rows + 1) * CHAN, :] = x_ref[...]
    near_at, far_at = jnp.where(odd, 0, rows + 1), jnp.where(odd, rows + 1, 0)
    near_row, far_row = jnp.where(odd, 3, 0), jnp.where(odd, 0, 3)
    for ref, at, row in ((xnear_ref, near_at, near_row), (xfar_ref, far_at, far_row)):
        source = pl.ds(pl.multiple_of(row * CHAN, CHAN), CHAN)
        xs[pl.ds(pl.multiple_of(at * CHAN, CHAN), CHAN), :] = ref[source, :]
    grad00 = grad_rows(d3, 1, xs, 0, rows)
    pairs = ((grad00, grad01[...]), (grad10[...], grad11[...]))
    for section, pair in enumerate(pairs):
        for which, value in enumerate(pair):
            for a in range(3):
                for b in range(3):
                    block = value[(2 - b) * CHAN : (3 - b) * CHAN, a * CHAN : (a + 1) * CHAN]
                    at = which * 9 * CHAN + (3 * a + b) * CHAN
                    both[section, :, at : at + CHAN] = block * scale
    mine = lax.rem(lax.axis_index("space"), 2)
    keep_ref[...] = both[mine]
    send_ref[...] = both[1 - mine].astype(BF16)


def input_grad_kernel(rows, dh0_ref, g1_ref, w_ref, out_ref, d3, wide):
    stack_rows(dh0_ref, range(rows + 2), d3, 0)

    def last_g(row, total):
        wide[row] = one(g1_ref, row).astype(F32) + total

    conv_rows(w_ref[1], d3, 0, rows, last_g)
    channels_first(wide, out_ref)


def gathered_kernel(own_ref, other_ref, out_ref):
    mine = lax.rem(lax.axis_index("space"), 2)
    for section, ref in ((mine, own_ref), (1 - mine, other_ref)):
        for which in range(2):
            piece = ref[:, which * 9 * CHAN : (which + 1) * 9 * CHAN]
            out_ref[section, which] = piece.astype(F32)


def exchange(value, mask, count):
    return lax.ppermute(value, "space", [(d, d ^ mask) for d in range(count)])


def local(features, cotangent, kernels):
    rows, width = features.shape[1], features.shape[2]
    count = lax.axis_size("space")
    height = rows * count
    scale = 1.0 / math.sqrt(height * width)
    place = lax.axis_index("space")
    beyond = [(i, i + 1) for i in range(1, count - 1, 2)]
    beyond += [(target, source) for source, target in beyond]

    def shape(n, dtype=BF16):
        return jax.ShapeDtypeStruct((n * CHAN, width), dtype)

    def vmem(n):
        return pltpu.VMEM((n * STACK, width), BF16)

    def neighbours(near, far):
        return exchange(near, 1, count), lax.ppermute(far, "space", beyond)

    row_flops = 2 * CHAN * 9 * CHAN * width * 4
    grad = jax.ShapeDtypeStruct((STACK, STACK), F32)
    tile = jax.ShapeDtypeStruct((CHAN, rows, width), BF16)
    wide = pltpu.VMEM((rows, CHAN, width), F32)
    half = (CHAN, 18 * CHAN)
    entry = [pltpu.VMEM((CHAN, rows, width), BF16), pltpu.SemaphoreType.DMA((PIECES,))]

    x, x_near, x_far = call(
        functools.partial(entry_kernel, 4), (features,), (shape(rows), shape(4), shape(4)),
        entry, 0, "x_rows", place=HBM,
    )
    xnear, xfar = neighbours(x_near, x_far)
    (weights,) = call(
        weights_kernel, (kernels,), (jax.ShapeDtypeStruct((8, 2 * CHAN, 4 * STACK), BF16),), [],
        row_flops, "weights", after=(x_near,),
    )
    inner = call(
        functools.partial(inner_kernel, rows), (x, weights),
        (shape(rows - 2), shape(rows - 4), shape(rows - 6)),
        [vmem(rows), vmem(rows - 2), vmem(rows - 4)], 12 * row_flops, "inner",
    )
    g, g_near, g_far = call(
        functools.partial(entry_kernel, 2), (cotangent,), (shape(rows), shape(2), shape(2)),
        entry, 0, "g_rows", after=(inner[2],), place=HBM,
    )
    gnear, gfar = neighbours(g_near, g_far)
    hid0, x1, hid1 = call(
        functools.partial(forward_kernel, rows, height), (x, xnear, xfar, weights, *inner),
        (shape(rows + 2),) * 3, [vmem(rows + 8), vmem(rows + 6), vmem(rows + 4)],
        24 * row_flops, "forward",
    )
    g1, g1_near, g1_far, dh1 = call(
        functools.partial(backward1_kernel, rows), (g, gnear, gfar, hid1, weights),
        (shape(rows), shape(2), shape(2), shape(rows)),
        [vmem(rows + 4), vmem(rows + 2)], 18 * row_flops, "backward1",
    )
    g1near, g1far = neighbours(g1_near, g1_far)
    grad01, grad10, grad11 = call(
        functools.partial(grads1_kernel, rows), (g, hid1, dh1, x1, g1, hid0), (grad,) * 3,
        [vmem(rows)] * 3, 24 * row_flops, "grads1",
    )
    (section_output,) = call(
        functools.partial(output_kernel, rows), (hid1, x1, weights), (tile,),
        [vmem(rows + 2), wide], 8 * row_flops, "output", after=(g1_near,),
    )
    g1near, g1far, section_output = lax.optimization_barrier((g1near, g1far, section_output))
    dh0, part, send = call(
        functools.partial(backward0_kernel, rows, scale),
        (g1, g1near, g1far, hid0, x, xnear, xfar, weights, grad01, grad10, grad11),
        (shape(rows + 2), jax.ShapeDtypeStruct(half, F32), jax.ShapeDtypeStruct(half, BF16)),
        [vmem(rows + 4), vmem(rows + 2), pltpu.VMEM(((rows + 2) * CHAN, width), BF16),
         pltpu.VMEM((2, *half), F32)],
        18 * row_flops, "backward0",
    )

    part = part + exchange(send, 1, count).astype(F32)
    low, high = part[: CHAN // 2], part[CHAN // 2 :]
    bit = (place & 2) != 0
    send = jnp.where(bit, low, high).astype(BF16)
    part = jnp.where(bit, high, low)
    arrived = exchange(send, 2, count)
    part = part + arrived.astype(F32)
    step = 4
    input_grad = None
    while step < count:
        send = part.astype(BF16)
        masks = [step, 2 * step, 3 * step] if 2 * step < count else [step]
        arrived = [exchange(send, mask, count) for mask in masks]
        if input_grad is None:
            (input_grad,) = call(
                functools.partial(input_grad_kernel, rows), (dh0, g1, weights), (tile,),
                [vmem(rows + 2), wide], 8 * row_flops, "input_grad", after=(send,),
            )
            arrived, input_grad = lax.optimization_barrier((arrived, input_grad))
        own = send.astype(F32)
        arrived = [value.astype(F32) for value in arrived]
        part = own + arrived[0]
        if len(masks) == 3:
            part = part + (arrived[1] + arrived[2])
        step *= len(masks) + 1
    done = part.astype(BF16)
    bit = (place & 2) != 0
    other = exchange(done, 2, count)
    done = jnp.where(bit, jnp.concatenate([other, done]), jnp.concatenate([done, other]))
    (kernel_grad,) = call(
        gathered_kernel, (done, exchange(done, 1, count)),
        (jax.ShapeDtypeStruct((2, 2, CHAN, 9 * CHAN), F32),), [], 0, "gathered",
    )
    return (section_output, input_grad, kernel_grad)


def solution(mesh):
    return jax.shard_map(
        local,
        mesh=mesh,
        in_specs=(P(None, "space", "groups"), P(None, "space", "groups"), P()),
        out_specs=(
            P(None, "space", "groups"),
            P(None, "space", "groups"),
            P("groups", None, None, None),
        ),
        check_vma=False,
    )
```

```python
import functools
import math

import jax
import jax.numpy as jnp
from jax import lax
from jax.experimental import pallas as pl
from jax.experimental.pallas import tpu as pltpu
from jax.sharding import PartitionSpec as P

CHAN = 64
STACK = 3 * CHAN
F32 = jnp.float32
BF16 = jnp.bfloat16
VMEM = pl.BlockSpec(memory_space=pltpu.VMEM)
ANY = pl.BlockSpec(memory_space=pl.ANY)
HBM = pl.BlockSpec(memory_space=pltpu.HBM)
PIECES = 4


def call(body, operands, outs, scratch, flops, name, after=(), place=VMEM):
    nbytes = sum(v.size * v.dtype.itemsize for v in (*operands, *outs))
    held = sum(math.prod(v.shape) * v.dtype.itemsize for v in scratch if v.dtype in (F32, BF16))

    def kernel(*refs):
        body(*refs[len(after) :])

    return pl.pallas_call(
        kernel,
        out_shape=outs,
        in_specs=[ANY] * len(after) + [place] + [VMEM] * (len(operands) - 1),
        out_specs=[VMEM] * len(outs),
        scratch_shapes=scratch,
        compiler_params=pltpu.CompilerParams(vmem_limit_bytes=nbytes + held + (6 << 20)),
        cost_estimate=pl.CostEstimate(flops=flops, bytes_accessed=nbytes, transcendentals=0),
        name=name,
    )(*after, *operands)


def stacked(field):
    width = field.shape[1]
    lane = lax.broadcasted_iota(jnp.int32, field.shape, 1)
    zero = jnp.zeros_like(field)
    left = jnp.where(lane == 0, zero, pltpu.roll(field, 1, 1))
    right = jnp.where(lane == width - 1, zero, pltpu.roll(field, width - 1, 1))
    return jnp.concatenate([left, field, right], axis=0)


def put(ref, row, field):
    ref[row * STACK : (row + 1) * STACK, :] = stacked(field)


def middle(ref, row):
    return ref[row * STACK + CHAN : row * STACK + 2 * CHAN, :]


def one(ref, row):
    return ref[row * CHAN : (row + 1) * CHAN, :]


def stack_rows(ref, rows, target, at):
    for row in rows:
        put(target, row + at, one(ref, row))


def g_entry_kernel(
    edge, tile_ref, w_ref, rows_ref, near_ref, far_ref, inner_ref, held, g3, arrived
):
    entry_kernel(edge, tile_ref, rows_ref, near_ref, far_ref, held, arrived)
    rows = tile_ref.shape[1]
    stack_rows(rows_ref, range(rows), g3, 0)

    def keep(row, total):
        inner_ref[row * CHAN : (row + 1) * CHAN, :] = total

    conv_rows(w_ref[7], g3, 0, rows - 2, keep)


def copy_rows(ref, count, target, at):
    target[at * CHAN : (at + count) * CHAN, :] = ref[: count * CHAN, :]


def two_rows(target, index, column, value):
    width = value.shape[1]
    target[index, :CHAN, column : column + width] = value
    target[index, CHAN:, STACK + column : STACK + column + width] = value


def weights_kernel(kernels_ref, target):
    target[...] = jnp.zeros_like(target)
    line = lax.broadcasted_iota(jnp.int32, (CHAN, CHAN), 0)
    same = line == lax.broadcasted_iota(jnp.int32, (CHAN, CHAN), 1)
    unit = jnp.where(same, 1.0, 0.0).astype(BF16)
    for section in range(2):
        for which in range(2):
            index = 2 * (2 * section + which)
            two_rows(target, index, 0, kernels_ref[section, which])
            for tap in range(9):
                at = (8 - tap) * CHAN
                block = kernels_ref[section, which, :, at : at + CHAN]
                turned = lax.dot_general(
                    unit, block, (((1,), (1,)), ((), ())), preferred_element_type=F32
                )
                two_rows(target, index + 1, tap * CHAN, turned.astype(BF16))


def conv_rows(weight, source, first, count, finish):
    for row in range(first, first + count, 2):
        total = jnp.dot(
            weight,
            source[row * STACK : (row + 4) * STACK, :],
            preferred_element_type=F32,
        )
        finish(row, total[:CHAN])
        finish(row + 1, total[CHAN:])


def grad_rows(upper, upper_row, lower, lower_row, count):
    total = None
    for row in range(0, count, 2):
        left = upper[(row + upper_row) * STACK : (row + upper_row + 2) * STACK, :]
        right = lower[(row + lower_row) * CHAN : (row + lower_row + 4) * CHAN, :]
        term = lax.dot_general(
            left, right, (((1,), (1,)), ((), ())), preferred_element_type=F32
        )
        total = term if total is None else total + term
    return total[:STACK, :STACK] + total[STACK:, CHAN:]


def channels_first(wide, target):
    target[...] = jnp.swapaxes(wide[...], 0, 1).astype(BF16)


def odd_place():
    return lax.rem(lax.axis_index("space"), 2) == 1


def put_at(ref, row, field):
    ref[pl.ds(pl.multiple_of(row * STACK, CHAN), STACK), :] = stacked(field)


def halo_rows(near_ref, far_ref, count, rows, target):
    odd = odd_place()
    above, below = 0, rows + count
    near_at = jnp.where(odd, above, below)
    far_at = jnp.where(odd, below, above)
    for row in range(count):
        put_at(target, near_at + row, one(near_ref, row))
        put_at(target, far_at + row, one(far_ref, row))


def send_edges(rows_ref, edge, near_ref, far_ref):
    odd = odd_place()
    last = rows_ref.shape[0] - edge * CHAN
    near_at = jnp.where(odd, 0, last)
    far_at = jnp.where(odd, last, 0)
    near_ref[...] = rows_ref[pl.ds(pl.multiple_of(near_at, CHAN), edge * CHAN), :]
    far_ref[...] = rows_ref[pl.ds(pl.multiple_of(far_at, CHAN), edge * CHAN), :]


def entry_kernel(edge, tile_ref, rows_ref, near_ref, far_ref, held, arrived):
    piece = CHAN // PIECES
    copies = [
        pltpu.make_async_copy(
            tile_ref.at[i * piece : (i + 1) * piece],
            held.at[i * piece : (i + 1) * piece],
            arrived.at[i],
        )
        for i in range(PIECES)
    ]
    for copy in copies:
        copy.start()
    for i, copy in enumerate(copies):
        copy.wait()
        part = held[i * piece : (i + 1) * piece].astype(F32)
        turned = jnp.swapaxes(part, 0, 1).astype(BF16)
        for row in range(turned.shape[0]):
            at = row * CHAN + i * piece
            rows_ref[at : at + piece, :] = turned[row]
    send_edges(rows_ref, edge, near_ref, far_ref)


def channels_first(wide, target):
    target[...] = jnp.swapaxes(wide[...], 0, 1).astype(BF16)


def inner_kernel(rows, x_ref, w_ref, hid0_ref, x1_ref, hid1_ref, x3, h3, y3):
    stack_rows(x_ref, range(rows), x3, 0)

    def hidden0(row, total):
        value = jnp.maximum(total, 0.0).astype(BF16)
        put(h3, row, value)
        hid0_ref[row * CHAN : (row + 1) * CHAN, :] = value

    conv_rows(w_ref[0], x3, 0, rows - 2, hidden0)

    def next_x(row, total):
        value = (one(x_ref, row + 2).astype(F32) + total).astype(BF16)
        put(y3, row, value)
        x1_ref[row * CHAN : (row + 1) * CHAN, :] = value

    conv_rows(w_ref[2], h3, 0, rows - 4, next_x)

    def hidden1(row, total):
        hid1_ref[row * CHAN : (row + 1) * CHAN, :] = jnp.maximum(total, 0.0).astype(BF16)

    conv_rows(w_ref[4], y3, 0, rows - 6, hidden1)


def forward_kernel(
    rows, height, x_ref, near_ref, far_ref, w_ref, hid0_in, x1_in, hid1_in,
    hid0_ref, x1_ref, hid1_ref, x3, h3, y3,
):
    first = lax.axis_index("space") * rows

    def inside(row, value):
        if 0 <= row < rows:
            return value
        keep = jnp.logical_and(first + row >= 0, first + row < height)
        return jnp.where(keep, value, 0.0)

    halo_rows(near_ref, far_ref, 4, rows, x3)
    stack_rows(x_ref, (0, 1, rows - 2, rows - 1), x3, 4)
    stack_rows(hid0_in, (0, 1, rows - 4, rows - 3), h3, 4)
    stack_rows(x1_in, (0, 1, rows - 6, rows - 5), y3, 4)
    copy_rows(hid0_in, rows - 2, hid0_ref, 2)
    copy_rows(x1_in, rows - 4, x1_ref, 3)
    copy_rows(hid1_in, rows - 6, hid1_ref, 4)

    def hidden0(row, total):
        value = inside(row - 3, jnp.maximum(total, 0.0)).astype(BF16)
        put(h3, row, value)
        if 2 <= row < rows + 4:
            hid0_ref[(row - 2) * CHAN : (row - 1) * CHAN, :] = value

    def next_x(row, total):
        value = inside(row - 2, middle(x3, row + 2).astype(F32) + total).astype(BF16)
        put(y3, row, value)
        if 1 <= row < rows + 3:
            x1_ref[(row - 1) * CHAN : row * CHAN, :] = value

    def hidden1(row, total):
        value = inside(row - 1, jnp.maximum(total, 0.0)).astype(BF16)
        hid1_ref[row * CHAN : (row + 1) * CHAN, :] = value

    for at in (0, rows + 2):
        conv_rows(w_ref[0], x3, at, 4, hidden0)
    for at in (0, rows):
        conv_rows(w_ref[2], h3, at, 4, next_x)
    for at in (0, rows - 2):
        conv_rows(w_ref[4], y3, at, 4, hidden1)


def backward1_kernel(
    rows, g_ref, near_ref, far_ref, hid1_ref, inner_ref, w_ref, next_near, next_far, edges_ref, dh1_ref,
    g3, d3,
):
    halo_rows(near_ref, far_ref, 2, rows, g3)
    stack_rows(g_ref, (0, 1, rows - 2, rows - 1), g3, 2)

    def dhidden1(row, total):
        value = jnp.where(one(hid1_ref, row) > 0, total, 0.0).astype(BF16)
        dh1_ref[row * CHAN : (row + 1) * CHAN, :] = value
        if row < 4 or row >= rows - 2:
            put(d3, row, value)

    for row in range(2, rows):
        dhidden1(row, one(inner_ref, row - 2))
    for at in (0, rows):
        conv_rows(w_ref[7], g3, at, 2, dhidden1)

    def next_g(row, total):
        value = (one(g_ref, row).astype(F32) + total).astype(BF16)
        at = row if row < 2 else row - (rows - 4)
        edges_ref[at * CHAN : (at + 1) * CHAN, :] = value

    for at in (0, rows - 2):
        conv_rows(w_ref[5], d3, at, 2, next_g)
    send_edges(edges_ref, 2, next_near, next_far)


def middle_kernel(
    rows, g_ref, edges_ref, hid1_ref, dh1_ref, x1_ref, hid0_ref, x_ref, w_ref,
    g1_ref, dh0_ref, grad00, grad01, grad10, grad11, s3, t3, u3, v3,
):
    stack_rows(dh1_ref, range(rows + 2), t3, 0)
    copy_rows(edges_ref, 2, g1_ref, 0)
    g1_ref[(rows - 2) * CHAN :, :] = edges_ref[2 * CHAN :, :]

    def next_g(row, total):
        value = (one(g_ref, row).astype(F32) + total).astype(BF16)
        g1_ref[row * CHAN : (row + 1) * CHAN, :] = value
        put(u3, row, value)

    conv_rows(w_ref[5], t3, 2, rows - 4, next_g)
    stack_rows(g1_ref, (0, 1, rows - 2, rows - 1), u3, 0)

    def dhidden0(row, total):
        value = jnp.where(one(hid0_ref, row + 2) > 0, total, 0.0).astype(BF16)
        dh0_ref[row * CHAN : (row + 1) * CHAN, :] = value
        put(v3, row, value)

    conv_rows(w_ref[3], u3, 0, rows - 2, dhidden0)
    stack_rows(g_ref, range(rows), s3, 0)
    grad11[...] = grad_rows(s3, 0, hid1_ref, 0, rows)
    grad10[...] = grad_rows(t3, 1, x1_ref, 0, rows)
    grad01[...] = grad_rows(u3, 0, hid0_ref, 0, rows)
    grad00[...] = grad_rows(v3, 0, x_ref, 0, rows - 2)


def output_kernel(rows, hid1_ref, x1_ref, w_ref, out_ref, k3, wide):
    stack_rows(hid1_ref, range(rows + 2), k3, 0)

    def last_x(row, total):
        wide[row] = one(x1_ref, row + 1).astype(F32) + total

    conv_rows(w_ref[6], k3, 0, rows, last_x)
    channels_first(wide, out_ref)


def backward0_kernel(
    rows, scale, g1_ref, near_ref, far_ref, hid0_ref, x_ref, xnear_ref, xfar_ref, w_ref, dh0_in,
    inner00, grad01, grad10, grad11, dh0_ref, keep_ref, send_ref, g3, d3, xs, both,
):
    halo_rows(near_ref, far_ref, 2, rows, g3)
    stack_rows(g1_ref, (0, 1, rows - 2, rows - 1), g3, 2)
    copy_rows(dh0_in, rows - 2, dh0_ref, 2)

    def dhidden0(row, total):
        value = jnp.where(one(hid0_ref, row) > 0, total, 0.0).astype(BF16)
        dh0_ref[row * CHAN : (row + 1) * CHAN, :] = value
        if row == 1:
            put(d3, 0, value)
        if row == rows:
            put(d3, 1, value)

    for at in (0, rows):
        conv_rows(w_ref[3], g3, at, 2, dhidden0)
    odd = odd_place()
    copy_rows(x_ref, 2, xs, 1)
    xs[3 * CHAN : 5 * CHAN, :] = x_ref[(rows - 2) * CHAN :, :]
    near_at, far_at = jnp.where(odd, 0, 5), jnp.where(odd, 5, 0)
    near_row, far_row = jnp.where(odd, 3, 0), jnp.where(odd, 0, 3)
    for ref, at, row in ((xnear_ref, near_at, near_row), (xfar_ref, far_at, far_row)):
        source = pl.ds(pl.multiple_of(row * CHAN, CHAN), CHAN)
        xs[pl.ds(pl.multiple_of(at * CHAN, CHAN), CHAN), :] = ref[source, :]
    grad00 = inner00[...]
    for end in range(2):
        grad00 = grad00 + lax.dot_general(
            d3[end * STACK : (end + 1) * STACK, :],
            xs[end * STACK : (end + 1) * STACK, :],
            (((1,), (1,)), ((), ())),
            preferred_element_type=F32,
        )
    pairs = ((grad00, grad01[...]), (grad10[...], grad11[...]))
    for section, pair in enumerate(pairs):
        for which, value in enumerate(pair):
            for a in range(3):
                for b in range(3):
                    block = value[(2 - b) * CHAN : (3 - b) * CHAN, a * CHAN : (a + 1) * CHAN]
                    at = which * 9 * CHAN + (3 * a + b) * CHAN
                    both[section, :, at : at + CHAN] = block * scale
    mine = lax.rem(lax.axis_index("space"), 2)
    keep_ref[...] = both[mine]
    send_ref[...] = both[1 - mine].astype(BF16)


def input_grad_kernel(rows, dh0_ref, g1_ref, w_ref, out_ref, d3, wide):
    stack_rows(dh0_ref, range(rows + 2), d3, 0)

    def last_g(row, total):
        wide[row] = one(g1_ref, row).astype(F32) + total

    conv_rows(w_ref[1], d3, 0, rows, last_g)
    channels_first(wide, out_ref)


def gathered_kernel(own_ref, other_ref, out_ref):
    mine = lax.rem(lax.axis_index("space"), 2)
    for section, ref in ((mine, own_ref), (1 - mine, other_ref)):
        for which in range(2):
            piece = ref[:, which * 9 * CHAN : (which + 1) * 9 * CHAN]
            out_ref[section, which] = piece.astype(F32)


def exchange(value, mask, count):
    return lax.ppermute(value, "space", [(d, d ^ mask) for d in range(count)])


def local(features, cotangent, kernels):
    rows, width = features.shape[1], features.shape[2]
    count = lax.axis_size("space")
    height = rows * count
    scale = 1.0 / math.sqrt(height * width)
    place = lax.axis_index("space")
    beyond = [(i, i + 1) for i in range(1, count - 1, 2)]
    beyond += [(target, source) for source, target in beyond]

    def shape(n, dtype=BF16):
        return jax.ShapeDtypeStruct((n * CHAN, width), dtype)

    def vmem(n):
        return pltpu.VMEM((n * STACK, width), BF16)

    def neighbours(near, far):
        return exchange(near, 1, count), lax.ppermute(far, "space", beyond)

    row_flops = 2 * CHAN * 9 * CHAN * width * 4
    grad = jax.ShapeDtypeStruct((STACK, STACK), F32)
    tile = jax.ShapeDtypeStruct((CHAN, rows, width), BF16)
    wide = pltpu.VMEM((rows, CHAN, width), F32)
    half = (CHAN, 18 * CHAN)
    entry = [pltpu.VMEM((CHAN, rows, width), BF16), pltpu.SemaphoreType.DMA((PIECES,))]

    x, x_near, x_far = call(
        functools.partial(entry_kernel, 4), (features,), (shape(rows), shape(4), shape(4)),
        entry, 0, "x_rows", place=HBM,
    )
    xnear, xfar = neighbours(x_near, x_far)
    (weights,) = call(
        weights_kernel, (kernels,), (jax.ShapeDtypeStruct((8, 2 * CHAN, 4 * STACK), BF16),), [],
        row_flops, "weights", after=(x_near,),
    )
    inner = call(
        functools.partial(inner_kernel, rows), (x, weights),
        (shape(rows - 2), shape(rows - 4), shape(rows - 6)),
        [vmem(rows), vmem(rows - 2), vmem(rows - 4)], 12 * row_flops, "inner",
    )
    g, g_near, g_far, g_inner = call(
        functools.partial(g_entry_kernel, 2), (cotangent, weights),
        (shape(rows), shape(2), shape(2), shape(rows - 2, F32)),
        [entry[0], vmem(rows), entry[1]], 6 * row_flops, "g_rows", after=(inner[2],), place=HBM,
    )
    gnear, gfar = neighbours(g_near, g_far)
    hid0, x1, hid1 = call(
        functools.partial(forward_kernel, rows, height), (x, xnear, xfar, weights, *inner),
        (shape(rows + 2),) * 3, [vmem(rows + 8), vmem(rows + 6), vmem(rows + 4)],
        24 * row_flops, "forward",
    )
    g1_near, g1_far, edges, dh1 = call(
        functools.partial(backward1_kernel, rows), (g, gnear, gfar, hid1, g_inner, weights),
        (shape(2), shape(2), shape(4), shape(rows + 2)),
        [vmem(rows + 4), vmem(rows + 2)], 8 * row_flops, "backward1",
    )
    g1near, g1far = neighbours(g1_near, g1_far)
    g1, dh0_inner, *grads = call(
        functools.partial(middle_kernel, rows), (g, edges, hid1, dh1, x1, hid0, x, weights),
        (shape(rows), shape(rows - 2)) + (grad,) * 4,
        [vmem(rows), vmem(rows + 2), vmem(rows), vmem(rows - 2)], 40 * row_flops, "middle",
    )
    (section_output,) = call(
        functools.partial(output_kernel, rows), (hid1, x1, weights), (tile,),
        [vmem(rows + 2), wide], 8 * row_flops, "output", after=(dh0_inner,),
    )
    g1near, g1far, section_output = lax.optimization_barrier((g1near, g1far, section_output))
    dh0, part, send = call(
        functools.partial(backward0_kernel, rows, scale),
        (g1, g1near, g1far, hid0, x, xnear, xfar, weights, dh0_inner, *grads),
        (shape(rows + 2), jax.ShapeDtypeStruct(half, F32), jax.ShapeDtypeStruct(half, BF16)),
        [vmem(rows + 4), vmem(2), pltpu.VMEM((6 * CHAN, width), BF16),
         pltpu.VMEM((2, *half), F32)],
        8 * row_flops, "backward0",
    )

    part = part + exchange(send, 1, count).astype(F32)
    low, high = part[: CHAN // 2], part[CHAN // 2 :]
    bit = (place & 2) != 0
    send = jnp.where(bit, low, high).astype(BF16)
    part = jnp.where(bit, high, low)
    arrived = exchange(send, 2, count)
    part = part + arrived.astype(F32)
    step = 4
    input_grad = None
    while step < count:
        send = part.astype(BF16)
        masks = [step, 2 * step, 3 * step] if 2 * step < count else [step]
        arrived = [exchange(send, mask, count) for mask in masks]
        if input_grad is None:
            (input_grad,) = call(
                functools.partial(input_grad_kernel, rows), (dh0, g1, weights), (tile,),
                [vmem(rows + 2), wide], 8 * row_flops, "input_grad", after=(send,),
            )
            arrived, input_grad = lax.optimization_barrier((arrived, input_grad))
        own = send.astype(F32)
        arrived = [value.astype(F32) for value in arrived]
        part = own + arrived[0]
        if len(masks) == 3:
            part = part + (arrived[1] + arrived[2])
        step *= len(masks) + 1
    done = part.astype(BF16)
    bit = (place & 2) != 0
    other = exchange(done, 2, count)
    done = jnp.where(bit, jnp.concatenate([other, done]), jnp.concatenate([done, other]))
    (kernel_grad,) = call(
        gathered_kernel, (done, exchange(done, 1, count)),
        (jax.ShapeDtypeStruct((2, 2, CHAN, 9 * CHAN), F32),), [], 0, "gathered",
    )
    return (section_output, input_grad, kernel_grad)


def solution(mesh):
    return jax.shard_map(
        local,
        mesh=mesh,
        in_specs=(P(None, "space", "groups"), P(None, "space", "groups"), P()),
        out_specs=(
            P(None, "space", "groups"),
            P(None, "space", "groups"),
            P("groups", None, None, None),
        ),
        check_vma=False,
    )
```

```python
import functools
import math

import jax
import jax.numpy as jnp
from jax import lax
from jax.experimental import pallas as pl
from jax.experimental.pallas import tpu as pltpu
from jax.sharding import PartitionSpec as P

CHAN = 64
STACK = 3 * CHAN
F32 = jnp.float32
BF16 = jnp.bfloat16
VMEM = pl.BlockSpec(memory_space=pltpu.VMEM)
ANY = pl.BlockSpec(memory_space=pl.ANY)
HBM = pl.BlockSpec(memory_space=pltpu.HBM)
PIECES = 4


def call(body, operands, outs, scratch, flops, name, after=(), place=VMEM):
    nbytes = sum(v.size * v.dtype.itemsize for v in (*operands, *outs))
    held = sum(math.prod(v.shape) * v.dtype.itemsize for v in scratch if v.dtype in (F32, BF16))

    def kernel(*refs):
        body(*refs[len(after) :])

    return pl.pallas_call(
        kernel,
        out_shape=outs,
        in_specs=[ANY] * len(after) + [place] + [VMEM] * (len(operands) - 1),
        out_specs=[VMEM] * len(outs),
        scratch_shapes=scratch,
        compiler_params=pltpu.CompilerParams(vmem_limit_bytes=nbytes + held + (6 << 20)),
        cost_estimate=pl.CostEstimate(flops=flops, bytes_accessed=nbytes, transcendentals=0),
        name=name,
    )(*after, *operands)


def stacked(field):
    width = field.shape[1]
    lane = lax.broadcasted_iota(jnp.int32, field.shape, 1)
    zero = jnp.zeros_like(field)
    left = jnp.where(lane == 0, zero, pltpu.roll(field, 1, 1))
    right = jnp.where(lane == width - 1, zero, pltpu.roll(field, width - 1, 1))
    return jnp.concatenate([left, field, right], axis=0)


def put(ref, row, field):
    ref[row * STACK : (row + 1) * STACK, :] = stacked(field)


def middle(ref, row):
    return ref[row * STACK + CHAN : row * STACK + 2 * CHAN, :]


def one(ref, row):
    return ref[row * CHAN : (row + 1) * CHAN, :]


def stack_rows(ref, rows, target, at):
    for row in rows:
        put(target, row + at, one(ref, row))


def g_entry_kernel(
    edge, tile_ref, w_ref, rows_ref, near_ref, far_ref, inner_ref, held, g3, arrived
):
    entry_kernel(edge, tile_ref, rows_ref, near_ref, far_ref, held, arrived)
    rows = tile_ref.shape[1]
    stack_rows(rows_ref, range(rows), g3, 0)

    def keep(row, total):
        inner_ref[row * CHAN : (row + 1) * CHAN, :] = total

    conv_rows(w_ref[7], g3, 0, rows - 2, keep)


def copy_rows(ref, count, target, at):
    target[at * CHAN : (at + count) * CHAN, :] = ref[: count * CHAN, :]


def two_rows(target, index, column, value):
    width = value.shape[1]
    target[index, :CHAN, column : column + width] = value
    target[index, CHAN:, STACK + column : STACK + column + width] = value


def weights_kernel(kernels_ref, target):
    target[...] = jnp.zeros_like(target)
    line = lax.broadcasted_iota(jnp.int32, (CHAN, CHAN), 0)
    same = line == lax.broadcasted_iota(jnp.int32, (CHAN, CHAN), 1)
    unit = jnp.where(same, 1.0, 0.0).astype(BF16)
    for section in range(2):
        for which in range(2):
            index = 2 * (2 * section + which)
            two_rows(target, index, 0, kernels_ref[section, which])
            for tap in range(9):
                at = (8 - tap) * CHAN
                block = kernels_ref[section, which, :, at : at + CHAN]
                turned = lax.dot_general(
                    unit, block, (((1,), (1,)), ((), ())), preferred_element_type=F32
                )
                two_rows(target, index + 1, tap * CHAN, turned.astype(BF16))


def conv_rows(weight, source, first, count, finish):
    for row in range(first, first + count, 2):
        total = jnp.dot(
            weight,
            source[row * STACK : (row + 4) * STACK, :],
            preferred_element_type=F32,
        )
        finish(row, total[:CHAN])
        finish(row + 1, total[CHAN:])


def grad_rows(upper, upper_row, lower, lower_row, count):
    total = None
    for row in range(0, count, 2):
        left = upper[(row + upper_row) * STACK : (row + upper_row + 2) * STACK, :]
        right = lower[(row + lower_row) * CHAN : (row + lower_row + 4) * CHAN, :]
        term = lax.dot_general(
            left, right, (((1,), (1,)), ((), ())), preferred_element_type=F32
        )
        total = term if total is None else total + term
    return total[:STACK, :STACK] + total[STACK:, CHAN:]


def channels_first(wide, target):
    target[...] = jnp.swapaxes(wide[...], 0, 1).astype(BF16)


def odd_place():
    return lax.rem(lax.axis_index("space"), 2) == 1


def put_at(ref, row, field):
    ref[pl.ds(pl.multiple_of(row * STACK, CHAN), STACK), :] = stacked(field)


def halo_rows(near_ref, far_ref, count, rows, target):
    odd = odd_place()
    above, below = 0, rows + count
    near_at = jnp.where(odd, above, below)
    far_at = jnp.where(odd, below, above)
    for row in range(count):
        put_at(target, near_at + row, one(near_ref, row))
        put_at(target, far_at + row, one(far_ref, row))


def send_edges(rows_ref, edge, near_ref, far_ref):
    odd = odd_place()
    last = rows_ref.shape[0] - edge * CHAN
    near_at = jnp.where(odd, 0, last)
    far_at = jnp.where(odd, last, 0)
    near_ref[...] = rows_ref[pl.ds(pl.multiple_of(near_at, CHAN), edge * CHAN), :]
    far_ref[...] = rows_ref[pl.ds(pl.multiple_of(far_at, CHAN), edge * CHAN), :]


def entry_kernel(edge, tile_ref, rows_ref, near_ref, far_ref, held, arrived):
    piece = CHAN // PIECES
    copies = [
        pltpu.make_async_copy(
            tile_ref.at[i * piece : (i + 1) * piece],
            held.at[i * piece : (i + 1) * piece],
            arrived.at[i],
        )
        for i in range(PIECES)
    ]
    for copy in copies:
        copy.start()
    for i, copy in enumerate(copies):
        copy.wait()
        part = held[i * piece : (i + 1) * piece].astype(F32)
        turned = jnp.swapaxes(part, 0, 1).astype(BF16)
        for row in range(turned.shape[0]):
            at = row * CHAN + i * piece
            rows_ref[at : at + piece, :] = turned[row]
    send_edges(rows_ref, edge, near_ref, far_ref)


def channels_first(wide, target):
    target[...] = jnp.swapaxes(wide[...], 0, 1).astype(BF16)


def inner_kernel(rows, x_ref, w_ref, hid0_ref, x1_ref, hid1_ref, x3, h3, y3):
    stack_rows(x_ref, range(rows), x3, 0)

    def hidden0(row, total):
        value = jnp.maximum(total, 0.0).astype(BF16)
        put(h3, row, value)
        hid0_ref[row * CHAN : (row + 1) * CHAN, :] = value

    conv_rows(w_ref[0], x3, 0, rows - 2, hidden0)

    def next_x(row, total):
        value = (one(x_ref, row + 2).astype(F32) + total).astype(BF16)
        put(y3, row, value)
        x1_ref[row * CHAN : (row + 1) * CHAN, :] = value

    conv_rows(w_ref[2], h3, 0, rows - 4, next_x)

    def hidden1(row, total):
        hid1_ref[row * CHAN : (row + 1) * CHAN, :] = jnp.maximum(total, 0.0).astype(BF16)

    conv_rows(w_ref[4], y3, 0, rows - 6, hidden1)


def forward_kernel(
    rows, height, x_ref, near_ref, far_ref, w_ref, hid0_in, x1_in, hid1_in,
    hid0_ref, x1_ref, hid1_ref, x3, h3, y3,
):
    first = lax.axis_index("space") * rows

    def inside(row, value):
        if 0 <= row < rows:
            return value
        keep = jnp.logical_and(first + row >= 0, first + row < height)
        return jnp.where(keep, value, 0.0)

    halo_rows(near_ref, far_ref, 4, rows, x3)
    stack_rows(x_ref, (0, 1, rows - 2, rows - 1), x3, 4)
    stack_rows(hid0_in, (0, 1, rows - 4, rows - 3), h3, 4)
    stack_rows(x1_in, (0, 1, rows - 6, rows - 5), y3, 4)
    copy_rows(hid0_in, rows - 2, hid0_ref, 2)
    copy_rows(x1_in, rows - 4, x1_ref, 3)
    copy_rows(hid1_in, rows - 6, hid1_ref, 4)

    def hidden0(row, total):
        value = inside(row - 3, jnp.maximum(total, 0.0)).astype(BF16)
        put(h3, row, value)
        if 2 <= row < rows + 4:
            hid0_ref[(row - 2) * CHAN : (row - 1) * CHAN, :] = value

    def next_x(row, total):
        value = inside(row - 2, middle(x3, row + 2).astype(F32) + total).astype(BF16)
        put(y3, row, value)
        if 1 <= row < rows + 3:
            x1_ref[(row - 1) * CHAN : row * CHAN, :] = value

    def hidden1(row, total):
        value = inside(row - 1, jnp.maximum(total, 0.0)).astype(BF16)
        hid1_ref[row * CHAN : (row + 1) * CHAN, :] = value

    for at in (0, rows + 2):
        conv_rows(w_ref[0], x3, at, 4, hidden0)
    for at in (0, rows):
        conv_rows(w_ref[2], h3, at, 4, next_x)
    for at in (0, rows - 2):
        conv_rows(w_ref[4], y3, at, 4, hidden1)


def backward1_kernel(
    rows, g_ref, near_ref, far_ref, hid1_ref, inner_ref, w_ref, next_near, next_far, edges_ref, dh1_ref,
    g3, d3,
):
    halo_rows(near_ref, far_ref, 2, rows, g3)
    stack_rows(g_ref, (0, 1, rows - 2, rows - 1), g3, 2)

    def dhidden1(row, total):
        value = jnp.where(one(hid1_ref, row) > 0, total, 0.0).astype(BF16)
        dh1_ref[row * CHAN : (row + 1) * CHAN, :] = value
        if row < 4 or row >= rows - 2:
            put(d3, row, value)

    for row in range(2, rows):
        dhidden1(row, one(inner_ref, row - 2))
    for at in (0, rows):
        conv_rows(w_ref[7], g3, at, 2, dhidden1)

    def next_g(row, total):
        value = (one(g_ref, row).astype(F32) + total).astype(BF16)
        at = row if row < 2 else row - (rows - 4)
        edges_ref[at * CHAN : (at + 1) * CHAN, :] = value

    for at in (0, rows - 2):
        conv_rows(w_ref[5], d3, at, 2, next_g)
    send_edges(edges_ref, 1, next_near, next_far)


def middle_kernel(
    rows, g_ref, edges_ref, hid1_ref, dh1_ref, x1_ref, hid0_ref, x_ref, w_ref,
    g1_ref, dh0_ref, grad00, grad01, grad10, grad11, s3, t3, u3, v3,
):
    stack_rows(dh1_ref, range(rows + 2), t3, 0)
    copy_rows(edges_ref, 2, g1_ref, 0)
    g1_ref[(rows - 2) * CHAN :, :] = edges_ref[2 * CHAN :, :]

    def next_g(row, total):
        value = (one(g_ref, row).astype(F32) + total).astype(BF16)
        g1_ref[row * CHAN : (row + 1) * CHAN, :] = value
        put(u3, row, value)

    conv_rows(w_ref[5], t3, 2, rows - 4, next_g)
    stack_rows(g1_ref, (0, 1, rows - 2, rows - 1), u3, 0)

    def dhidden0(row, total):
        value = jnp.where(one(hid0_ref, row + 2) > 0, total, 0.0).astype(BF16)
        dh0_ref[(row - 1) * CHAN : row * CHAN, :] = value
        put(v3, row - 1, value)

    conv_rows(w_ref[3], u3, 1, rows - 4, dhidden0)
    stack_rows(g_ref, range(rows), s3, 0)
    grad11[...] = grad_rows(s3, 0, hid1_ref, 0, rows)
    grad10[...] = grad_rows(t3, 1, x1_ref, 0, rows)
    grad01[...] = grad_rows(u3, 0, hid0_ref, 0, rows)
    grad00[...] = grad_rows(v3, 0, x_ref, 1, rows - 4)


def output_kernel(rows, hid1_ref, x1_ref, w_ref, out_ref, k3, wide):
    stack_rows(hid1_ref, range(rows + 2), k3, 0)

    def last_x(row, total):
        wide[row] = one(x1_ref, row + 1).astype(F32) + total

    conv_rows(w_ref[6], k3, 0, rows, last_x)
    channels_first(wide, out_ref)


def backward0_kernel(
    rows, scale, g1_ref, near_ref, far_ref, hid0_ref, x_ref, xnear_ref, xfar_ref, w_ref, inner00,
    grad01, grad10, grad11, dh0_ref, next_near, next_far, keep_ref, send_ref,
    g3, d3, xs, both,
):
    halo_rows(near_ref, far_ref, 1, rows, g3)
    stack_rows(g1_ref, (0, 1, 2, rows - 3, rows - 2, rows - 1), g3, 1)

    def dhidden0(row, total):
        value = jnp.where(one(hid0_ref, row + 1) > 0, total, 0.0).astype(BF16)
        at = row if row < 2 else row - (rows - 4)
        dh0_ref[at * CHAN : (at + 1) * CHAN, :] = value
        put(d3, at, value)

    for at in (0, rows - 2):
        conv_rows(w_ref[3], g3, at, 2, dhidden0)
    send_edges(dh0_ref, 1, next_near, next_far)
    odd = odd_place()
    copy_rows(x_ref, 3, xs, 1)
    xs[4 * CHAN : 7 * CHAN, :] = x_ref[(rows - 3) * CHAN :, :]
    near_at, far_at = jnp.where(odd, 0, 7), jnp.where(odd, 7, 0)
    near_row, far_row = jnp.where(odd, 3, 0), jnp.where(odd, 0, 3)
    for ref, at, row in ((xnear_ref, near_at, near_row), (xfar_ref, far_at, far_row)):
        source = pl.ds(pl.multiple_of(row * CHAN, CHAN), CHAN)
        xs[pl.ds(pl.multiple_of(at * CHAN, CHAN), CHAN), :] = ref[source, :]
    grad00 = inner00[...] + grad_rows(d3, 0, xs, 0, 2) + grad_rows(d3, 2, xs, 4, 2)
    pairs = ((grad00, grad01[...]), (grad10[...], grad11[...]))
    for section, pair in enumerate(pairs):
        for which, value in enumerate(pair):
            for a in range(3):
                for b in range(3):
                    block = value[(2 - b) * CHAN : (3 - b) * CHAN, a * CHAN : (a + 1) * CHAN]
                    at = which * 9 * CHAN + (3 * a + b) * CHAN
                    both[section, :, at : at + CHAN] = block * scale
    mine = lax.rem(lax.axis_index("space"), 2)
    keep_ref[...] = both[mine]
    send_ref[...] = both[1 - mine].astype(BF16)


def input_grad_kernel(rows, dh0_in, dh0_ref, near_ref, far_ref, g1_ref, w_ref, out_ref, d3, wide):
    halo_rows(near_ref, far_ref, 1, rows, d3)
    stack_rows(dh0_in, range(rows - 4), d3, 3)
    stack_rows(dh0_ref, (0, 1), d3, 1)
    stack_rows(dh0_ref, (2, 3), d3, rows - 3)

    def last_g(row, total):
        wide[row] = one(g1_ref, row).astype(F32) + total

    conv_rows(w_ref[1], d3, 0, rows, last_g)
    channels_first(wide, out_ref)


def gathered_kernel(own_ref, other_ref, out_ref):
    mine = lax.rem(lax.axis_index("space"), 2)
    for section, ref in ((mine, own_ref), (1 - mine, other_ref)):
        for which in range(2):
            piece = ref[:, which * 9 * CHAN : (which + 1) * 9 * CHAN]
            out_ref[section, which] = piece.astype(F32)


def exchange(value, mask, count):
    return lax.ppermute(value, "space", [(d, d ^ mask) for d in range(count)])


def local(features, cotangent, kernels):
    rows, width = features.shape[1], features.shape[2]
    count = lax.axis_size("space")
    height = rows * count
    scale = 1.0 / math.sqrt(height * width)
    place = lax.axis_index("space")
    beyond = [(i, i + 1) for i in range(1, count - 1, 2)]
    beyond += [(target, source) for source, target in beyond]

    def shape(n, dtype=BF16):
        return jax.ShapeDtypeStruct((n * CHAN, width), dtype)

    def vmem(n):
        return pltpu.VMEM((n * STACK, width), BF16)

    def neighbours(near, far):
        from_far = lax.ppermute(far, "space", beyond)
        return exchange(near, 1, count), from_far

    row_flops = 2 * CHAN * 9 * CHAN * width * 4
    grad = jax.ShapeDtypeStruct((STACK, STACK), F32)
    tile = jax.ShapeDtypeStruct((CHAN, rows, width), BF16)
    wide = pltpu.VMEM((rows, CHAN, width), F32)
    half = (CHAN, 18 * CHAN)
    entry = [pltpu.VMEM((CHAN, rows, width), BF16), pltpu.SemaphoreType.DMA((PIECES,))]

    x, x_near, x_far = call(
        functools.partial(entry_kernel, 4), (features,), (shape(rows), shape(4), shape(4)),
        entry, 0, "x_rows", place=HBM,
    )
    xnear, xfar = neighbours(x_near, x_far)
    (weights,) = call(
        weights_kernel, (kernels,), (jax.ShapeDtypeStruct((8, 2 * CHAN, 4 * STACK), BF16),), [],
        row_flops, "weights", after=(x_far,),
    )
    inner = call(
        functools.partial(inner_kernel, rows), (x, weights),
        (shape(rows - 2), shape(rows - 4), shape(rows - 6)),
        [vmem(rows), vmem(rows - 2), vmem(rows - 4)], 12 * row_flops, "inner",
    )
    g, g_near, g_far, g_inner = call(
        functools.partial(g_entry_kernel, 2), (cotangent, weights),
        (shape(rows), shape(2), shape(2), shape(rows - 2, F32)),
        [entry[0], vmem(rows), entry[1]], 6 * row_flops, "g_rows", after=(inner[2],), place=HBM,
    )
    gnear, gfar = neighbours(g_near, g_far)
    hid0, x1, hid1 = call(
        functools.partial(forward_kernel, rows, height), (x, xnear, xfar, weights, *inner),
        (shape(rows + 2),) * 3, [vmem(rows + 8), vmem(rows + 6), vmem(rows + 4)],
        24 * row_flops, "forward",
    )
    g1_near, g1_far, edges, dh1 = call(
        functools.partial(backward1_kernel, rows), (g, gnear, gfar, hid1, g_inner, weights),
        (shape(1), shape(1), shape(4), shape(rows + 2)),
        [vmem(rows + 4), vmem(rows + 2)], 8 * row_flops, "backward1",
    )
    g1near, g1far = neighbours(g1_near, g1_far)
    g1, dh0_inner, *grads = call(
        functools.partial(middle_kernel, rows), (g, edges, hid1, dh1, x1, hid0, x, weights),
        (shape(rows), shape(rows - 4)) + (grad,) * 4,
        [vmem(rows), vmem(rows + 2), vmem(rows), vmem(rows - 4)], 36 * row_flops, "middle",
    )
    dh0, dh0_near, dh0_far, part, send = call(
        functools.partial(backward0_kernel, rows, scale),
        (g1, g1near, g1far, hid0, x, xnear, xfar, weights, *grads),
        (shape(4), shape(1), shape(1), jax.ShapeDtypeStruct(half, F32),
         jax.ShapeDtypeStruct(half, BF16)),
        [vmem(rows + 2), vmem(4), pltpu.VMEM((8 * CHAN, width), BF16),
         pltpu.VMEM((2, *half), F32)],
        8 * row_flops, "backward0",
    )

    part = part + exchange(send, 1, count).astype(F32)
    low, high = part[: CHAN // 2], part[CHAN // 2 :]
    bit = (place & 2) != 0
    send = jnp.where(bit, low, high).astype(BF16)
    part = jnp.where(bit, high, low)
    arrived = exchange(send, 2, count)
    dh0_near, dh0_far, _ = lax.optimization_barrier((dh0_near, dh0_far, send))
    dh0near, dh0far = neighbours(dh0_near, dh0_far)
    part = part + arrived.astype(F32)
    step = 4
    input_grad = None
    while step < count:
        send = part.astype(BF16)
        masks = [step, 2 * step, 3 * step] if 2 * step < count else [step]
        arrived = [exchange(send, mask, count) for mask in masks]
        if input_grad is None:
            (input_grad,) = call(
                functools.partial(input_grad_kernel, rows), (dh0_inner, dh0, dh0near, dh0far, g1, weights),
                (tile,),
                [vmem(rows + 2), wide], 8 * row_flops, "input_grad", after=(send,),
            )
            arrived, input_grad = lax.optimization_barrier((arrived, input_grad))
        own = send.astype(F32)
        arrived = [value.astype(F32) for value in arrived]
        part = own + arrived[0]
        if len(masks) == 3:
            part = part + (arrived[1] + arrived[2])
        step *= len(masks) + 1
    done = part.astype(BF16)
    bit = (place & 2) != 0
    other = exchange(done, 2, count)
    (section_output,) = call(
        functools.partial(output_kernel, rows), (hid1, x1, weights), (tile,),
        [vmem(rows + 2), wide], 8 * row_flops, "output", after=(done,),
    )
    other, section_output = lax.optimization_barrier((other, section_output))
    done = jnp.where(bit, jnp.concatenate([other, done]), jnp.concatenate([done, other]))
    (kernel_grad,) = call(
        gathered_kernel, (done, exchange(done, 1, count)),
        (jax.ShapeDtypeStruct((2, 2, CHAN, 9 * CHAN), F32),), [], 0, "gathered",
    )
    return (section_output, input_grad, kernel_grad)


def solution(mesh):
    return jax.shard_map(
        local,
        mesh=mesh,
        in_specs=(P(None, "space", "groups"), P(None, "space", "groups"), P()),
        out_specs=(
            P(None, "space", "groups"),
            P(None, "space", "groups"),
            P("groups", None, None, None),
        ),
        check_vma=False,
    )
```

```python
import functools
import math

import jax
import jax.numpy as jnp
from jax import lax
from jax.experimental import pallas as pl
from jax.experimental.pallas import tpu as pltpu
from jax.sharding import PartitionSpec as P

CHAN = 64
STACK = 3 * CHAN
F32 = jnp.float32
BF16 = jnp.bfloat16
VMEM = pl.BlockSpec(memory_space=pltpu.VMEM)
ANY = pl.BlockSpec(memory_space=pl.ANY)
HBM = pl.BlockSpec(memory_space=pltpu.HBM)
PIECES = 4


def call(body, operands, outs, scratch, flops, name, after=(), place=VMEM, to_hbm=()):
    nbytes = sum(v.size * v.dtype.itemsize for v in (*operands, *outs))
    held = sum(math.prod(v.shape) * v.dtype.itemsize for v in scratch if v.dtype in (F32, BF16))

    def kernel(*refs):
        body(*refs[len(after) :])

    return pl.pallas_call(
        kernel,
        out_shape=outs,
        in_specs=[ANY] * len(after) + [place] + [VMEM] * (len(operands) - 1),
        out_specs=[HBM if i in to_hbm else VMEM for i in range(len(outs))],
        scratch_shapes=scratch,
        compiler_params=pltpu.CompilerParams(vmem_limit_bytes=nbytes + held + (6 << 20)),
        cost_estimate=pl.CostEstimate(flops=flops, bytes_accessed=nbytes, transcendentals=0),
        name=name,
    )(*after, *operands)


def stacked(field):
    width = field.shape[1]
    lane = lax.broadcasted_iota(jnp.int32, field.shape, 1)
    zero = jnp.zeros_like(field)
    left = jnp.where(lane == 0, zero, pltpu.roll(field, 1, 1))
    right = jnp.where(lane == width - 1, zero, pltpu.roll(field, width - 1, 1))
    return jnp.concatenate([left, field, right], axis=0)


def put(ref, row, field):
    ref[row * STACK : (row + 1) * STACK, :] = stacked(field)


def middle(ref, row):
    return ref[row * STACK + CHAN : row * STACK + 2 * CHAN, :]


def one(ref, row):
    return ref[row * CHAN : (row + 1) * CHAN, :]


def stack_rows(ref, rows, target, at):
    for row in rows:
        put(target, row + at, one(ref, row))


def g_entry_kernel(
    edge, tile_ref, w_ref, rows_ref, near_ref, far_ref, inner_ref, held, g3, arrived
):
    entry_kernel(edge, tile_ref, rows_ref, near_ref, far_ref, held, arrived)
    rows = tile_ref.shape[1]
    stack_rows(rows_ref, range(rows), g3, 0)

    def keep(row, total):
        inner_ref[row * CHAN : (row + 1) * CHAN, :] = total

    conv_rows(w_ref[7], g3, 0, rows - 2, keep)


def copy_rows(ref, count, target, at):
    target[at * CHAN : (at + count) * CHAN, :] = ref[: count * CHAN, :]


def two_rows(target, index, column, value):
    width = value.shape[1]
    target[index, :CHAN, column : column + width] = value
    target[index, CHAN:, STACK + column : STACK + column + width] = value


def weights_kernel(kernels_ref, target):
    target[...] = jnp.zeros_like(target)
    line = lax.broadcasted_iota(jnp.int32, (CHAN, CHAN), 0)
    same = line == lax.broadcasted_iota(jnp.int32, (CHAN, CHAN), 1)
    unit = jnp.where(same, 1.0, 0.0).astype(BF16)
    for section in range(2):
        for which in range(2):
            index = 2 * (2 * section + which)
            two_rows(target, index, 0, kernels_ref[section, which])
            for tap in range(9):
                at = (8 - tap) * CHAN
                block = kernels_ref[section, which, :, at : at + CHAN]
                turned = lax.dot_general(
                    unit, block, (((1,), (1,)), ((), ())), preferred_element_type=F32
                )
                two_rows(target, index + 1, tap * CHAN, turned.astype(BF16))


def conv_rows(weight, source, first, count, finish):
    for row in range(first, first + count, 2):
        total = jnp.dot(
            weight,
            source[row * STACK : (row + 4) * STACK, :],
            preferred_element_type=F32,
        )
        finish(row, total[:CHAN])
        finish(row + 1, total[CHAN:])


def grad_rows(upper, upper_row, lower, lower_row, count):
    total = None
    for row in range(0, count, 2):
        left = upper[(row + upper_row) * STACK : (row + upper_row + 2) * STACK, :]
        right = lower[(row + lower_row) * CHAN : (row + lower_row + 4) * CHAN, :]
        term = lax.dot_general(
            left, right, (((1,), (1,)), ((), ())), preferred_element_type=F32
        )
        total = term if total is None else total + term
    return total[:STACK, :STACK] + total[STACK:, CHAN:]


def channels_first(wide, target):
    target[...] = jnp.swapaxes(wide[...], 0, 1).astype(BF16)


def odd_place():
    return lax.rem(lax.axis_index("space"), 2) == 1


def put_at(ref, row, field):
    ref[pl.ds(pl.multiple_of(row * STACK, CHAN), STACK), :] = stacked(field)


def halo_rows(near_ref, far_ref, count, rows, target):
    odd = odd_place()
    above, below = 0, rows + count
    near_at = jnp.where(odd, above, below)
    far_at = jnp.where(odd, below, above)
    for row in range(count):
        put_at(target, near_at + row, one(near_ref, row))
        put_at(target, far_at + row, one(far_ref, row))


def send_edges(rows_ref, edge, near_ref, far_ref):
    odd = odd_place()
    last = rows_ref.shape[0] - edge * CHAN
    near_at = jnp.where(odd, 0, last)
    far_at = jnp.where(odd, last, 0)
    near_ref[...] = rows_ref[pl.ds(pl.multiple_of(near_at, CHAN), edge * CHAN), :]
    far_ref[...] = rows_ref[pl.ds(pl.multiple_of(far_at, CHAN), edge * CHAN), :]


def entry_kernel(edge, tile_ref, rows_ref, near_ref, far_ref, held, arrived):
    piece = CHAN // PIECES
    copies = [
        pltpu.make_async_copy(
            tile_ref.at[i * piece : (i + 1) * piece],
            held.at[i * piece : (i + 1) * piece],
            arrived.at[i],
        )
        for i in range(PIECES)
    ]
    for copy in copies:
        copy.start()
    for i, copy in enumerate(copies):
        copy.wait()
        part = held[i * piece : (i + 1) * piece].astype(F32)
        turned = jnp.swapaxes(part, 0, 1).astype(BF16)
        for row in range(turned.shape[0]):
            at = row * CHAN + i * piece
            rows_ref[at : at + piece, :] = turned[row]
    send_edges(rows_ref, edge, near_ref, far_ref)


def channels_first(wide, target):
    target[...] = jnp.swapaxes(wide[...], 0, 1).astype(BF16)


def inner_kernel(rows, x_ref, w_ref, hid0_ref, x1_ref, hid1_ref, x3, h3, y3):
    stack_rows(x_ref, range(rows), x3, 0)

    def hidden0(row, total):
        value = jnp.maximum(total, 0.0).astype(BF16)
        put(h3, row, value)
        hid0_ref[row * CHAN : (row + 1) * CHAN, :] = value

    conv_rows(w_ref[0], x3, 0, rows - 2, hidden0)

    def next_x(row, total):
        value = (one(x_ref, row + 2).astype(F32) + total).astype(BF16)
        put(y3, row, value)
        x1_ref[row * CHAN : (row + 1) * CHAN, :] = value

    conv_rows(w_ref[2], h3, 0, rows - 4, next_x)

    def hidden1(row, total):
        hid1_ref[row * CHAN : (row + 1) * CHAN, :] = jnp.maximum(total, 0.0).astype(BF16)

    conv_rows(w_ref[4], y3, 0, rows - 6, hidden1)


def at_row(ref, row, count=1):
    return ref.at[pl.ds(pl.multiple_of(row * CHAN, CHAN), count * CHAN), :]


def side_rows(rows, height, top, x_ref, halo_ref, w_ref, hid0_in, x1_in, hid0, x1, hid1, x3, h3, y3):
    first = lax.axis_index("space") * rows
    own = jnp.where(top, 0, 2)
    rest = jnp.where(top, 4, 0)

    def inside(row, value):
        keep = jnp.logical_and(first + row >= 0, first + row < height)
        return jnp.where(keep, value, 0.0)

    for i in range(4):
        put_at(x3, own + i, one(halo_ref, i))
    for i in range(2):
        put_at(x3, rest + i, at_row(x_ref, jnp.where(top, 0, rows - 2) + i)[...])
        put_at(h3, rest + i, at_row(hid0_in, jnp.where(top, 0, rows - 4) + i)[...])
        put_at(y3, rest + i, at_row(x1_in, jnp.where(top, 0, rows - 6) + i)[...])

    def hidden0(row, total):
        at = jnp.where(top, -3, rows - 1) + row
        value = inside(at, jnp.maximum(total, 0.0)).astype(BF16)
        hid0[row * CHAN : (row + 1) * CHAN, :] = value
        put_at(h3, own + row, value)

    conv_rows(w_ref[0], x3, 0, 4, hidden0)

    def next_x(row, total):
        at = jnp.where(top, -2, rows - 2) + row
        start = pl.multiple_of((jnp.where(top, 2, 0) + row) * STACK + CHAN, CHAN)
        value = inside(at, x3[pl.ds(start, CHAN), :].astype(F32) + total).astype(BF16)
        x1[row * CHAN : (row + 1) * CHAN, :] = value
        put_at(y3, own + row, value)

    conv_rows(w_ref[2], h3, 0, 4, next_x)

    def hidden1(row, total):
        at = jnp.where(top, -1, rows - 3) + row
        value = inside(at, jnp.maximum(total, 0.0)).astype(BF16)
        hid1[row * CHAN : (row + 1) * CHAN, :] = value

    conv_rows(w_ref[4], y3, 0, 4, hidden1)


def near_kernel(rows, height, *refs):
    side_rows(rows, height, odd_place(), *refs)


def far_kernel(
    rows, height, x_ref, far_ref, w_ref, hid0_in, x1_in, hid1_in, near0, near1, near2,
    hid0_ref, x1_ref, hid1_ref, far0, far1, far2, *scratch,
):
    odd = odd_place()
    side_rows(
        rows, height, jnp.logical_not(odd), x_ref, far_ref, w_ref, hid0_in, x1_in, far0, far1, far2,
        *scratch,
    )
    copy_rows(hid0_in, rows - 2, hid0_ref, 2)
    copy_rows(x1_in, rows - 4, x1_ref, 3)
    copy_rows(hid1_in, rows - 6, hid1_ref, 4)
    sides = ((odd, near0, near1, near2), (jnp.logical_not(odd), far0, far1, far2))
    for top, hid0, x1, hid1 in sides:
        for target, source, count in ((hid0_ref, hid0, 2), (x1_ref, x1, 3), (hid1_ref, hid1, 4)):
            to = at_row(target, jnp.where(top, 0, rows + 2 - count), count)
            to[...] = at_row(source, jnp.where(top, 4 - count, 0), count)[...]


def backward1_kernel(
    rows, g_ref, near_ref, far_ref, hid1_ref, inner_ref, w_ref, next_near, next_far, edges_ref, dh1_ref,
    g3, d3,
):
    halo_rows(near_ref, far_ref, 2, rows, g3)
    stack_rows(g_ref, (0, 1, rows - 2, rows - 1), g3, 2)

    def dhidden1(row, total):
        value = jnp.where(one(hid1_ref, row) > 0, total, 0.0).astype(BF16)
        dh1_ref[row * CHAN : (row + 1) * CHAN, :] = value
        if row < 4 or row >= rows - 2:
            put(d3, row, value)

    for row in range(2, rows):
        dhidden1(row, one(inner_ref, row - 2))
    for at in (0, rows):
        conv_rows(w_ref[7], g3, at, 2, dhidden1)

    def next_g(row, total):
        value = (one(g_ref, row).astype(F32) + total).astype(BF16)
        at = row if row < 2 else row - (rows - 4)
        edges_ref[at * CHAN : (at + 1) * CHAN, :] = value

    for at in (0, rows - 2):
        conv_rows(w_ref[5], d3, at, 2, next_g)
    send_edges(edges_ref, 1, next_near, next_far)


def middle_kernel(
    rows, g_ref, edges_ref, hid1_ref, dh1_ref, x1_ref, hid0_ref, x_ref, w_ref,
    g1_ref, dh0_out, grad00, grad01, grad10, grad11, s3, t3, u3, v3, dh0_ref, copied,
):
    stack_rows(dh1_ref, range(rows + 2), t3, 0)
    copy_rows(edges_ref, 2, g1_ref, 0)
    g1_ref[(rows - 2) * CHAN :, :] = edges_ref[2 * CHAN :, :]

    def next_g(row, total):
        value = (one(g_ref, row).astype(F32) + total).astype(BF16)
        g1_ref[row * CHAN : (row + 1) * CHAN, :] = value
        put(u3, row, value)

    conv_rows(w_ref[5], t3, 2, rows - 4, next_g)
    stack_rows(g1_ref, (0, 1, rows - 2, rows - 1), u3, 0)

    def dhidden0(row, total):
        value = jnp.where(one(hid0_ref, row + 2) > 0, total, 0.0).astype(BF16)
        dh0_ref[(row - 1) * CHAN : row * CHAN, :] = value
        put(v3, row - 1, value)

    conv_rows(w_ref[3], u3, 1, rows - 4, dhidden0)
    copy = pltpu.make_async_copy(dh0_ref, dh0_out, copied)
    copy.start()
    stack_rows(g_ref, range(rows), s3, 0)
    grad11[...] = grad_rows(s3, 0, hid1_ref, 0, rows)
    grad10[...] = grad_rows(t3, 1, x1_ref, 0, rows)
    grad01[...] = grad_rows(u3, 0, hid0_ref, 0, rows)
    grad00[...] = grad_rows(v3, 0, x_ref, 1, rows - 4)
    copy.wait()


def output_kernel(rows, hid1_ref, x1_ref, w_ref, out_ref, k3, wide):
    stack_rows(hid1_ref, range(rows + 2), k3, 0)

    def last_x(row, total):
        wide[row] = one(x1_ref, row + 1).astype(F32) + total

    conv_rows(w_ref[6], k3, 0, rows, last_x)
    channels_first(wide, out_ref)


def backward0_kernel(
    rows, scale, g1_ref, near_ref, far_ref, hid0_ref, x_ref, xnear_ref, xfar_ref, w_ref, inner00,
    grad01, grad10, grad11, dh0_out, next_near, next_far, keep_ref, send_ref,
    g3, d3, xs, both, dh0_ref, copied,
):
    halo_rows(near_ref, far_ref, 1, rows, g3)
    stack_rows(g1_ref, (0, 1, 2, rows - 3, rows - 2, rows - 1), g3, 1)

    def dhidden0(row, total):
        value = jnp.where(one(hid0_ref, row + 1) > 0, total, 0.0).astype(BF16)
        at = row if row < 2 else row - (rows - 4)
        dh0_ref[at * CHAN : (at + 1) * CHAN, :] = value
        put(d3, at, value)

    for at in (0, rows - 2):
        conv_rows(w_ref[3], g3, at, 2, dhidden0)
    copy = pltpu.make_async_copy(dh0_ref, dh0_out, copied)
    copy.start()
    send_edges(dh0_ref, 1, next_near, next_far)
    odd = odd_place()
    copy_rows(x_ref, 3, xs, 1)
    xs[4 * CHAN : 7 * CHAN, :] = x_ref[(rows - 3) * CHAN :, :]
    near_at, far_at = jnp.where(odd, 0, 7), jnp.where(odd, 7, 0)
    near_row, far_row = jnp.where(odd, 3, 0), jnp.where(odd, 0, 3)
    for ref, at, row in ((xnear_ref, near_at, near_row), (xfar_ref, far_at, far_row)):
        source = pl.ds(pl.multiple_of(row * CHAN, CHAN), CHAN)
        xs[pl.ds(pl.multiple_of(at * CHAN, CHAN), CHAN), :] = ref[source, :]
    grad00 = inner00[...] + grad_rows(d3, 0, xs, 0, 2) + grad_rows(d3, 2, xs, 4, 2)
    pairs = ((grad00, grad01[...]), (grad10[...], grad11[...]))
    for section, pair in enumerate(pairs):
        for which, value in enumerate(pair):
            for a in range(3):
                for b in range(3):
                    block = value[(2 - b) * CHAN : (3 - b) * CHAN, a * CHAN : (a + 1) * CHAN]
                    at = which * 9 * CHAN + (3 * a + b) * CHAN
                    both[section, :, at : at + CHAN] = block * scale
    mine = lax.rem(lax.axis_index("space"), 2)
    keep_ref[...] = both[mine]
    send_ref[...] = both[1 - mine].astype(BF16)
    copy.wait()


def input_grad_kernel(rows, dh0_in, dh0_ref, near_ref, far_ref, g1_ref, w_ref, out_ref, d3, wide):
    halo_rows(near_ref, far_ref, 1, rows, d3)
    stack_rows(dh0_in, range(rows - 4), d3, 3)
    stack_rows(dh0_ref, (0, 1), d3, 1)
    stack_rows(dh0_ref, (2, 3), d3, rows - 3)

    def last_g(row, total):
        wide[row] = one(g1_ref, row).astype(F32) + total

    conv_rows(w_ref[1], d3, 0, rows, last_g)
    channels_first(wide, out_ref)


def gathered_kernel(own_ref, other_ref, out_ref):
    mine = lax.rem(lax.axis_index("space"), 2)
    for section, ref in ((mine, own_ref), (1 - mine, other_ref)):
        for which in range(2):
            piece = ref[:, which * 9 * CHAN : (which + 1) * 9 * CHAN]
            out_ref[section, which] = piece.astype(F32)


def exchange(value, mask, count):
    return lax.ppermute(value, "space", [(d, d ^ mask) for d in range(count)])


def local(features, cotangent, kernels):
    rows, width = features.shape[1], features.shape[2]
    count = lax.axis_size("space")
    height = rows * count
    scale = 1.0 / math.sqrt(height * width)
    place = lax.axis_index("space")
    beyond = [(i, i + 1) for i in range(1, count - 1, 2)]
    beyond += [(target, source) for source, target in beyond]

    def shape(n, dtype=BF16):
        return jax.ShapeDtypeStruct((n * CHAN, width), dtype)

    def vmem(n):
        return pltpu.VMEM((n * STACK, width), BF16)

    def plain(n):
        return pltpu.VMEM((n * CHAN, width), BF16)

    one_copy = pltpu.SemaphoreType.DMA

    def neighbours(near, far):
        from_far = lax.ppermute(far, "space", beyond)
        return exchange(near, 1, count), from_far

    row_flops = 2 * CHAN * 9 * CHAN * width * 4
    grad = jax.ShapeDtypeStruct((STACK, STACK), F32)
    tile = jax.ShapeDtypeStruct((CHAN, rows, width), BF16)
    wide = pltpu.VMEM((rows, CHAN, width), F32)
    half = (CHAN, 18 * CHAN)
    entry = [pltpu.VMEM((CHAN, rows, width), BF16), pltpu.SemaphoreType.DMA((PIECES,))]

    x, x_near, x_far = call(
        functools.partial(entry_kernel, 4), (features,), (shape(rows), shape(4), shape(4)),
        entry, 0, "x_rows", place=HBM,
    )
    xnear, xfar = neighbours(x_near, x_far)
    (weights,) = call(
        weights_kernel, (kernels,), (jax.ShapeDtypeStruct((8, 2 * CHAN, 4 * STACK), BF16),), [],
        row_flops, "weights", after=(x_far,),
    )
    inner = call(
        functools.partial(inner_kernel, rows), (x, weights),
        (shape(rows - 2), shape(rows - 4), shape(rows - 6)),
        [vmem(rows), vmem(rows - 2), vmem(rows - 4)], 12 * row_flops, "inner",
    )
    g, g_near, g_far, g_inner = call(
        functools.partial(g_entry_kernel, 2), (cotangent, weights),
        (shape(rows), shape(2), shape(2), shape(rows - 2, F32)),
        [entry[0], vmem(rows), entry[1]], 6 * row_flops, "g_rows", after=(inner[2],), place=HBM,
    )
    gnear, gfar = neighbours(g_near, g_far)
    near = call(
        functools.partial(near_kernel, rows, height), (x, xnear, weights, inner[0], inner[1]),
        (shape(4),) * 3, [vmem(6)] * 3, 12 * row_flops, "forward_near", after=(g_near,),
    )
    hid0, x1, hid1 = call(
        functools.partial(far_kernel, rows, height), (x, xfar, weights, *inner, *near),
        (shape(rows + 2),) * 3, [plain(4)] * 3 + [vmem(6)] * 3, 12 * row_flops, "forward_far",
    )
    g1_near, g1_far, edges, dh1 = call(
        functools.partial(backward1_kernel, rows), (g, gnear, gfar, hid1, g_inner, weights),
        (shape(1), shape(1), shape(4), shape(rows + 2)),
        [vmem(rows + 4), vmem(rows + 2)], 8 * row_flops, "backward1",
    )
    g1near, g1far = neighbours(g1_near, g1_far)
    g1, dh0_inner, *grads = call(
        functools.partial(middle_kernel, rows), (g, edges, hid1, dh1, x1, hid0, x, weights),
        (shape(rows), shape(rows - 4)) + (grad,) * 4,
        [vmem(rows), vmem(rows + 2), vmem(rows), vmem(rows - 4), plain(rows - 4), one_copy],
        36 * row_flops, "middle", to_hbm=(1,),
    )
    dh0, dh0_near, dh0_far, part, send = call(
        functools.partial(backward0_kernel, rows, scale),
        (g1, g1near, g1far, hid0, x, xnear, xfar, weights, *grads),
        (shape(4), shape(1), shape(1), jax.ShapeDtypeStruct(half, F32),
         jax.ShapeDtypeStruct(half, BF16)),
        [vmem(rows + 2), vmem(4), pltpu.VMEM((8 * CHAN, width), BF16),
         pltpu.VMEM((2, *half), F32), plain(4), one_copy],
        8 * row_flops, "backward0", to_hbm=(0,),
    )

    part = part + exchange(send, 1, count).astype(F32)
    low, high = part[: CHAN // 2], part[CHAN // 2 :]
    bit = (place & 2) != 0
    send = jnp.where(bit, low, high).astype(BF16)
    part = jnp.where(bit, high, low)
    arrived = exchange(send, 2, count)
    dh0_near, dh0_far, _ = lax.optimization_barrier((dh0_near, dh0_far, send))
    dh0near, dh0far = neighbours(dh0_near, dh0_far)
    part = part + arrived.astype(F32)
    step = 4
    input_grad = None
    while step < count:
        send = part.astype(BF16)
        masks = [step, 2 * step, 3 * step] if 2 * step < count else [step]
        arrived = [exchange(send, mask, count) for mask in masks]
        if input_grad is None:
            (input_grad,) = call(
                functools.partial(input_grad_kernel, rows), (dh0_inner, dh0, dh0near, dh0far, g1, weights),
                (tile,),
                [vmem(rows + 2), wide], 8 * row_flops, "input_grad", after=(send,),
            )
            arrived, input_grad = lax.optimization_barrier((arrived, input_grad))
        own = send.astype(F32)
        arrived = [value.astype(F32) for value in arrived]
        part = own + arrived[0]
        if len(masks) == 3:
            part = part + (arrived[1] + arrived[2])
        step *= len(masks) + 1
    done = part.astype(BF16)
    bit = (place & 2) != 0
    other = exchange(done, 2, count)
    (section_output,) = call(
        functools.partial(output_kernel, rows), (hid1, x1, weights), (tile,),
        [vmem(rows + 2), wide], 8 * row_flops, "output", after=(done,),
    )
    other, section_output = lax.optimization_barrier((other, section_output))
    done = jnp.where(bit, jnp.concatenate([other, done]), jnp.concatenate([done, other]))
    (kernel_grad,) = call(
        gathered_kernel, (done, exchange(done, 1, count)),
        (jax.ShapeDtypeStruct((2, 2, CHAN, 9 * CHAN), F32),), [], 0, "gathered",
    )
    return (section_output, input_grad, kernel_grad)


def solution(mesh):
    return jax.shard_map(
        local,
        mesh=mesh,
        in_specs=(P(None, "space", "groups"), P(None, "space", "groups"), P()),
        out_specs=(
            P(None, "space", "groups"),
            P(None, "space", "groups"),
            P("groups", None, None, None),
        ),
        check_vma=False,
    )
```

```python
import functools
import math

import jax
import jax.numpy as jnp
from jax import lax
from jax.experimental import pallas as pl
from jax.experimental.pallas import tpu as pltpu
from jax.sharding import PartitionSpec as P

CHAN = 64
STACK = 3 * CHAN
F32 = jnp.float32
BF16 = jnp.bfloat16
VMEM = pl.BlockSpec(memory_space=pltpu.VMEM)
ANY = pl.BlockSpec(memory_space=pl.ANY)
HBM = pl.BlockSpec(memory_space=pltpu.HBM)
PIECES = 4


def call(body, operands, outs, scratch, flops, name, after=(), place=VMEM):
    nbytes = sum(v.size * v.dtype.itemsize for v in (*operands, *outs))
    held = sum(math.prod(v.shape) * v.dtype.itemsize for v in scratch if v.dtype in (F32, BF16))

    def kernel(*refs):
        body(*refs[len(after) :])

    return pl.pallas_call(
        kernel,
        out_shape=outs,
        in_specs=[ANY] * len(after) + [place] + [VMEM] * (len(operands) - 1),
        out_specs=[VMEM] * len(outs),
        scratch_shapes=scratch,
        compiler_params=pltpu.CompilerParams(vmem_limit_bytes=nbytes + held + (6 << 20)),
        cost_estimate=pl.CostEstimate(flops=flops, bytes_accessed=nbytes, transcendentals=0),
        name=name,
    )(*after, *operands)


def stacked(field):
    width = field.shape[1]
    lane = lax.broadcasted_iota(jnp.int32, field.shape, 1)
    zero = jnp.zeros_like(field)
    left = jnp.where(lane == 0, zero, pltpu.roll(field, 1, 1))
    right = jnp.where(lane == width - 1, zero, pltpu.roll(field, width - 1, 1))
    return jnp.concatenate([left, field, right], axis=0)


def put(ref, row, field):
    ref[row * STACK : (row + 1) * STACK, :] = stacked(field)


def middle(ref, row):
    return ref[row * STACK + CHAN : row * STACK + 2 * CHAN, :]


def one(ref, row):
    return ref[row * CHAN : (row + 1) * CHAN, :]


def stack_rows(ref, rows, target, at):
    for row in rows:
        put(target, row + at, one(ref, row))


def g_entry_kernel(
    edge, tile_ref, w_ref, rows_ref, near_ref, far_ref, inner_ref, held, g3, arrived
):
    entry_kernel(edge, tile_ref, rows_ref, near_ref, far_ref, held, arrived)
    rows = tile_ref.shape[1]
    stack_rows(rows_ref, range(rows), g3, 0)

    def keep(row, total):
        inner_ref[row * CHAN : (row + 1) * CHAN, :] = total

    conv_rows(w_ref[7], g3, 0, rows - 2, keep)


def copy_rows(ref, count, target, at):
    target[at * CHAN : (at + count) * CHAN, :] = ref[: count * CHAN, :]


def two_rows(target, index, column, value):
    width = value.shape[1]
    target[index, :CHAN, column : column + width] = value
    target[index, CHAN:, STACK + column : STACK + column + width] = value


def weights_kernel(kernels_ref, target):
    target[...] = jnp.zeros_like(target)
    line = lax.broadcasted_iota(jnp.int32, (CHAN, CHAN), 0)
    same = line == lax.broadcasted_iota(jnp.int32, (CHAN, CHAN), 1)
    unit = jnp.where(same, 1.0, 0.0).astype(BF16)
    for section in range(2):
        for which in range(2):
            index = 2 * (2 * section + which)
            two_rows(target, index, 0, kernels_ref[section, which])
            for tap in range(9):
                at = (8 - tap) * CHAN
                block = kernels_ref[section, which, :, at : at + CHAN]
                turned = lax.dot_general(
                    unit, block, (((1,), (1,)), ((), ())), preferred_element_type=F32
                )
                two_rows(target, index + 1, tap * CHAN, turned.astype(BF16))


def conv_rows(weight, source, first, count, finish):
    for row in range(first, first + count, 2):
        total = jnp.dot(
            weight,
            source[row * STACK : (row + 4) * STACK, :],
            preferred_element_type=F32,
        )
        finish(row, total[:CHAN])
        finish(row + 1, total[CHAN:])


def grad_rows(upper, upper_row, lower, lower_row, count):
    total = None
    for row in range(0, count, 2):
        left = upper[(row + upper_row) * STACK : (row + upper_row + 2) * STACK, :]
        right = lower[(row + lower_row) * CHAN : (row + lower_row + 4) * CHAN, :]
        term = lax.dot_general(
            left, right, (((1,), (1,)), ((), ())), preferred_element_type=F32
        )
        total = term if total is None else total + term
    return total[:STACK, :STACK] + total[STACK:, CHAN:]


def channels_first(wide, target):
    target[...] = jnp.swapaxes(wide[...], 0, 1).astype(BF16)


def odd_place():
    return lax.rem(lax.axis_index("space"), 2) == 1


def put_at(ref, row, field):
    ref[pl.ds(pl.multiple_of(row * STACK, CHAN), STACK), :] = stacked(field)


def halo_rows(near_ref, far_ref, count, rows, target):
    odd = odd_place()
    above, below = 0, rows + count
    near_at = jnp.where(odd, above, below)
    far_at = jnp.where(odd, below, above)
    for row in range(count):
        put_at(target, near_at + row, one(near_ref, row))
        put_at(target, far_at + row, one(far_ref, row))


def send_edges(rows_ref, edge, near_ref, far_ref):
    odd = odd_place()
    last = rows_ref.shape[0] - edge * CHAN
    near_at = jnp.where(odd, 0, last)
    far_at = jnp.where(odd, last, 0)
    near_ref[...] = rows_ref[pl.ds(pl.multiple_of(near_at, CHAN), edge * CHAN), :]
    far_ref[...] = rows_ref[pl.ds(pl.multiple_of(far_at, CHAN), edge * CHAN), :]


def entry_kernel(edge, tile_ref, rows_ref, near_ref, far_ref, held, arrived):
    piece = CHAN // PIECES
    copies = [
        pltpu.make_async_copy(
            tile_ref.at[i * piece : (i + 1) * piece],
            held.at[i * piece : (i + 1) * piece],
            arrived.at[i],
        )
        for i in range(PIECES)
    ]
    for copy in copies:
        copy.start()
    for i, copy in enumerate(copies):
        copy.wait()
        part = held[i * piece : (i + 1) * piece].astype(F32)
        turned = jnp.swapaxes(part, 0, 1).astype(BF16)
        for row in range(turned.shape[0]):
            at = row * CHAN + i * piece
            rows_ref[at : at + piece, :] = turned[row]
    send_edges(rows_ref, edge, near_ref, far_ref)


def channels_first(wide, target):
    target[...] = jnp.swapaxes(wide[...], 0, 1).astype(BF16)


def inner_kernel(rows, x_ref, w_ref, hid0_ref, x1_ref, hid1_ref, x3, h3, y3):
    stack_rows(x_ref, range(rows), x3, 0)

    def hidden0(row, total):
        value = jnp.maximum(total, 0.0).astype(BF16)
        put(h3, row, value)
        hid0_ref[row * CHAN : (row + 1) * CHAN, :] = value

    conv_rows(w_ref[0], x3, 0, rows - 2, hidden0)

    def next_x(row, total):
        value = (one(x_ref, row + 2).astype(F32) + total).astype(BF16)
        put(y3, row, value)
        x1_ref[row * CHAN : (row + 1) * CHAN, :] = value

    conv_rows(w_ref[2], h3, 0, rows - 4, next_x)

    def hidden1(row, total):
        hid1_ref[row * CHAN : (row + 1) * CHAN, :] = jnp.maximum(total, 0.0).astype(BF16)

    conv_rows(w_ref[4], y3, 0, rows - 6, hidden1)


def side_rows(rows, height, top, x_ref, halo_ref, w_ref, hid0_in, x1_in, hid0, x1, hid1, x3, h3, y3):
    first = lax.axis_index("space") * rows
    own, rest = (0, 4) if top else (2, 0)

    def inside(row, value):
        if 0 <= row < rows:
            return value
        keep = jnp.logical_and(first + row >= 0, first + row < height)
        return jnp.where(keep, value, 0.0)

    for i in range(4):
        put(x3, own + i, one(halo_ref, i))
    for i in range(2):
        put(x3, rest + i, one(x_ref, (0 if top else rows - 2) + i))
        put(h3, rest + i, one(hid0_in, (0 if top else rows - 4) + i))
        put(y3, rest + i, one(x1_in, (0 if top else rows - 6) + i))

    def hidden0(row, total):
        at = (-3 if top else rows - 1) + row
        value = inside(at, jnp.maximum(total, 0.0)).astype(BF16)
        hid0[row * CHAN : (row + 1) * CHAN, :] = value
        put(h3, own + row, value)

    conv_rows(w_ref[0], x3, 0, 4, hidden0)

    def next_x(row, total):
        at = (-2 if top else rows - 2) + row
        value = middle(x3, (2 if top else 0) + row).astype(F32) + total
        value = inside(at, value).astype(BF16)
        x1[row * CHAN : (row + 1) * CHAN, :] = value
        put(y3, own + row, value)

    conv_rows(w_ref[2], h3, 0, 4, next_x)

    def hidden1(row, total):
        at = (-1 if top else rows - 3) + row
        value = inside(at, jnp.maximum(total, 0.0)).astype(BF16)
        hid1[row * CHAN : (row + 1) * CHAN, :] = value

    conv_rows(w_ref[4], y3, 0, 4, hidden1)


def near_kernel(rows, height, *refs):
    odd = odd_place()
    for top in (True, False):
        pl.when(odd == top)(functools.partial(side_rows, rows, height, top, *refs))


def far_kernel(
    rows, height, x_ref, far_ref, w_ref, hid0_in, x1_in, hid1_in, near0, near1, near2,
    hid0_ref, x1_ref, hid1_ref, far0, far1, far2, *scratch,
):
    def far_side(top):
        side_rows(
            rows, height, top, x_ref, far_ref, w_ref, hid0_in, x1_in, far0, far1, far2, *scratch
        )
        for edge, hid0, x1, hid1 in ((top, far0, far1, far2), (not top, near0, near1, near2)):
            for target, source, count in ((hid0_ref, hid0, 2), (x1_ref, x1, 3), (hid1_ref, hid1, 4)):
                to = 0 if edge else rows + 2 - count
                at = 4 - count if edge else 0
                target[to * CHAN : (to + count) * CHAN, :] = source[at * CHAN : (at + count) * CHAN, :]

    copy_rows(hid0_in, rows - 2, hid0_ref, 2)
    copy_rows(x1_in, rows - 4, x1_ref, 3)
    copy_rows(hid1_in, rows - 6, hid1_ref, 4)
    odd = odd_place()
    for top in (True, False):
        pl.when(odd != top)(functools.partial(far_side, top))


def backward1_kernel(
    rows, g_ref, near_ref, far_ref, hid1_ref, inner_ref, w_ref, next_near, next_far, edges_ref, dh1_ref,
    g3, d3,
):
    halo_rows(near_ref, far_ref, 2, rows, g3)
    stack_rows(g_ref, (0, 1, rows - 2, rows - 1), g3, 2)

    def dhidden1(row, total):
        value = jnp.where(one(hid1_ref, row) > 0, total, 0.0).astype(BF16)
        dh1_ref[row * CHAN : (row + 1) * CHAN, :] = value
        if row < 4 or row >= rows - 2:
            put(d3, row, value)

    for row in range(2, rows):
        dhidden1(row, one(inner_ref, row - 2))
    for at in (0, rows):
        conv_rows(w_ref[7], g3, at, 2, dhidden1)

    def next_g(row, total):
        value = (one(g_ref, row).astype(F32) + total).astype(BF16)
        at = row if row < 2 else row - (rows - 4)
        edges_ref[at * CHAN : (at + 1) * CHAN, :] = value

    for at in (0, rows - 2):
        conv_rows(w_ref[5], d3, at, 2, next_g)
    send_edges(edges_ref, 1, next_near, next_far)


def middle_kernel(
    rows, g_ref, edges_ref, hid1_ref, dh1_ref, x1_ref, hid0_ref, x_ref, w_ref,
    g1_ref, dh0_ref, grad00, grad01, grad10, grad11, s3, t3, u3, v3,
):
    stack_rows(dh1_ref, range(rows + 2), t3, 0)
    copy_rows(edges_ref, 2, g1_ref, 0)
    g1_ref[(rows - 2) * CHAN :, :] = edges_ref[2 * CHAN :, :]

    def next_g(row, total):
        value = (one(g_ref, row).astype(F32) + total).astype(BF16)
        g1_ref[row * CHAN : (row + 1) * CHAN, :] = value
        put(u3, row, value)

    conv_rows(w_ref[5], t3, 2, rows - 4, next_g)
    stack_rows(g1_ref, (0, 1, rows - 2, rows - 1), u3, 0)

    def dhidden0(row, total):
        value = jnp.where(one(hid0_ref, row + 2) > 0, total, 0.0).astype(BF16)
        dh0_ref[(row - 1) * CHAN : row * CHAN, :] = value
        put(v3, row - 1, value)

    conv_rows(w_ref[3], u3, 1, rows - 4, dhidden0)
    stack_rows(g_ref, range(rows), s3, 0)
    grad11[...] = grad_rows(s3, 0, hid1_ref, 0, rows)
    grad10[...] = grad_rows(t3, 1, x1_ref, 0, rows)
    grad01[...] = grad_rows(u3, 0, hid0_ref, 0, rows)
    grad00[...] = grad_rows(v3, 0, x_ref, 1, rows - 4)


def output_kernel(rows, hid1_ref, x1_ref, w_ref, out_ref, k3, wide):
    stack_rows(hid1_ref, range(rows + 2), k3, 0)

    def last_x(row, total):
        wide[row] = one(x1_ref, row + 1).astype(F32) + total

    conv_rows(w_ref[6], k3, 0, rows, last_x)
    channels_first(wide, out_ref)


def backward0_kernel(
    rows, scale, g1_ref, near_ref, far_ref, hid0_ref, x_ref, xnear_ref, xfar_ref, w_ref, inner00,
    grad01, grad10, grad11, dh0_ref, next_near, next_far, keep_ref, send_ref,
    g3, d3, xs, both,
):
    halo_rows(near_ref, far_ref, 1, rows, g3)
    stack_rows(g1_ref, (0, 1, 2, rows - 3, rows - 2, rows - 1), g3, 1)

    def dhidden0(row, total):
        value = jnp.where(one(hid0_ref, row + 1) > 0, total, 0.0).astype(BF16)
        at = row if row < 2 else row - (rows - 4)
        dh0_ref[at * CHAN : (at + 1) * CHAN, :] = value
        put(d3, at, value)

    for at in (0, rows - 2):
        conv_rows(w_ref[3], g3, at, 2, dhidden0)
    send_edges(dh0_ref, 1, next_near, next_far)
    odd = odd_place()
    copy_rows(x_ref, 3, xs, 1)
    xs[4 * CHAN : 7 * CHAN, :] = x_ref[(rows - 3) * CHAN :, :]
    near_at, far_at = jnp.where(odd, 0, 7), jnp.where(odd, 7, 0)
    near_row, far_row = jnp.where(odd, 3, 0), jnp.where(odd, 0, 3)
    for ref, at, row in ((xnear_ref, near_at, near_row), (xfar_ref, far_at, far_row)):
        source = pl.ds(pl.multiple_of(row * CHAN, CHAN), CHAN)
        xs[pl.ds(pl.multiple_of(at * CHAN, CHAN), CHAN), :] = ref[source, :]
    grad00 = inner00[...] + grad_rows(d3, 0, xs, 0, 2) + grad_rows(d3, 2, xs, 4, 2)
    pairs = ((grad00, grad01[...]), (grad10[...], grad11[...]))
    for section, pair in enumerate(pairs):
        for which, value in enumerate(pair):
            for a in range(3):
                for b in range(3):
                    block = value[(2 - b) * CHAN : (3 - b) * CHAN, a * CHAN : (a + 1) * CHAN]
                    at = which * 9 * CHAN + (3 * a + b) * CHAN
                    both[section, :, at : at + CHAN] = block * scale
    mine = lax.rem(lax.axis_index("space"), 2)
    keep_ref[...] = both[mine]
    send_ref[...] = both[1 - mine].astype(BF16)


def input_grad_kernel(rows, dh0_in, dh0_ref, near_ref, far_ref, g1_ref, w_ref, out_ref, d3, wide):
    halo_rows(near_ref, far_ref, 1, rows, d3)
    stack_rows(dh0_in, range(rows - 4), d3, 3)
    stack_rows(dh0_ref, (0, 1), d3, 1)
    stack_rows(dh0_ref, (2, 3), d3, rows - 3)

    def last_g(row, total):
        wide[row] = one(g1_ref, row).astype(F32) + total

    conv_rows(w_ref[1], d3, 0, rows, last_g)
    channels_first(wide, out_ref)


def gathered_kernel(own_ref, other_ref, out_ref):
    mine = lax.rem(lax.axis_index("space"), 2)
    for section, ref in ((mine, own_ref), (1 - mine, other_ref)):
        for which in range(2):
            piece = ref[:, which * 9 * CHAN : (which + 1) * 9 * CHAN]
            out_ref[section, which] = piece.astype(F32)


def exchange(value, mask, count):
    return lax.ppermute(value, "space", [(d, d ^ mask) for d in range(count)])


def local(features, cotangent, kernels):
    rows, width = features.shape[1], features.shape[2]
    count = lax.axis_size("space")
    height = rows * count
    scale = 1.0 / math.sqrt(height * width)
    place = lax.axis_index("space")
    beyond = [(i, i + 1) for i in range(1, count - 1, 2)]
    beyond += [(target, source) for source, target in beyond]

    def shape(n, dtype=BF16):
        return jax.ShapeDtypeStruct((n * CHAN, width), dtype)

    def vmem(n):
        return pltpu.VMEM((n * STACK, width), BF16)

    def plain(n):
        return pltpu.VMEM((n * CHAN, width), BF16)

    def neighbours(near, far):
        from_far = lax.ppermute(far, "space", beyond)
        return exchange(near, 1, count), from_far

    row_flops = 2 * CHAN * 9 * CHAN * width * 4
    grad = jax.ShapeDtypeStruct((STACK, STACK), F32)
    tile = jax.ShapeDtypeStruct((CHAN, rows, width), BF16)
    wide = pltpu.VMEM((rows, CHAN, width), F32)
    half = (CHAN, 18 * CHAN)
    entry = [pltpu.VMEM((CHAN, rows, width), BF16), pltpu.SemaphoreType.DMA((PIECES,))]

    x, x_near, x_far = call(
        functools.partial(entry_kernel, 4), (features,), (shape(rows), shape(4), shape(4)),
        entry, 0, "x_rows", place=HBM,
    )
    xnear, xfar = neighbours(x_near, x_far)
    (weights,) = call(
        weights_kernel, (kernels,), (jax.ShapeDtypeStruct((8, 2 * CHAN, 4 * STACK), BF16),), [],
        row_flops, "weights", after=(x_far,),
    )
    inner = call(
        functools.partial(inner_kernel, rows), (x, weights),
        (shape(rows - 2), shape(rows - 4), shape(rows - 6)),
        [vmem(rows), vmem(rows - 2), vmem(rows - 4)], 12 * row_flops, "inner",
    )
    g, g_near, g_far, g_inner = call(
        functools.partial(g_entry_kernel, 2), (cotangent, weights),
        (shape(rows), shape(2), shape(2), shape(rows - 2, F32)),
        [entry[0], vmem(rows), entry[1]], 6 * row_flops, "g_rows", after=(inner[2],), place=HBM,
    )
    gnear, gfar = neighbours(g_near, g_far)
    near = call(
        functools.partial(near_kernel, rows, height), (x, xnear, weights, inner[0], inner[1]),
        (shape(4),) * 3, [vmem(6)] * 3, 12 * row_flops, "forward_near", after=(g_near,),
    )
    hid0, x1, hid1 = call(
        functools.partial(far_kernel, rows, height), (x, xfar, weights, *inner, *near),
        (shape(rows + 2),) * 3, [plain(4)] * 3 + [vmem(6)] * 3, 12 * row_flops, "forward_far",
    )
    g1_near, g1_far, edges, dh1 = call(
        functools.partial(backward1_kernel, rows), (g, gnear, gfar, hid1, g_inner, weights),
        (shape(1), shape(1), shape(4), shape(rows + 2)),
        [vmem(rows + 4), vmem(rows + 2)], 8 * row_flops, "backward1",
    )
    g1near, g1far = neighbours(g1_near, g1_far)
    g1, dh0_inner, *grads = call(
        functools.partial(middle_kernel, rows), (g, edges, hid1, dh1, x1, hid0, x, weights),
        (shape(rows), shape(rows - 4)) + (grad,) * 4,
        [vmem(rows), vmem(rows + 2), vmem(rows), vmem(rows - 4)],
        36 * row_flops, "middle",
    )
    dh0, dh0_near, dh0_far, part, send = call(
        functools.partial(backward0_kernel, rows, scale),
        (g1, g1near, g1far, hid0, x, xnear, xfar, weights, *grads),
        (shape(4), shape(1), shape(1), jax.ShapeDtypeStruct(half, F32),
         jax.ShapeDtypeStruct(half, BF16)),
        [vmem(rows + 2), vmem(4), pltpu.VMEM((8 * CHAN, width), BF16),
         pltpu.VMEM((2, *half), F32)],
        8 * row_flops, "backward0",
    )

    part = part + exchange(send, 1, count).astype(F32)
    low, high = part[: CHAN // 2], part[CHAN // 2 :]
    bit = (place & 2) != 0
    send = jnp.where(bit, low, high).astype(BF16)
    part = jnp.where(bit, high, low)
    arrived = exchange(send, 2, count)
    dh0_near, dh0_far, _ = lax.optimization_barrier((dh0_near, dh0_far, send))
    dh0near, dh0far = neighbours(dh0_near, dh0_far)
    part = part + arrived.astype(F32)
    step = 4
    input_grad = None
    while step < count:
        send = part.astype(BF16)
        masks = [step, 2 * step, 3 * step] if 2 * step < count else [step]
        arrived = [exchange(send, mask, count) for mask in masks]
        if input_grad is None:
            (input_grad,) = call(
                functools.partial(input_grad_kernel, rows), (dh0_inner, dh0, dh0near, dh0far, g1, weights),
                (tile,),
                [vmem(rows + 2), wide], 8 * row_flops, "input_grad", after=(send,),
            )
            arrived, input_grad = lax.optimization_barrier((arrived, input_grad))
        own = send.astype(F32)
        arrived = [value.astype(F32) for value in arrived]
        part = own + arrived[0]
        if len(masks) == 3:
            part = part + (arrived[1] + arrived[2])
        step *= len(masks) + 1
    done = part.astype(BF16)
    bit = (place & 2) != 0
    other = exchange(done, 2, count)
    (section_output,) = call(
        functools.partial(output_kernel, rows), (hid1, x1, weights), (tile,),
        [vmem(rows + 2), wide], 8 * row_flops, "output", after=(done,),
    )
    other, section_output = lax.optimization_barrier((other, section_output))
    done = jnp.where(bit, jnp.concatenate([other, done]), jnp.concatenate([done, other]))
    (kernel_grad,) = call(
        gathered_kernel, (done, exchange(done, 1, count)),
        (jax.ShapeDtypeStruct((2, 2, CHAN, 9 * CHAN), F32),), [], 0, "gathered",
    )
    return (section_output, input_grad, kernel_grad)


def solution(mesh):
    return jax.shard_map(
        local,
        mesh=mesh,
        in_specs=(P(None, "space", "groups"), P(None, "space", "groups"), P()),
        out_specs=(
            P(None, "space", "groups"),
            P(None, "space", "groups"),
            P("groups", None, None, None),
        ),
        check_vma=False,
    )
```

```python
import functools
import math

import jax
import jax.numpy as jnp
from jax import lax
from jax.experimental import pallas as pl
from jax.experimental.pallas import tpu as pltpu
from jax.sharding import PartitionSpec as P

CHAN = 64
STACK = 3 * CHAN
F32 = jnp.float32
BF16 = jnp.bfloat16
VMEM = pl.BlockSpec(memory_space=pltpu.VMEM)
ANY = pl.BlockSpec(memory_space=pl.ANY)
HBM = pl.BlockSpec(memory_space=pltpu.HBM)
PIECES = 4


def call(body, operands, outs, scratch, flops, name, after=(), place=VMEM):
    nbytes = sum(v.size * v.dtype.itemsize for v in (*operands, *outs))
    held = sum(math.prod(v.shape) * v.dtype.itemsize for v in scratch if v.dtype in (F32, BF16))

    def kernel(*refs):
        body(*refs[len(after) :])

    return pl.pallas_call(
        kernel,
        out_shape=outs,
        in_specs=[ANY] * len(after) + [place] + [VMEM] * (len(operands) - 1),
        out_specs=[VMEM] * len(outs),
        scratch_shapes=scratch,
        compiler_params=pltpu.CompilerParams(vmem_limit_bytes=nbytes + held + (6 << 20)),
        cost_estimate=pl.CostEstimate(flops=flops, bytes_accessed=nbytes, transcendentals=0),
        name=name,
    )(*after, *operands)


def stacked(field):
    width = field.shape[1]
    lane = lax.broadcasted_iota(jnp.int32, field.shape, 1)
    zero = jnp.zeros_like(field)
    left = jnp.where(lane == 0, zero, pltpu.roll(field, 1, 1))
    right = jnp.where(lane == width - 1, zero, pltpu.roll(field, width - 1, 1))
    return jnp.concatenate([left, field, right], axis=0)


def put(ref, row, field):
    ref[row * STACK : (row + 1) * STACK, :] = stacked(field)


def middle(ref, row):
    return ref[row * STACK + CHAN : row * STACK + 2 * CHAN, :]


def one(ref, row):
    return ref[row * CHAN : (row + 1) * CHAN, :]


def stack_rows(ref, rows, target, at):
    for row in rows:
        put(target, row + at, one(ref, row))


def g_entry_kernel(
    edge, tile_ref, w_ref, rows_ref, near_ref, far_ref, inner_ref, held, g3, arrived
):
    entry_kernel(edge, tile_ref, rows_ref, near_ref, far_ref, held, arrived)
    rows = tile_ref.shape[1]
    stack_rows(rows_ref, range(rows), g3, 0)

    def keep(row, total):
        inner_ref[row * CHAN : (row + 1) * CHAN, :] = total

    conv_rows(w_ref[7], g3, 0, rows - 2, keep)


def copy_rows(ref, count, target, at):
    target[at * CHAN : (at + count) * CHAN, :] = ref[: count * CHAN, :]


def two_rows(target, index, column, value):
    width = value.shape[1]
    target[index, :CHAN, column : column + width] = value
    target[index, CHAN:, STACK + column : STACK + column + width] = value


def weights_kernel(kernels_ref, target):
    target[...] = jnp.zeros_like(target)
    line = lax.broadcasted_iota(jnp.int32, (CHAN, CHAN), 0)
    same = line == lax.broadcasted_iota(jnp.int32, (CHAN, CHAN), 1)
    unit = jnp.where(same, 1.0, 0.0).astype(BF16)
    for section in range(2):
        for which in range(2):
            index = 2 * (2 * section + which)
            two_rows(target, index, 0, kernels_ref[section, which])
            for tap in range(9):
                at = (8 - tap) * CHAN
                block = kernels_ref[section, which, :, at : at + CHAN]
                turned = lax.dot_general(
                    unit, block, (((1,), (1,)), ((), ())), preferred_element_type=F32
                )
                two_rows(target, index + 1, tap * CHAN, turned.astype(BF16))


def conv_rows(weight, source, first, count, finish):
    for row in range(first, first + count, 2):
        total = jnp.dot(
            weight,
            source[row * STACK : (row + 4) * STACK, :],
            preferred_element_type=F32,
        )
        finish(row, total[:CHAN])
        finish(row + 1, total[CHAN:])


def grad_rows(upper, upper_row, lower, lower_row, count):
    total = None
    for row in range(0, count, 2):
        left = upper[(row + upper_row) * STACK : (row + upper_row + 2) * STACK, :]
        right = lower[(row + lower_row) * CHAN : (row + lower_row + 4) * CHAN, :]
        term = lax.dot_general(
            left, right, (((1,), (1,)), ((), ())), preferred_element_type=F32
        )
        total = term if total is None else total + term
    return total[:STACK, :STACK] + total[STACK:, CHAN:]


def channels_first(wide, target):
    target[...] = jnp.swapaxes(wide[...], 0, 1).astype(BF16)


def odd_place():
    return lax.rem(lax.axis_index("space"), 2) == 1


def put_at(ref, row, field):
    ref[pl.ds(pl.multiple_of(row * STACK, CHAN), STACK), :] = stacked(field)


def halo_rows(near_ref, far_ref, count, rows, target):
    odd = odd_place()
    above, below = 0, rows + count
    near_at = jnp.where(odd, above, below)
    far_at = jnp.where(odd, below, above)
    for row in range(count):
        put_at(target, near_at + row, one(near_ref, row))
        put_at(target, far_at + row, one(far_ref, row))


def send_edges(rows_ref, edge, near_ref, far_ref):
    odd = odd_place()
    last = rows_ref.shape[0] - edge * CHAN
    near_at = jnp.where(odd, 0, last)
    far_at = jnp.where(odd, last, 0)
    near_ref[...] = rows_ref[pl.ds(pl.multiple_of(near_at, CHAN), edge * CHAN), :]
    far_ref[...] = rows_ref[pl.ds(pl.multiple_of(far_at, CHAN), edge * CHAN), :]


def entry_kernel(edge, tile_ref, rows_ref, near_ref, far_ref, held, arrived):
    piece = CHAN // PIECES
    copies = [
        pltpu.make_async_copy(
            tile_ref.at[i * piece : (i + 1) * piece],
            held.at[i * piece : (i + 1) * piece],
            arrived.at[i],
        )
        for i in range(PIECES)
    ]
    for copy in copies:
        copy.start()
    for i, copy in enumerate(copies):
        copy.wait()
        part = held[i * piece : (i + 1) * piece].astype(F32)
        turned = jnp.swapaxes(part, 0, 1).astype(BF16)
        for row in range(turned.shape[0]):
            at = row * CHAN + i * piece
            rows_ref[at : at + piece, :] = turned[row]
    send_edges(rows_ref, edge, near_ref, far_ref)


def channels_first(wide, target):
    target[...] = jnp.swapaxes(wide[...], 0, 1).astype(BF16)


def inner_kernel(rows, x_ref, w_ref, hid0_ref, x1_ref, hid1_ref, x3, h3, y3):
    stack_rows(x_ref, range(rows), x3, 0)

    def hidden0(row, total):
        value = jnp.maximum(total, 0.0).astype(BF16)
        put(h3, row, value)
        hid0_ref[row * CHAN : (row + 1) * CHAN, :] = value

    conv_rows(w_ref[0], x3, 0, rows - 2, hidden0)

    def next_x(row, total):
        value = (one(x_ref, row + 2).astype(F32) + total).astype(BF16)
        put(y3, row, value)
        x1_ref[row * CHAN : (row + 1) * CHAN, :] = value

    conv_rows(w_ref[2], h3, 0, rows - 4, next_x)

    def hidden1(row, total):
        hid1_ref[row * CHAN : (row + 1) * CHAN, :] = jnp.maximum(total, 0.0).astype(BF16)

    conv_rows(w_ref[4], y3, 0, rows - 6, hidden1)


def side_rows(rows, height, top, x_ref, halo_ref, w_ref, hid0_in, x1_in, hid0, x1, hid1, x3, h3, y3):
    first = lax.axis_index("space") * rows
    own, rest = (0, 4) if top else (2, 0)

    def inside(row, value):
        if 0 <= row < rows:
            return value
        keep = jnp.logical_and(first + row >= 0, first + row < height)
        return jnp.where(keep, value, 0.0)

    for i in range(4):
        put(x3, own + i, one(halo_ref, i))
    for i in range(2):
        put(x3, rest + i, one(x_ref, (0 if top else rows - 2) + i))
        put(h3, rest + i, one(hid0_in, (0 if top else rows - 4) + i))
        put(y3, rest + i, one(x1_in, (0 if top else rows - 6) + i))

    def hidden0(row, total):
        at = (-3 if top else rows - 1) + row
        value = inside(at, jnp.maximum(total, 0.0)).astype(BF16)
        hid0[row * CHAN : (row + 1) * CHAN, :] = value
        put(h3, own + row, value)

    conv_rows(w_ref[0], x3, 0, 4, hidden0)

    def next_x(row, total):
        at = (-2 if top else rows - 2) + row
        value = middle(x3, (2 if top else 0) + row).astype(F32) + total
        value = inside(at, value).astype(BF16)
        x1[row * CHAN : (row + 1) * CHAN, :] = value
        put(y3, own + row, value)

    conv_rows(w_ref[2], h3, 0, 4, next_x)

    def hidden1(row, total):
        at = (-1 if top else rows - 3) + row
        value = inside(at, jnp.maximum(total, 0.0)).astype(BF16)
        hid1[row * CHAN : (row + 1) * CHAN, :] = value

    conv_rows(w_ref[4], y3, 0, 4, hidden1)


def near_kernel(rows, height, *refs):
    odd = odd_place()
    for top in (True, False):
        pl.when(odd == top)(functools.partial(side_rows, rows, height, top, *refs))


def far_kernel(
    rows, height, x_ref, far_ref, w_ref, hid0_in, x1_in, hid1_in, near0, near1, near2,
    hid0_ref, x1_ref, hid1_ref, far0, far1, far2, *scratch,
):
    def far_side(top):
        side_rows(
            rows, height, top, x_ref, far_ref, w_ref, hid0_in, x1_in, far0, far1, far2, *scratch
        )
        for edge, hid0, x1, hid1 in ((top, far0, far1, far2), (not top, near0, near1, near2)):
            for target, source, count in ((hid0_ref, hid0, 2), (x1_ref, x1, 3), (hid1_ref, hid1, 4)):
                to = 0 if edge else rows + 2 - count
                at = 4 - count if edge else 0
                target[to * CHAN : (to + count) * CHAN, :] = source[at * CHAN : (at + count) * CHAN, :]

    copy_rows(hid0_in, rows - 2, hid0_ref, 2)
    copy_rows(x1_in, rows - 4, x1_ref, 3)
    copy_rows(hid1_in, rows - 6, hid1_ref, 4)
    odd = odd_place()
    for top in (True, False):
        pl.when(odd != top)(functools.partial(far_side, top))


def backward_side(
    rows, top, g_ref, halo_ref, hid1_row, inner_ref, w_ref, inner_rows, keep_dh1, keep_edge, g3, d3
):
    start = 0 if top else rows - 2
    for i in range(2):
        put(g3, (0 if top else 2) + i, one(halo_ref, i))
        put(g3, (2 if top else 0) + i, one(g_ref, start + i))

    def dhidden1(row, total):
        value = jnp.where(hid1_row(row) > 0, total, 0.0).astype(BF16)
        keep_dh1(row, value)
        at = row + 1 if top else row - (rows - 3)
        if 0 <= at < 4:
            put(d3, at, value)

    for row in inner_rows:
        dhidden1(row, one(inner_ref, row - 1))
    edge = -1 if top else rows - 1
    conv_rows(w_ref[7], g3, 0, 2, lambda row, total: dhidden1(edge + row, total))

    def next_g(row, total):
        keep_edge(row, (one(g_ref, start + row).astype(F32) + total).astype(BF16))

    conv_rows(w_ref[5], d3, 0, 2, next_g)


def backward1_near_kernel(
    rows, g_ref, near_ref, hid1_near, hid1_in, inner_ref, w_ref, dh1_ref, edge_ref, g3, d3
):
    def near_side(top):
        def hid1_row(row):
            if 3 <= row < rows - 3:
                return one(hid1_in, row - 3)
            return one(hid1_near, row + 1 if top else row - (rows - 3))

        def keep_dh1(row, value):
            at = row + 1 if top else row - 3
            dh1_ref[at * CHAN : (at + 1) * CHAN, :] = value

        def keep_edge(row, value):
            edge_ref[row * CHAN : (row + 1) * CHAN, :] = value

        inner_rows = range(1, rows - 3) if top else range(3, rows - 1)
        backward_side(
            rows, top, g_ref, near_ref, hid1_row, inner_ref, w_ref, inner_rows, keep_dh1, keep_edge, g3, d3
        )

    odd = odd_place()
    for top in (True, False):
        pl.when(odd == top)(functools.partial(near_side, top))


def backward1_far_kernel(
    rows, g_ref, far_ref, hid1_ref, inner_ref, w_ref, dh1_near, edge_near,
    next_near, next_far, edges_ref, dh1_ref, g3, d3,
):
    def far_side(top):
        def keep_dh1(row, value):
            dh1_ref[(row + 1) * CHAN : (row + 2) * CHAN, :] = value

        def keep_edge(row, value):
            at = row if top else 2 + row
            edges_ref[at * CHAN : (at + 1) * CHAN, :] = value

        inner_rows = (1, 2) if top else (rows - 3, rows - 2)
        backward_side(
            rows, top, g_ref, far_ref, lambda row: one(hid1_ref, row + 1), inner_ref, w_ref, inner_rows,
            keep_dh1, keep_edge, g3, d3,
        )
        copy_rows(dh1_near, rows - 2, dh1_ref, 4 if top else 0)
        copy_rows(edge_near, 2, edges_ref, 2 if top else 0)

    odd = odd_place()
    for top in (True, False):
        pl.when(odd != top)(functools.partial(far_side, top))
    send_edges(edges_ref, 1, next_near, next_far)


def middle_kernel(
    rows, g_ref, edges_ref, hid1_ref, dh1_ref, x1_ref, hid0_ref, x_ref, w_ref,
    g1_ref, dh0_ref, grad00, grad01, grad10, grad11, s3, t3, u3, v3,
):
    stack_rows(dh1_ref, range(rows + 2), t3, 0)
    copy_rows(edges_ref, 2, g1_ref, 0)
    g1_ref[(rows - 2) * CHAN :, :] = edges_ref[2 * CHAN :, :]

    def next_g(row, total):
        value = (one(g_ref, row).astype(F32) + total).astype(BF16)
        g1_ref[row * CHAN : (row + 1) * CHAN, :] = value
        put(u3, row, value)

    conv_rows(w_ref[5], t3, 2, rows - 4, next_g)
    stack_rows(g1_ref, (0, 1, rows - 2, rows - 1), u3, 0)

    def dhidden0(row, total):
        value = jnp.where(one(hid0_ref, row + 2) > 0, total, 0.0).astype(BF16)
        dh0_ref[row * CHAN : (row + 1) * CHAN, :] = value
        put(v3, row, value)

    conv_rows(w_ref[3], u3, 0, rows - 2, dhidden0)
    stack_rows(g_ref, range(rows), s3, 0)
    grad11[...] = grad_rows(s3, 0, hid1_ref, 0, rows)
    grad10[...] = grad_rows(t3, 1, x1_ref, 0, rows)
    grad01[...] = grad_rows(u3, 0, hid0_ref, 0, rows)
    grad00[...] = grad_rows(v3, 0, x_ref, 0, rows - 2)


def output_kernel(rows, hid1_ref, x1_ref, w_ref, out_ref, k3, wide):
    stack_rows(hid1_ref, range(rows + 2), k3, 0)

    def last_x(row, total):
        wide[row] = one(x1_ref, row + 1).astype(F32) + total

    conv_rows(w_ref[6], k3, 0, rows, last_x)
    channels_first(wide, out_ref)


def backward0_kernel(
    rows, scale, g1_ref, near_ref, far_ref, hid0_ref, x_ref, xnear_ref, xfar_ref, w_ref, inner00,
    grad01, grad10, grad11, next_near, next_far, keep_ref, send_ref,
    d0, g3, d3, xs, both,
):
    odd = odd_place()
    near_at, far_at = jnp.where(odd, 0, 5), jnp.where(odd, 5, 0)
    put_at(g3, near_at, one(near_ref, 0))
    put_at(g3, far_at, one(far_ref, 0))
    stack_rows(g1_ref, (0, 1), g3, 1)
    stack_rows(g1_ref, (rows - 2, rows - 1), g3, 5 - rows)
    copy_rows(x_ref, 2, xs, 1)
    xs[3 * CHAN : 5 * CHAN, :] = x_ref[(rows - 2) * CHAN :, :]
    near_row, far_row = jnp.where(odd, 3, 0), jnp.where(odd, 0, 3)
    for ref, at, row in ((xnear_ref, near_at, near_row), (xfar_ref, far_at, far_row)):
        source = pl.ds(pl.multiple_of(row * CHAN, CHAN), CHAN)
        xs[pl.ds(pl.multiple_of(at * CHAN, CHAN), CHAN), :] = ref[source, :]
    grad00 = inner00[...]
    for end, row in ((0, 0), (1, rows - 1)):
        total = jnp.dot(
            w_ref[3, :CHAN, : 3 * STACK],
            g3[3 * end * STACK : 3 * (end + 1) * STACK, :],
            preferred_element_type=F32,
        )
        value = jnp.where(one(hid0_ref, row + 1) > 0, total, 0.0).astype(BF16)
        d0[end * CHAN : (end + 1) * CHAN, :] = value
        put(d3, end, value)
    for end in range(2):
        grad00 = grad00 + lax.dot_general(
            d3[end * STACK : (end + 1) * STACK, :],
            xs[end * STACK : (end + 1) * STACK, :],
            (((1,), (1,)), ((), ())),
            preferred_element_type=F32,
        )
    send_edges(d0, 1, next_near, next_far)
    pairs = ((grad00, grad01[...]), (grad10[...], grad11[...]))
    for section, pair in enumerate(pairs):
        for which, value in enumerate(pair):
            for a in range(3):
                for b in range(3):
                    block = value[(2 - b) * CHAN : (3 - b) * CHAN, a * CHAN : (a + 1) * CHAN]
                    at = which * 9 * CHAN + (3 * a + b) * CHAN
                    both[section, :, at : at + CHAN] = block * scale
    mine = lax.rem(lax.axis_index("space"), 2)
    keep_ref[...] = both[mine]
    send_ref[...] = both[1 - mine].astype(BF16)


def input_grad_kernel(rows, dh0_in, own_near, own_far, near_ref, far_ref, g1_ref, w_ref, out_ref, d3, wide):
    halo_rows(near_ref, far_ref, 1, rows, d3)
    stack_rows(dh0_in, range(rows - 2), d3, 2)
    odd = odd_place()
    put_at(d3, jnp.where(odd, 1, rows), one(own_near, 0))
    put_at(d3, jnp.where(odd, rows, 1), one(own_far, 0))

    def last_g(row, total):
        wide[row] = one(g1_ref, row).astype(F32) + total

    conv_rows(w_ref[1], d3, 0, rows, last_g)
    channels_first(wide, out_ref)


def gathered_kernel(own_ref, other_ref, out_ref):
    mine = lax.rem(lax.axis_index("space"), 2)
    for section, ref in ((mine, own_ref), (1 - mine, other_ref)):
        for which in range(2):
            piece = ref[:, which * 9 * CHAN : (which + 1) * 9 * CHAN]
            out_ref[section, which] = piece.astype(F32)


def exchange(value, mask, count):
    return lax.ppermute(value, "space", [(d, d ^ mask) for d in range(count)])


def local(features, cotangent, kernels):
    rows, width = features.shape[1], features.shape[2]
    count = lax.axis_size("space")
    height = rows * count
    scale = 1.0 / math.sqrt(height * width)
    place = lax.axis_index("space")
    beyond = [(i, i + 1) for i in range(1, count - 1, 2)]
    beyond += [(target, source) for source, target in beyond]

    def shape(n, dtype=BF16):
        return jax.ShapeDtypeStruct((n * CHAN, width), dtype)

    def vmem(n):
        return pltpu.VMEM((n * STACK, width), BF16)

    def plain(n):
        return pltpu.VMEM((n * CHAN, width), BF16)

    def neighbours(near, far):
        from_far = lax.ppermute(far, "space", beyond)
        return exchange(near, 1, count), from_far

    row_flops = 2 * CHAN * 9 * CHAN * width * 4
    grad = jax.ShapeDtypeStruct((STACK, STACK), F32)
    tile = jax.ShapeDtypeStruct((CHAN, rows, width), BF16)
    wide = pltpu.VMEM((rows, CHAN, width), F32)
    half = (CHAN, 18 * CHAN)
    entry = [pltpu.VMEM((CHAN, rows, width), BF16), pltpu.SemaphoreType.DMA((PIECES,))]

    x, x_near, x_far = call(
        functools.partial(entry_kernel, 4), (features,), (shape(rows), shape(4), shape(4)),
        entry, 0, "x_rows", place=HBM,
    )
    xnear, xfar = neighbours(x_near, x_far)
    (weights,) = call(
        weights_kernel, (kernels,), (jax.ShapeDtypeStruct((8, 2 * CHAN, 4 * STACK), BF16),), [],
        row_flops, "weights", after=(x_far,),
    )
    inner = call(
        functools.partial(inner_kernel, rows), (x, weights),
        (shape(rows - 2), shape(rows - 4), shape(rows - 6)),
        [vmem(rows), vmem(rows - 2), vmem(rows - 4)], 12 * row_flops, "inner",
    )
    g, g_near, g_far, g_inner = call(
        functools.partial(g_entry_kernel, 2), (cotangent, weights),
        (shape(rows), shape(2), shape(2), shape(rows - 2, F32)),
        [entry[0], vmem(rows), entry[1]], 6 * row_flops, "g_rows", after=(inner[2],), place=HBM,
    )
    gnear, gfar = neighbours(g_near, g_far)
    near = call(
        functools.partial(near_kernel, rows, height), (x, xnear, weights, inner[0], inner[1]),
        (shape(4),) * 3, [vmem(6)] * 3, 12 * row_flops, "forward_near", after=(g_near,),
    )
    dh1_near, edge_near = call(
        functools.partial(backward1_near_kernel, rows),
        (g, gnear, near[2], inner[2], g_inner, weights), (shape(rows - 2), shape(2)),
        [vmem(4)] * 2, 4 * row_flops, "backward1_near",
    )
    hid0, x1, hid1 = call(
        functools.partial(far_kernel, rows, height), (x, xfar, weights, *inner, *near),
        (shape(rows + 2),) * 3, [plain(4)] * 3 + [vmem(6)] * 3, 12 * row_flops, "forward_far",
    )
    g1_near, g1_far, edges, dh1 = call(
        functools.partial(backward1_far_kernel, rows),
        (g, gfar, hid1, g_inner, weights, dh1_near, edge_near),
        (shape(1), shape(1), shape(4), shape(rows + 2)), [vmem(4)] * 2, 4 * row_flops, "backward1_far",
    )
    g1near, g1far = neighbours(g1_near, g1_far)
    g1, dh0_inner, *grads = call(
        functools.partial(middle_kernel, rows), (g, edges, hid1, dh1, x1, hid0, x, weights),
        (shape(rows), shape(rows - 2)) + (grad,) * 4,
        [vmem(rows), vmem(rows + 2), vmem(rows), vmem(rows - 2)],
        36 * row_flops, "middle",
    )
    dh0_near, dh0_far, part, send = call(
        functools.partial(backward0_kernel, rows, scale),
        (g1, g1near, g1far, hid0, x, xnear, xfar, weights, *grads),
        (shape(1), shape(1), jax.ShapeDtypeStruct(half, F32),
         jax.ShapeDtypeStruct(half, BF16)),
        [plain(2), vmem(6), vmem(2), plain(6),
         pltpu.VMEM((2, *half), F32)],
        8 * row_flops, "backward0",
    )

    part = part + exchange(send, 1, count).astype(F32)
    low, high = part[: CHAN // 2], part[CHAN // 2 :]
    bit = (place & 2) != 0
    send = jnp.where(bit, low, high).astype(BF16)
    part = jnp.where(bit, high, low)
    arrived = exchange(send, 2, count)
    dh0_near, dh0_far, _ = lax.optimization_barrier((dh0_near, dh0_far, send))
    dh0near, dh0far = neighbours(dh0_near, dh0_far)
    part = part + arrived.astype(F32)
    step = 4
    input_grad = None
    while step < count:
        send = part.astype(BF16)
        masks = [step, 2 * step, 3 * step] if 2 * step < count else [step]
        arrived = [exchange(send, mask, count) for mask in masks]
        if input_grad is None:
            (input_grad,) = call(
                functools.partial(input_grad_kernel, rows), (dh0_inner, dh0_near, dh0_far, dh0near, dh0far, g1, weights),
                (tile,),
                [vmem(rows + 2), wide], 8 * row_flops, "input_grad", after=(send,),
            )
            arrived, input_grad = lax.optimization_barrier((arrived, input_grad))
        own = send.astype(F32)
        arrived = [value.astype(F32) for value in arrived]
        part = own + arrived[0]
        if len(masks) == 3:
            part = part + (arrived[1] + arrived[2])
        step *= len(masks) + 1
    done = part.astype(BF16)
    bit = (place & 2) != 0
    other = exchange(done, 2, count)
    (section_output,) = call(
        functools.partial(output_kernel, rows), (hid1, x1, weights), (tile,),
        [vmem(rows + 2), wide], 8 * row_flops, "output", after=(done,),
    )
    other, section_output = lax.optimization_barrier((other, section_output))
    done = jnp.where(bit, jnp.concatenate([other, done]), jnp.concatenate([done, other]))
    (kernel_grad,) = call(
        gathered_kernel, (done, exchange(done, 1, count)),
        (jax.ShapeDtypeStruct((2, 2, CHAN, 9 * CHAN), F32),), [], 0, "gathered",
    )
    return (section_output, input_grad, kernel_grad)


def solution(mesh):
    return jax.shard_map(
        local,
        mesh=mesh,
        in_specs=(P(None, "space", "groups"), P(None, "space", "groups"), P()),
        out_specs=(
            P(None, "space", "groups"),
            P(None, "space", "groups"),
            P("groups", None, None, None),
        ),
        check_vma=False,
    )
```

```python
import functools
import math

import jax
import jax.numpy as jnp
from jax import lax
from jax.experimental import pallas as pl
from jax.experimental.pallas import tpu as pltpu
from jax.sharding import PartitionSpec as P

CHAN = 64
STACK = 3 * CHAN
F32 = jnp.float32
BF16 = jnp.bfloat16
VMEM = pl.BlockSpec(memory_space=pltpu.VMEM)
ANY = pl.BlockSpec(memory_space=pl.ANY)
HBM = pl.BlockSpec(memory_space=pltpu.HBM)
PIECES = 4


def call(body, operands, outs, scratch, flops, name, after=(), place=VMEM):
    nbytes = sum(v.size * v.dtype.itemsize for v in (*operands, *outs))
    held = sum(math.prod(v.shape) * v.dtype.itemsize for v in scratch if v.dtype in (F32, BF16))

    def kernel(*refs):
        body(*refs[len(after) :])

    return pl.pallas_call(
        kernel,
        out_shape=outs,
        in_specs=[ANY] * len(after) + [place] + [VMEM] * (len(operands) - 1),
        out_specs=[VMEM] * len(outs),
        scratch_shapes=scratch,
        compiler_params=pltpu.CompilerParams(vmem_limit_bytes=nbytes + held + (6 << 20)),
        cost_estimate=pl.CostEstimate(flops=flops, bytes_accessed=nbytes, transcendentals=0),
        name=name,
    )(*after, *operands)


def stacked(field):
    width = field.shape[1]
    lane = lax.broadcasted_iota(jnp.int32, field.shape, 1)
    zero = jnp.zeros_like(field)
    left = jnp.where(lane == 0, zero, pltpu.roll(field, 1, 1))
    right = jnp.where(lane == width - 1, zero, pltpu.roll(field, width - 1, 1))
    return jnp.concatenate([left, field, right], axis=0)


def put(ref, row, field):
    ref[row * STACK : (row + 1) * STACK, :] = stacked(field)


def middle(ref, row):
    return ref[row * STACK + CHAN : row * STACK + 2 * CHAN, :]


def one(ref, row):
    return ref[row * CHAN : (row + 1) * CHAN, :]


def stack_rows(ref, rows, target, at):
    for row in rows:
        put(target, row + at, one(ref, row))


def g_entry_kernel(
    edge, tile_ref, w_ref, rows_ref, near_ref, far_ref, inner_ref, held, g3, arrived
):
    entry_kernel(edge, tile_ref, rows_ref, near_ref, far_ref, held, arrived)
    rows = tile_ref.shape[1]
    stack_rows(rows_ref, range(rows), g3, 0)

    def keep(row, total):
        inner_ref[row * CHAN : (row + 1) * CHAN, :] = total

    conv_rows(w_ref[7], g3, 0, rows - 2, keep)


def copy_rows(ref, count, target, at):
    target[at * CHAN : (at + count) * CHAN, :] = ref[: count * CHAN, :]


def two_rows(target, index, column, value):
    width = value.shape[1]
    target[index, :CHAN, column : column + width] = value
    target[index, CHAN:, STACK + column : STACK + column + width] = value


def weights_kernel(kernels_ref, target):
    target[...] = jnp.zeros_like(target)
    line = lax.broadcasted_iota(jnp.int32, (CHAN, CHAN), 0)
    same = line == lax.broadcasted_iota(jnp.int32, (CHAN, CHAN), 1)
    unit = jnp.where(same, 1.0, 0.0).astype(BF16)
    for section in range(2):
        for which in range(2):
            index = 2 * (2 * section + which)
            two_rows(target, index, 0, kernels_ref[section, which])
            for tap in range(9):
                at = (8 - tap) * CHAN
                block = kernels_ref[section, which, :, at : at + CHAN]
                turned = lax.dot_general(
                    unit, block, (((1,), (1,)), ((), ())), preferred_element_type=F32
                )
                two_rows(target, index + 1, tap * CHAN, turned.astype(BF16))


def conv_rows(weight, source, first, count, finish):
    for row in range(first, first + count, 2):
        total = jnp.dot(
            weight,
            source[row * STACK : (row + 4) * STACK, :],
            preferred_element_type=F32,
        )
        finish(row, total[:CHAN])
        finish(row + 1, total[CHAN:])


def grad_rows(upper, upper_row, lower, lower_row, count):
    total = None
    for row in range(0, count, 2):
        left = upper[(row + upper_row) * STACK : (row + upper_row + 2) * STACK, :]
        right = lower[(row + lower_row) * CHAN : (row + lower_row + 4) * CHAN, :]
        term = lax.dot_general(
            left, right, (((1,), (1,)), ((), ())), preferred_element_type=F32
        )
        total = term if total is None else total + term
    return total[:STACK, :STACK] + total[STACK:, CHAN:]


def channels_first(wide, target):
    target[...] = jnp.swapaxes(wide[...], 0, 1).astype(BF16)


def odd_place():
    return lax.rem(lax.axis_index("space"), 2) == 1


def put_at(ref, row, field):
    ref[pl.ds(pl.multiple_of(row * STACK, CHAN), STACK), :] = stacked(field)


def halo_rows(near_ref, far_ref, count, rows, target):
    odd = odd_place()
    above, below = 0, rows + count
    near_at = jnp.where(odd, above, below)
    far_at = jnp.where(odd, below, above)
    for row in range(count):
        put_at(target, near_at + row, one(near_ref, row))
        put_at(target, far_at + row, one(far_ref, row))


def send_edges(rows_ref, edge, near_ref, far_ref):
    odd = odd_place()
    last = rows_ref.shape[0] - edge * CHAN
    near_at = jnp.where(odd, 0, last)
    far_at = jnp.where(odd, last, 0)
    near_ref[...] = rows_ref[pl.ds(pl.multiple_of(near_at, CHAN), edge * CHAN), :]
    far_ref[...] = rows_ref[pl.ds(pl.multiple_of(far_at, CHAN), edge * CHAN), :]


def entry_kernel(edge, tile_ref, rows_ref, near_ref, far_ref, held, arrived):
    piece = CHAN // PIECES
    copies = [
        pltpu.make_async_copy(
            tile_ref.at[i * piece : (i + 1) * piece],
            held.at[i * piece : (i + 1) * piece],
            arrived.at[i],
        )
        for i in range(PIECES)
    ]
    for copy in copies:
        copy.start()
    for i, copy in enumerate(copies):
        copy.wait()
        part = held[i * piece : (i + 1) * piece].astype(F32)
        turned = jnp.swapaxes(part, 0, 1).astype(BF16)
        for row in range(turned.shape[0]):
            at = row * CHAN + i * piece
            rows_ref[at : at + piece, :] = turned[row]
    send_edges(rows_ref, edge, near_ref, far_ref)


def channels_first(wide, target):
    target[...] = jnp.swapaxes(wide[...], 0, 1).astype(BF16)


def inner_kernel(rows, x_ref, w_ref, hid0_ref, x1_ref, hid1_ref, x3, h3, y3):
    stack_rows(x_ref, range(rows), x3, 0)

    def hidden0(row, total):
        value = jnp.maximum(total, 0.0).astype(BF16)
        put(h3, row, value)
        hid0_ref[row * CHAN : (row + 1) * CHAN, :] = value

    conv_rows(w_ref[0], x3, 0, rows - 2, hidden0)

    def next_x(row, total):
        value = (one(x_ref, row + 2).astype(F32) + total).astype(BF16)
        put(y3, row, value)
        x1_ref[row * CHAN : (row + 1) * CHAN, :] = value

    conv_rows(w_ref[2], h3, 0, rows - 4, next_x)

    def hidden1(row, total):
        hid1_ref[row * CHAN : (row + 1) * CHAN, :] = jnp.maximum(total, 0.0).astype(BF16)

    conv_rows(w_ref[4], y3, 0, rows - 6, hidden1)


def side_rows(rows, height, top, x_ref, halo_ref, w_ref, hid0_in, x1_in, hid0, x1, hid1, x3, h3, y3):
    first = lax.axis_index("space") * rows
    own, rest = (0, 4) if top else (2, 0)

    def inside(row, value):
        if 0 <= row < rows:
            return value
        keep = jnp.logical_and(first + row >= 0, first + row < height)
        return jnp.where(keep, value, 0.0)

    for i in range(4):
        put(x3, own + i, one(halo_ref, i))
    for i in range(2):
        put(x3, rest + i, one(x_ref, (0 if top else rows - 2) + i))
        put(h3, rest + i, one(hid0_in, (0 if top else rows - 4) + i))
        put(y3, rest + i, one(x1_in, (0 if top else rows - 6) + i))

    def hidden0(row, total):
        at = (-3 if top else rows - 1) + row
        value = inside(at, jnp.maximum(total, 0.0)).astype(BF16)
        hid0[row * CHAN : (row + 1) * CHAN, :] = value
        put(h3, own + row, value)

    conv_rows(w_ref[0], x3, 0, 4, hidden0)

    def next_x(row, total):
        at = (-2 if top else rows - 2) + row
        value = middle(x3, (2 if top else 0) + row).astype(F32) + total
        value = inside(at, value).astype(BF16)
        x1[row * CHAN : (row + 1) * CHAN, :] = value
        put(y3, own + row, value)

    conv_rows(w_ref[2], h3, 0, 4, next_x)

    def hidden1(row, total):
        at = (-1 if top else rows - 3) + row
        value = inside(at, jnp.maximum(total, 0.0)).astype(BF16)
        hid1[row * CHAN : (row + 1) * CHAN, :] = value

    conv_rows(w_ref[4], y3, 0, 4, hidden1)


def near_kernel(rows, height, *refs):
    odd = odd_place()
    for top in (True, False):
        pl.when(odd == top)(functools.partial(side_rows, rows, height, top, *refs))


def far_kernel(
    rows, height, x_ref, far_ref, w_ref, hid0_in, x1_in, hid1_in, near0, near1, near2,
    hid0_ref, x1_ref, hid1_ref, far0, far1, far2, *scratch,
):
    def far_side(top):
        side_rows(
            rows, height, top, x_ref, far_ref, w_ref, hid0_in, x1_in, far0, far1, far2, *scratch
        )
        for edge, hid0, x1, hid1 in ((top, far0, far1, far2), (not top, near0, near1, near2)):
            for target, source, count in ((hid0_ref, hid0, 2), (x1_ref, x1, 3), (hid1_ref, hid1, 4)):
                to = 0 if edge else rows + 2 - count
                at = 4 - count if edge else 0
                target[to * CHAN : (to + count) * CHAN, :] = source[at * CHAN : (at + count) * CHAN, :]

    copy_rows(hid0_in, rows - 2, hid0_ref, 2)
    copy_rows(x1_in, rows - 4, x1_ref, 3)
    copy_rows(hid1_in, rows - 6, hid1_ref, 4)
    odd = odd_place()
    for top in (True, False):
        pl.when(odd != top)(functools.partial(far_side, top))


def backward_side(
    rows, top, g_ref, halo_ref, hid1_row, inner_ref, w_ref, inner_rows, keep_dh1, keep_edge, g3, d3
):
    start = 0 if top else rows - 2
    for i in range(2):
        put(g3, (0 if top else 2) + i, one(halo_ref, i))
        put(g3, (2 if top else 0) + i, one(g_ref, start + i))

    def dhidden1(row, total):
        value = jnp.where(hid1_row(row) > 0, total, 0.0).astype(BF16)
        keep_dh1(row, value)
        at = row + 1 if top else row - (rows - 3)
        if 0 <= at < 4:
            put(d3, at, value)

    for row in inner_rows:
        dhidden1(row, one(inner_ref, row - 1))
    edge = -1 if top else rows - 1
    conv_rows(w_ref[7], g3, 0, 2, lambda row, total: dhidden1(edge + row, total))

    def next_g(row, total):
        keep_edge(row, (one(g_ref, start + row).astype(F32) + total).astype(BF16))

    conv_rows(w_ref[5], d3, 0, 2, next_g)


def backward1_near_kernel(
    rows, g_ref, near_ref, hid1_near, hid1_in, inner_ref, w_ref, dh1_ref, edge_ref, g3, d3
):
    def near_side(top):
        def hid1_row(row):
            if 3 <= row < rows - 3:
                return one(hid1_in, row - 3)
            return one(hid1_near, row + 1 if top else row - (rows - 3))

        def keep_dh1(row, value):
            at = row + 1 if top else row - 3
            dh1_ref[at * CHAN : (at + 1) * CHAN, :] = value

        def keep_edge(row, value):
            edge_ref[row * CHAN : (row + 1) * CHAN, :] = value

        inner_rows = range(1, rows - 3) if top else range(3, rows - 1)
        backward_side(
            rows, top, g_ref, near_ref, hid1_row, inner_ref, w_ref, inner_rows, keep_dh1, keep_edge, g3, d3
        )

    odd = odd_place()
    for top in (True, False):
        pl.when(odd == top)(functools.partial(near_side, top))


def backward1_far_kernel(
    rows, g_ref, far_ref, hid1_ref, inner_ref, w_ref, dh1_near, edge_near,
    next_near, next_far, edges_ref, dh1_ref, g3, d3,
):
    def far_side(top):
        def keep_dh1(row, value):
            dh1_ref[(row + 1) * CHAN : (row + 2) * CHAN, :] = value

        def keep_edge(row, value):
            at = row if top else 2 + row
            edges_ref[at * CHAN : (at + 1) * CHAN, :] = value

        inner_rows = (1, 2) if top else (rows - 3, rows - 2)
        backward_side(
            rows, top, g_ref, far_ref, lambda row: one(hid1_ref, row + 1), inner_ref, w_ref, inner_rows,
            keep_dh1, keep_edge, g3, d3,
        )
        copy_rows(dh1_near, rows - 2, dh1_ref, 4 if top else 0)
        copy_rows(edge_near, 2, edges_ref, 2 if top else 0)

    odd = odd_place()
    for top in (True, False):
        pl.when(odd != top)(functools.partial(far_side, top))
    send_edges(edges_ref, 1, next_near, next_far)


def middle_kernel(
    rows, g_ref, edges_ref, hid1_ref, dh1_ref, x1_ref, hid0_ref, x_ref, w_ref,
    g1_ref, dh0_ref, grad00, grad01, grad10, grad11, s3, t3, u3, v3,
):
    stack_rows(dh1_ref, range(rows + 2), t3, 0)
    copy_rows(edges_ref, 2, g1_ref, 0)
    g1_ref[(rows - 2) * CHAN :, :] = edges_ref[2 * CHAN :, :]

    def next_g(row, total):
        value = (one(g_ref, row).astype(F32) + total).astype(BF16)
        g1_ref[row * CHAN : (row + 1) * CHAN, :] = value
        put(u3, row, value)

    conv_rows(w_ref[5], t3, 2, rows - 4, next_g)
    stack_rows(g1_ref, (0, 1, rows - 2, rows - 1), u3, 0)

    def dhidden0(row, total):
        value = jnp.where(one(hid0_ref, row + 2) > 0, total, 0.0).astype(BF16)
        dh0_ref[row * CHAN : (row + 1) * CHAN, :] = value
        put(v3, row, value)

    conv_rows(w_ref[3], u3, 0, rows - 2, dhidden0)
    stack_rows(g_ref, range(rows), s3, 0)
    grad11[...] = grad_rows(s3, 0, hid1_ref, 0, rows)
    grad10[...] = grad_rows(t3, 1, x1_ref, 0, rows)
    grad01[...] = grad_rows(u3, 0, hid0_ref, 0, rows)
    grad00[...] = grad_rows(v3, 0, x_ref, 0, rows - 2)


def output_kernel(rows, hid1_ref, x1_ref, w_ref, out_ref, k3, wide):
    stack_rows(hid1_ref, range(rows + 2), k3, 0)

    def last_x(row, total):
        wide[row] = one(x1_ref, row + 1).astype(F32) + total

    conv_rows(w_ref[6], k3, 0, rows, last_x)
    channels_first(wide, out_ref)


def backward0_kernel(
    rows, scale, g1_ref, near_ref, far_ref, hid0_ref, x_ref, xnear_ref, xfar_ref, w_ref, inner00,
    grad01, grad10, grad11, next_near, next_far, keep_ref, send_ref,
    d0, g3, d3, xs, both,
):
    odd = odd_place()
    near_at, far_at = jnp.where(odd, 0, 5), jnp.where(odd, 5, 0)
    put_at(g3, near_at, one(near_ref, 0))
    put_at(g3, far_at, one(far_ref, 0))
    stack_rows(g1_ref, (0, 1), g3, 1)
    stack_rows(g1_ref, (rows - 2, rows - 1), g3, 5 - rows)
    copy_rows(x_ref, 2, xs, 1)
    xs[3 * CHAN : 5 * CHAN, :] = x_ref[(rows - 2) * CHAN :, :]
    near_row, far_row = jnp.where(odd, 3, 0), jnp.where(odd, 0, 3)
    for ref, at, row in ((xnear_ref, near_at, near_row), (xfar_ref, far_at, far_row)):
        source = pl.ds(pl.multiple_of(row * CHAN, CHAN), CHAN)
        xs[pl.ds(pl.multiple_of(at * CHAN, CHAN), CHAN), :] = ref[source, :]
    grad00 = inner00[...]
    for end, row in ((0, 0), (1, rows - 1)):
        total = jnp.dot(
            w_ref[3, :CHAN, : 3 * STACK],
            g3[3 * end * STACK : 3 * (end + 1) * STACK, :],
            preferred_element_type=F32,
        )
        value = jnp.where(one(hid0_ref, row + 1) > 0, total, 0.0).astype(BF16)
        d0[end * CHAN : (end + 1) * CHAN, :] = value
        put(d3, end, value)
    for end in range(2):
        grad00 = grad00 + lax.dot_general(
            d3[end * STACK : (end + 1) * STACK, :],
            xs[end * STACK : (end + 1) * STACK, :],
            (((1,), (1,)), ((), ())),
            preferred_element_type=F32,
        )
    send_edges(d0, 1, next_near, next_far)
    pairs = ((grad00, grad01[...]), (grad10[...], grad11[...]))
    for section, pair in enumerate(pairs):
        for which, value in enumerate(pair):
            for a in range(3):
                for b in range(3):
                    block = value[(2 - b) * CHAN : (3 - b) * CHAN, a * CHAN : (a + 1) * CHAN]
                    at = which * 9 * CHAN + (3 * a + b) * CHAN
                    both[section, :, at : at + CHAN] = block * scale
    mine = lax.rem(lax.axis_index("space"), 2)
    keep_ref[...] = both[mine]
    send_ref[...] = both[1 - mine].astype(BF16)


def input_grad_kernel(rows, dh0_in, own_near, own_far, near_ref, far_ref, g1_ref, w_ref, out_ref, d3, wide):
    halo_rows(near_ref, far_ref, 1, rows, d3)
    stack_rows(dh0_in, range(rows - 2), d3, 2)
    odd = odd_place()
    put_at(d3, jnp.where(odd, 1, rows), one(own_near, 0))
    put_at(d3, jnp.where(odd, rows, 1), one(own_far, 0))

    def last_g(row, total):
        wide[row] = one(g1_ref, row).astype(F32) + total

    conv_rows(w_ref[1], d3, 0, rows, last_g)
    channels_first(wide, out_ref)


def halved_kernel(part_ref, other_ref, keep_ref, send_ref):
    low, high = (
        part_ref[at : at + CHAN // 2, :] + other_ref[at : at + CHAN // 2, :].astype(F32)
        for at in (0, CHAN // 2)
    )
    bit = lax.rem(lax.axis_index("space"), 4) >= 2
    keep_ref[...] = jnp.where(bit, high, low)
    send_ref[...] = jnp.where(bit, low, high).astype(BF16)


def gathered_kernel(own_ref, other_ref, out_ref):
    mine = lax.rem(lax.axis_index("space"), 2)
    for section, ref in ((mine, own_ref), (1 - mine, other_ref)):
        for which in range(2):
            piece = ref[:, which * 9 * CHAN : (which + 1) * 9 * CHAN]
            out_ref[section, which] = piece.astype(F32)

def exchange(value, mask, count):
    return lax.ppermute(value, "space", [(d, d ^ mask) for d in range(count)])


def local(features, cotangent, kernels):
    rows, width = features.shape[1], features.shape[2]
    count = lax.axis_size("space")
    height = rows * count
    scale = 1.0 / math.sqrt(height * width)
    place = lax.axis_index("space")
    beyond = [(i, i + 1) for i in range(1, count - 1, 2)]
    beyond += [(target, source) for source, target in beyond]

    def shape(n, dtype=BF16):
        return jax.ShapeDtypeStruct((n * CHAN, width), dtype)

    def vmem(n):
        return pltpu.VMEM((n * STACK, width), BF16)

    def plain(n):
        return pltpu.VMEM((n * CHAN, width), BF16)

    def neighbours(near, far):
        from_far = lax.ppermute(far, "space", beyond)
        return exchange(near, 1, count), from_far

    row_flops = 2 * CHAN * 9 * CHAN * width * 4
    grad = jax.ShapeDtypeStruct((STACK, STACK), F32)
    tile = jax.ShapeDtypeStruct((CHAN, rows, width), BF16)
    wide = pltpu.VMEM((rows, CHAN, width), F32)
    half = (CHAN, 18 * CHAN)
    entry = [pltpu.VMEM((CHAN, rows, width), BF16), pltpu.SemaphoreType.DMA((PIECES,))]

    x, x_near, x_far = call(
        functools.partial(entry_kernel, 4), (features,), (shape(rows), shape(4), shape(4)),
        entry, 0, "x_rows", place=HBM,
    )
    xnear, xfar = neighbours(x_near, x_far)
    (weights,) = call(
        weights_kernel, (kernels,), (jax.ShapeDtypeStruct((8, 2 * CHAN, 4 * STACK), BF16),), [],
        row_flops, "weights", after=(x_far,),
    )
    inner = call(
        functools.partial(inner_kernel, rows), (x, weights),
        (shape(rows - 2), shape(rows - 4), shape(rows - 6)),
        [vmem(rows), vmem(rows - 2), vmem(rows - 4)], 12 * row_flops, "inner",
    )
    g, g_near, g_far, g_inner = call(
        functools.partial(g_entry_kernel, 2), (cotangent, weights),
        (shape(rows), shape(2), shape(2), shape(rows - 2, F32)),
        [entry[0], vmem(rows), entry[1]], 6 * row_flops, "g_rows", after=(inner[2],), place=HBM,
    )
    gnear, gfar = neighbours(g_near, g_far)
    near = call(
        functools.partial(near_kernel, rows, height), (x, xnear, weights, inner[0], inner[1]),
        (shape(4),) * 3, [vmem(6)] * 3, 12 * row_flops, "forward_near", after=(g_near,),
    )
    dh1_near, edge_near = call(
        functools.partial(backward1_near_kernel, rows),
        (g, gnear, near[2], inner[2], g_inner, weights), (shape(rows - 2), shape(2)),
        [vmem(4)] * 2, 4 * row_flops, "backward1_near",
    )
    hid0, x1, hid1 = call(
        functools.partial(far_kernel, rows, height), (x, xfar, weights, *inner, *near),
        (shape(rows + 2),) * 3, [plain(4)] * 3 + [vmem(6)] * 3, 12 * row_flops, "forward_far",
    )
    g1_near, g1_far, edges, dh1 = call(
        functools.partial(backward1_far_kernel, rows),
        (g, gfar, hid1, g_inner, weights, dh1_near, edge_near),
        (shape(1), shape(1), shape(4), shape(rows + 2)), [vmem(4)] * 2, 4 * row_flops, "backward1_far",
    )
    g1near, g1far = neighbours(g1_near, g1_far)
    g1, dh0_inner, *grads = call(
        functools.partial(middle_kernel, rows), (g, edges, hid1, dh1, x1, hid0, x, weights),
        (shape(rows), shape(rows - 2)) + (grad,) * 4,
        [vmem(rows), vmem(rows + 2), vmem(rows), vmem(rows - 2)],
        36 * row_flops, "middle",
    )
    dh0_near, dh0_far, part, send = call(
        functools.partial(backward0_kernel, rows, scale),
        (g1, g1near, g1far, hid0, x, xnear, xfar, weights, *grads),
        (shape(1), shape(1), jax.ShapeDtypeStruct(half, F32),
         jax.ShapeDtypeStruct(half, BF16)),
        [plain(2), vmem(6), vmem(2), plain(6),
         pltpu.VMEM((2, *half), F32)],
        8 * row_flops, "backward0",
    )

    quarter = (CHAN // 2, 18 * CHAN)
    part, send = call(
        halved_kernel, (part, exchange(send, 1, count)),
        (jax.ShapeDtypeStruct(quarter, F32), jax.ShapeDtypeStruct(quarter, BF16)), [], 0, "halved",
    )
    arrived = exchange(send, 2, count)
    dh0_near, dh0_far, _ = lax.optimization_barrier((dh0_near, dh0_far, send))
    dh0near, dh0far = neighbours(dh0_near, dh0_far)
    part = part + arrived.astype(F32)
    step = 4
    input_grad = None
    while step < count:
        send = part.astype(BF16)
        masks = [step, 2 * step, 3 * step] if 2 * step < count else [step]
        arrived = [exchange(send, mask, count) for mask in masks]
        if input_grad is None:
            (input_grad,) = call(
                functools.partial(input_grad_kernel, rows), (dh0_inner, dh0_near, dh0_far, dh0near, dh0far, g1, weights),
                (tile,),
                [vmem(rows + 2), wide], 8 * row_flops, "input_grad", after=(send,),
            )
            arrived, input_grad = lax.optimization_barrier((arrived, input_grad))
        own = send.astype(F32)
        arrived = [value.astype(F32) for value in arrived]
        part = own + arrived[0]
        if len(masks) == 3:
            part = part + (arrived[1] + arrived[2])
        step *= len(masks) + 1
    done = part.astype(BF16)
    bit = (place & 2) != 0
    other = exchange(done, 2, count)
    (section_output,) = call(
        functools.partial(output_kernel, rows), (hid1, x1, weights), (tile,),
        [vmem(rows + 2), wide], 8 * row_flops, "output", after=(done,),
    )
    other, section_output = lax.optimization_barrier((other, section_output))
    done = jnp.where(bit, jnp.concatenate([other, done]), jnp.concatenate([done, other]))
    (kernel_grad,) = call(
        gathered_kernel, (done, exchange(done, 1, count)),
        (jax.ShapeDtypeStruct((2, 2, CHAN, 9 * CHAN), F32),), [], 0, "gathered",
    )
    return (section_output, input_grad, kernel_grad)


def solution(mesh):
    return jax.shard_map(
        local,
        mesh=mesh,
        in_specs=(P(None, "space", "groups"), P(None, "space", "groups"), P()),
        out_specs=(
            P(None, "space", "groups"),
            P(None, "space", "groups"),
            P("groups", None, None, None),
        ),
        check_vma=False,
    )
```

```python
import functools
import math

import jax
import jax.numpy as jnp
from jax import lax
from jax.experimental import pallas as pl
from jax.experimental.pallas import tpu as pltpu
from jax.sharding import PartitionSpec as P

CHAN = 64
STACK = 3 * CHAN
F32 = jnp.float32
BF16 = jnp.bfloat16
VMEM = pl.BlockSpec(memory_space=pltpu.VMEM)
ANY = pl.BlockSpec(memory_space=pl.ANY)
HBM = pl.BlockSpec(memory_space=pltpu.HBM)
PIECES = 4


def call(body, operands, outs, scratch, flops, name, after=(), place=VMEM):
    nbytes = sum(v.size * v.dtype.itemsize for v in (*operands, *outs))
    held = sum(math.prod(v.shape) * v.dtype.itemsize for v in scratch if v.dtype in (F32, BF16))

    def kernel(*refs):
        body(*refs[len(after) :])

    return pl.pallas_call(
        kernel,
        out_shape=outs,
        in_specs=[ANY] * len(after) + [place] + [VMEM] * (len(operands) - 1),
        out_specs=[VMEM] * len(outs),
        scratch_shapes=scratch,
        compiler_params=pltpu.CompilerParams(vmem_limit_bytes=nbytes + held + (6 << 20)),
        cost_estimate=pl.CostEstimate(flops=flops, bytes_accessed=nbytes, transcendentals=0),
        name=name,
    )(*after, *operands)


def stacked(field):
    width = field.shape[1]
    lane = lax.broadcasted_iota(jnp.int32, field.shape, 1)
    zero = jnp.zeros_like(field)
    left = jnp.where(lane == 0, zero, pltpu.roll(field, 1, 1))
    right = jnp.where(lane == width - 1, zero, pltpu.roll(field, width - 1, 1))
    return jnp.concatenate([left, field, right], axis=0)


def put(ref, row, field):
    ref[row * STACK : (row + 1) * STACK, :] = stacked(field)


def middle(ref, row):
    return ref[row * STACK + CHAN : row * STACK + 2 * CHAN, :]


def one(ref, row):
    return ref[row * CHAN : (row + 1) * CHAN, :]


def stack_rows(ref, rows, target, at):
    for row in rows:
        put(target, row + at, one(ref, row))


def g_entry_kernel(
    edge, tile_ref, w_ref, rows_ref, near_ref, far_ref, inner_ref, held, g3, arrived
):
    entry_kernel(edge, tile_ref, rows_ref, near_ref, far_ref, held, arrived)
    rows = tile_ref.shape[1]
    stack_rows(rows_ref, range(rows), g3, 0)

    def keep(row, total):
        inner_ref[row * CHAN : (row + 1) * CHAN, :] = total

    conv_rows(w_ref[7], g3, 0, rows - 2, keep)


def copy_rows(ref, count, target, at):
    target[at * CHAN : (at + count) * CHAN, :] = ref[: count * CHAN, :]


def two_rows(target, index, column, value):
    width = value.shape[1]
    target[index, :CHAN, column : column + width] = value
    target[index, CHAN:, STACK + column : STACK + column + width] = value


def weights_kernel(kernels_ref, target):
    target[...] = jnp.zeros_like(target)
    line = lax.broadcasted_iota(jnp.int32, (CHAN, CHAN), 0)
    same = line == lax.broadcasted_iota(jnp.int32, (CHAN, CHAN), 1)
    unit = jnp.where(same, 1.0, 0.0).astype(BF16)
    for section in range(2):
        for which in range(2):
            index = 2 * (2 * section + which)
            two_rows(target, index, 0, kernels_ref[section, which])
            for tap in range(9):
                at = (8 - tap) * CHAN
                block = kernels_ref[section, which, :, at : at + CHAN]
                turned = lax.dot_general(
                    unit, block, (((1,), (1,)), ((), ())), preferred_element_type=F32
                )
                two_rows(target, index + 1, tap * CHAN, turned.astype(BF16))


def conv_rows(weight, source, first, count, finish):
    for row in range(first, first + count, 2):
        total = jnp.dot(
            weight,
            source[row * STACK : (row + 4) * STACK, :],
            preferred_element_type=F32,
        )
        finish(row, total[:CHAN])
        finish(row + 1, total[CHAN:])


def grad_rows(upper, upper_row, lower, lower_row, count):
    total = None
    for row in range(0, count, 2):
        left = upper[(row + upper_row) * STACK : (row + upper_row + 2) * STACK, :]
        right = lower[(row + lower_row) * CHAN : (row + lower_row + 4) * CHAN, :]
        term = lax.dot_general(
            left, right, (((1,), (1,)), ((), ())), preferred_element_type=F32
        )
        total = term if total is None else total + term
    return total[:STACK, :STACK] + total[STACK:, CHAN:]


def channels_first(wide, target):
    target[...] = jnp.swapaxes(wide[...], 0, 1).astype(BF16)


def odd_place():
    return lax.rem(lax.axis_index("space"), 2) == 1


def put_at(ref, row, field):
    ref[pl.ds(pl.multiple_of(row * STACK, CHAN), STACK), :] = stacked(field)


def halo_rows(near_ref, far_ref, count, rows, target):
    odd = odd_place()
    above, below = 0, rows + count
    near_at = jnp.where(odd, above, below)
    far_at = jnp.where(odd, below, above)
    for row in range(count):
        put_at(target, near_at + row, one(near_ref, row))
        put_at(target, far_at + row, one(far_ref, row))


def send_edges(rows_ref, edge, near_ref, far_ref):
    odd = odd_place()
    last = rows_ref.shape[0] - edge * CHAN
    near_at = jnp.where(odd, 0, last)
    far_at = jnp.where(odd, last, 0)
    near_ref[...] = rows_ref[pl.ds(pl.multiple_of(near_at, CHAN), edge * CHAN), :]
    far_ref[...] = rows_ref[pl.ds(pl.multiple_of(far_at, CHAN), edge * CHAN), :]


def entry_kernel(edge, tile_ref, rows_ref, near_ref, far_ref, held, arrived):
    piece = CHAN // PIECES
    copies = [
        pltpu.make_async_copy(
            tile_ref.at[i * piece : (i + 1) * piece],
            held.at[i * piece : (i + 1) * piece],
            arrived.at[i],
        )
        for i in range(PIECES)
    ]
    for copy in copies:
        copy.start()
    for i, copy in enumerate(copies):
        copy.wait()
        part = held[i * piece : (i + 1) * piece].astype(F32)
        turned = jnp.swapaxes(part, 0, 1).astype(BF16)
        for row in range(turned.shape[0]):
            at = row * CHAN + i * piece
            rows_ref[at : at + piece, :] = turned[row]
    send_edges(rows_ref, edge, near_ref, far_ref)


def channels_first(wide, target):
    target[...] = jnp.swapaxes(wide[...], 0, 1).astype(BF16)


def inner_kernel(rows, x_ref, w_ref, hid0_ref, x1_ref, hid1_ref, x3, h3, y3):
    stack_rows(x_ref, range(rows), x3, 0)

    def hidden0(row, total):
        value = jnp.maximum(total, 0.0).astype(BF16)
        put(h3, row, value)
        hid0_ref[row * CHAN : (row + 1) * CHAN, :] = value

    conv_rows(w_ref[0], x3, 0, rows - 2, hidden0)

    def next_x(row, total):
        value = (one(x_ref, row + 2).astype(F32) + total).astype(BF16)
        put(y3, row, value)
        x1_ref[row * CHAN : (row + 1) * CHAN, :] = value

    conv_rows(w_ref[2], h3, 0, rows - 4, next_x)

    def hidden1(row, total):
        hid1_ref[row * CHAN : (row + 1) * CHAN, :] = jnp.maximum(total, 0.0).astype(BF16)

    conv_rows(w_ref[4], y3, 0, rows - 6, hidden1)


def side_rows(rows, height, top, x_ref, halo_ref, w_ref, hid0_in, x1_in, hid0, x1, hid1, x3, h3, y3):
    first = lax.axis_index("space") * rows
    own, rest = (0, 4) if top else (2, 0)

    def inside(row, value):
        if 0 <= row < rows:
            return value
        keep = jnp.logical_and(first + row >= 0, first + row < height)
        return jnp.where(keep, value, 0.0)

    for i in range(4):
        put(x3, own + i, one(halo_ref, i))
    for i in range(2):
        put(x3, rest + i, one(x_ref, (0 if top else rows - 2) + i))
        put(h3, rest + i, one(hid0_in, (0 if top else rows - 4) + i))
        put(y3, rest + i, one(x1_in, (0 if top else rows - 6) + i))

    def hidden0(row, total):
        at = (-3 if top else rows - 1) + row
        value = inside(at, jnp.maximum(total, 0.0)).astype(BF16)
        hid0[row * CHAN : (row + 1) * CHAN, :] = value
        put(h3, own + row, value)

    conv_rows(w_ref[0], x3, 0, 4, hidden0)

    def next_x(row, total):
        at = (-2 if top else rows - 2) + row
        value = middle(x3, (2 if top else 0) + row).astype(F32) + total
        value = inside(at, value).astype(BF16)
        x1[row * CHAN : (row + 1) * CHAN, :] = value
        put(y3, own + row, value)

    conv_rows(w_ref[2], h3, 0, 4, next_x)

    def hidden1(row, total):
        at = (-1 if top else rows - 3) + row
        value = inside(at, jnp.maximum(total, 0.0)).astype(BF16)
        hid1[row * CHAN : (row + 1) * CHAN, :] = value

    conv_rows(w_ref[4], y3, 0, 4, hidden1)


def near_kernel(rows, height, *refs):
    odd = odd_place()
    for top in (True, False):
        pl.when(odd == top)(functools.partial(side_rows, rows, height, top, *refs))


def far_kernel(
    rows, height, x_ref, far_ref, w_ref, hid0_in, x1_in, hid1_in, near0, near1, near2,
    hid0_ref, x1_ref, hid1_ref, far0, far1, far2, *scratch,
):
    def far_side(top):
        side_rows(
            rows, height, top, x_ref, far_ref, w_ref, hid0_in, x1_in, far0, far1, far2, *scratch
        )
        for edge, hid0, x1, hid1 in ((top, far0, far1, far2), (not top, near0, near1, near2)):
            for target, source, count in ((hid0_ref, hid0, 2), (x1_ref, x1, 3), (hid1_ref, hid1, 4)):
                to = 0 if edge else rows + 2 - count
                at = 4 - count if edge else 0
                target[to * CHAN : (to + count) * CHAN, :] = source[at * CHAN : (at + count) * CHAN, :]

    copy_rows(hid0_in, rows - 2, hid0_ref, 2)
    copy_rows(x1_in, rows - 4, x1_ref, 3)
    copy_rows(hid1_in, rows - 6, hid1_ref, 4)
    odd = odd_place()
    for top in (True, False):
        pl.when(odd != top)(functools.partial(far_side, top))


def backward_side(
    rows, top, g_ref, halo_ref, hid1_row, inner_ref, w_ref, inner_rows, keep_dh1, keep_edge, g3, d3
):
    start = 0 if top else rows - 2
    for i in range(2):
        put(g3, (0 if top else 2) + i, one(halo_ref, i))
        put(g3, (2 if top else 0) + i, one(g_ref, start + i))

    def dhidden1(row, total):
        value = jnp.where(hid1_row(row) > 0, total, 0.0).astype(BF16)
        keep_dh1(row, value)
        at = row + 1 if top else row - (rows - 3)
        if 0 <= at < 4:
            put(d3, at, value)

    for row in inner_rows:
        dhidden1(row, one(inner_ref, row - 1))
    edge = -1 if top else rows - 1
    conv_rows(w_ref[7], g3, 0, 2, lambda row, total: dhidden1(edge + row, total))

    def next_g(row, total):
        keep_edge(row, (one(g_ref, start + row).astype(F32) + total).astype(BF16))

    conv_rows(w_ref[5], d3, 0, 2, next_g)


def backward1_near_kernel(
    rows, g_ref, near_ref, hid1_near, hid1_in, inner_ref, w_ref, dh1_ref, edge_ref, g3, d3
):
    def near_side(top):
        def hid1_row(row):
            if 3 <= row < rows - 3:
                return one(hid1_in, row - 3)
            return one(hid1_near, row + 1 if top else row - (rows - 3))

        def keep_dh1(row, value):
            at = row + 1 if top else row - 3
            dh1_ref[at * CHAN : (at + 1) * CHAN, :] = value

        def keep_edge(row, value):
            edge_ref[row * CHAN : (row + 1) * CHAN, :] = value

        inner_rows = range(1, rows - 3) if top else range(3, rows - 1)
        backward_side(
            rows, top, g_ref, near_ref, hid1_row, inner_ref, w_ref, inner_rows, keep_dh1, keep_edge, g3, d3
        )

    odd = odd_place()
    for top in (True, False):
        pl.when(odd == top)(functools.partial(near_side, top))


def backward1_far_kernel(
    rows, g_ref, far_ref, hid1_ref, inner_ref, w_ref, dh1_near, edge_near,
    next_near, next_far, edges_ref, dh1_ref, g3, d3,
):
    def far_side(top):
        def keep_dh1(row, value):
            dh1_ref[(row + 1) * CHAN : (row + 2) * CHAN, :] = value

        def keep_edge(row, value):
            at = row if top else 2 + row
            edges_ref[at * CHAN : (at + 1) * CHAN, :] = value

        inner_rows = (1, 2) if top else (rows - 3, rows - 2)
        backward_side(
            rows, top, g_ref, far_ref, lambda row: one(hid1_ref, row + 1), inner_ref, w_ref, inner_rows,
            keep_dh1, keep_edge, g3, d3,
        )
        copy_rows(dh1_near, rows - 2, dh1_ref, 4 if top else 0)
        copy_rows(edge_near, 2, edges_ref, 2 if top else 0)

    odd = odd_place()
    for top in (True, False):
        pl.when(odd != top)(functools.partial(far_side, top))
    send_edges(edges_ref, 1, next_near, next_far)


def grads_near_kernel(
    rows, g_ref, hid1_near, hid1_in, dh1_near, x1_near, x1_in, grad11, grad10, s3, t3, hid1, x1
):
    def near_side(top):
        start = 0 if top else rows - 4
        for i in range(4):
            put(s3, i, one(g_ref, start + i))
            put(t3, i, one(dh1_near, start + i + 1 if top else start + i - 3))
        for i in range(6):
            row = start - 1 + i
            if 3 <= row < rows - 3:
                value = one(hid1_in, row - 3)
            else:
                value = one(hid1_near, row + 1 if top else row - (rows - 3))
            hid1[i * CHAN : (i + 1) * CHAN, :] = value
            if 2 <= row < rows - 2:
                value = one(x1_in, row - 2)
            else:
                value = one(x1_near, row + 2 if top else row - (rows - 2))
            x1[i * CHAN : (i + 1) * CHAN, :] = value
        grad11[...] = grad_rows(s3, 0, hid1, 0, 4)
        grad10[...] = grad_rows(t3, 0, x1, 0, 4)

    odd = odd_place()
    for top in (True, False):
        pl.when(odd == top)(functools.partial(near_side, top))


def grad_rows_from(upper, upper_row, lower, lower_row, count):
    total = None
    for row in range(0, count, 2):
        left = pl.ds(pl.multiple_of((row + upper_row) * STACK, CHAN), 2 * STACK)
        right = pl.ds(pl.multiple_of((row + lower_row) * CHAN, CHAN), 4 * CHAN)
        term = lax.dot_general(
            upper[left, :], lower[right, :], (((1,), (1,)), ((), ())), preferred_element_type=F32
        )
        total = term if total is None else total + term
    return total[:STACK, :STACK] + total[STACK:, CHAN:]


def middle_kernel(
    rows, g_ref, edges_ref, hid1_ref, dh1_ref, x1_ref, hid0_ref, x_ref, w_ref, near11, near10,
    g1_ref, dh0_ref, grad00, grad01, grad10, grad11, s3, t3, u3, v3,
):
    stack_rows(dh1_ref, range(1, rows + 1), t3, 0)
    copy_rows(edges_ref, 2, g1_ref, 0)
    g1_ref[(rows - 2) * CHAN :, :] = edges_ref[2 * CHAN :, :]

    def next_g(row, total):
        value = (one(g_ref, row).astype(F32) + total).astype(BF16)
        g1_ref[row * CHAN : (row + 1) * CHAN, :] = value
        put(u3, row, value)

    conv_rows(w_ref[5], t3, 2, rows - 4, next_g)
    stack_rows(g1_ref, (0, 1, rows - 2, rows - 1), u3, 0)

    def dhidden0(row, total):
        value = jnp.where(one(hid0_ref, row + 2) > 0, total, 0.0).astype(BF16)
        dh0_ref[row * CHAN : (row + 1) * CHAN, :] = value
        put(v3, row, value)

    conv_rows(w_ref[3], u3, 0, rows - 2, dhidden0)
    start = jnp.where(odd_place(), 4, 0)
    for row in range(rows - 4):
        source = pl.ds(pl.multiple_of((start + row) * CHAN, CHAN), CHAN)
        put(s3, row, g_ref[source, :])
    grad11[...] = near11[...] + grad_rows_from(s3, 0, hid1_ref, start, rows - 4)
    grad10[...] = near10[...] + grad_rows_from(t3, start + 1, x1_ref, start, rows - 4)
    grad01[...] = grad_rows(u3, 0, hid0_ref, 0, rows)
    grad00[...] = grad_rows(v3, 0, x_ref, 0, rows - 2)


def output_kernel(rows, hid1_ref, x1_ref, w_ref, out_ref, k3, wide):
    stack_rows(hid1_ref, range(rows + 2), k3, 0)

    def last_x(row, total):
        wide[row] = one(x1_ref, row + 1).astype(F32) + total

    conv_rows(w_ref[6], k3, 0, rows, last_x)
    channels_first(wide, out_ref)


def backward0_kernel(
    rows, scale, g1_ref, near_ref, far_ref, hid0_ref, x_ref, xnear_ref, xfar_ref, w_ref, inner00,
    grad01, grad10, grad11, next_near, next_far, keep_ref, send_ref,
    d0, g3, d3, xs, both,
):
    odd = odd_place()
    near_at, far_at = jnp.where(odd, 0, 5), jnp.where(odd, 5, 0)
    put_at(g3, near_at, one(near_ref, 0))
    put_at(g3, far_at, one(far_ref, 0))
    stack_rows(g1_ref, (0, 1), g3, 1)
    stack_rows(g1_ref, (rows - 2, rows - 1), g3, 5 - rows)
    copy_rows(x_ref, 2, xs, 1)
    xs[3 * CHAN : 5 * CHAN, :] = x_ref[(rows - 2) * CHAN :, :]
    near_row, far_row = jnp.where(odd, 3, 0), jnp.where(odd, 0, 3)
    for ref, at, row in ((xnear_ref, near_at, near_row), (xfar_ref, far_at, far_row)):
        source = pl.ds(pl.multiple_of(row * CHAN, CHAN), CHAN)
        xs[pl.ds(pl.multiple_of(at * CHAN, CHAN), CHAN), :] = ref[source, :]
    grad00 = inner00[...]
    for end, row in ((0, 0), (1, rows - 1)):
        total = jnp.dot(
            w_ref[3, :CHAN, : 3 * STACK],
            g3[3 * end * STACK : 3 * (end + 1) * STACK, :],
            preferred_element_type=F32,
        )
        value = jnp.where(one(hid0_ref, row + 1) > 0, total, 0.0).astype(BF16)
        d0[end * CHAN : (end + 1) * CHAN, :] = value
        put(d3, end, value)
    for end in range(2):
        grad00 = grad00 + lax.dot_general(
            d3[end * STACK : (end + 1) * STACK, :],
            xs[end * STACK : (end + 1) * STACK, :],
            (((1,), (1,)), ((), ())),
            preferred_element_type=F32,
        )
    send_edges(d0, 1, next_near, next_far)
    pairs = ((grad00, grad01[...]), (grad10[...], grad11[...]))
    for section, pair in enumerate(pairs):
        for which, value in enumerate(pair):
            for a in range(3):
                for b in range(3):
                    block = value[(2 - b) * CHAN : (3 - b) * CHAN, a * CHAN : (a + 1) * CHAN]
                    at = which * 9 * CHAN + (3 * a + b) * CHAN
                    both[section, :, at : at + CHAN] = block * scale
    mine = lax.rem(lax.axis_index("space"), 2)
    keep_ref[...] = both[mine]
    send_ref[...] = both[1 - mine].astype(BF16)


def input_grad_kernel(rows, dh0_in, own_near, own_far, near_ref, far_ref, g1_ref, w_ref, out_ref, d3, wide):
    halo_rows(near_ref, far_ref, 1, rows, d3)
    stack_rows(dh0_in, range(rows - 2), d3, 2)
    odd = odd_place()
    put_at(d3, jnp.where(odd, 1, rows), one(own_near, 0))
    put_at(d3, jnp.where(odd, rows, 1), one(own_far, 0))

    def last_g(row, total):
        wide[row] = one(g1_ref, row).astype(F32) + total

    conv_rows(w_ref[1], d3, 0, rows, last_g)
    channels_first(wide, out_ref)


def halved_kernel(part_ref, other_ref, keep_ref, send_ref):
    low, high = (
        part_ref[at : at + CHAN // 2, :] + other_ref[at : at + CHAN // 2, :].astype(F32)
        for at in (0, CHAN // 2)
    )
    bit = lax.rem(lax.axis_index("space"), 4) >= 2
    keep_ref[...] = jnp.where(bit, high, low)
    send_ref[...] = jnp.where(bit, low, high).astype(BF16)


def gathered_kernel(own_ref, other_ref, out_ref):
    mine = lax.rem(lax.axis_index("space"), 2)
    for section, ref in ((mine, own_ref), (1 - mine, other_ref)):
        for which in range(2):
            piece = ref[:, which * 9 * CHAN : (which + 1) * 9 * CHAN]
            out_ref[section, which] = piece.astype(F32)

def exchange(value, mask, count):
    return lax.ppermute(value, "space", [(d, d ^ mask) for d in range(count)])


def local(features, cotangent, kernels):
    rows, width = features.shape[1], features.shape[2]
    count = lax.axis_size("space")
    height = rows * count
    scale = 1.0 / math.sqrt(height * width)
    place = lax.axis_index("space")
    beyond = [(i, i + 1) for i in range(1, count - 1, 2)]
    beyond += [(target, source) for source, target in beyond]

    def shape(n, dtype=BF16):
        return jax.ShapeDtypeStruct((n * CHAN, width), dtype)

    def vmem(n):
        return pltpu.VMEM((n * STACK, width), BF16)

    def plain(n):
        return pltpu.VMEM((n * CHAN, width), BF16)

    def neighbours(near, far):
        from_far = lax.ppermute(far, "space", beyond)
        return exchange(near, 1, count), from_far

    row_flops = 2 * CHAN * 9 * CHAN * width * 4
    grad = jax.ShapeDtypeStruct((STACK, STACK), F32)
    tile = jax.ShapeDtypeStruct((CHAN, rows, width), BF16)
    wide = pltpu.VMEM((rows, CHAN, width), F32)
    half = (CHAN, 18 * CHAN)
    entry = [pltpu.VMEM((CHAN, rows, width), BF16), pltpu.SemaphoreType.DMA((PIECES,))]

    x, x_near, x_far = call(
        functools.partial(entry_kernel, 4), (features,), (shape(rows), shape(4), shape(4)),
        entry, 0, "x_rows", place=HBM,
    )
    xnear, xfar = neighbours(x_near, x_far)
    (weights,) = call(
        weights_kernel, (kernels,), (jax.ShapeDtypeStruct((8, 2 * CHAN, 4 * STACK), BF16),), [],
        row_flops, "weights", after=(x_far,),
    )
    inner = call(
        functools.partial(inner_kernel, rows), (x, weights),
        (shape(rows - 2), shape(rows - 4), shape(rows - 6)),
        [vmem(rows), vmem(rows - 2), vmem(rows - 4)], 12 * row_flops, "inner",
    )
    g, g_near, g_far, g_inner = call(
        functools.partial(g_entry_kernel, 2), (cotangent, weights),
        (shape(rows), shape(2), shape(2), shape(rows - 2, F32)),
        [entry[0], vmem(rows), entry[1]], 6 * row_flops, "g_rows", after=(inner[2],), place=HBM,
    )
    gnear, gfar = neighbours(g_near, g_far)
    near = call(
        functools.partial(near_kernel, rows, height), (x, xnear, weights, inner[0], inner[1]),
        (shape(4),) * 3, [vmem(6)] * 3, 12 * row_flops, "forward_near", after=(g_near,),
    )
    dh1_near, edge_near = call(
        functools.partial(backward1_near_kernel, rows),
        (g, gnear, near[2], inner[2], g_inner, weights), (shape(rows - 2), shape(2)),
        [vmem(4)] * 2, 4 * row_flops, "backward1_near",
    )
    near_grads = call(
        functools.partial(grads_near_kernel, rows),
        (g, near[2], inner[2], dh1_near, near[1], inner[1]), (grad, grad),
        [vmem(4), vmem(4), plain(6), plain(6)], 8 * row_flops, "grads_near", after=(edge_near,),
    )
    hid0, x1, hid1 = call(
        functools.partial(far_kernel, rows, height), (x, xfar, weights, *inner, *near),
        (shape(rows + 2),) * 3, [plain(4)] * 3 + [vmem(6)] * 3, 12 * row_flops, "forward_far",
        after=(near_grads[1],),
    )
    g1_near, g1_far, edges, dh1 = call(
        functools.partial(backward1_far_kernel, rows),
        (g, gfar, hid1, g_inner, weights, dh1_near, edge_near),
        (shape(1), shape(1), shape(4), shape(rows + 2)), [vmem(4)] * 2, 4 * row_flops, "backward1_far",
    )
    g1near, g1far = neighbours(g1_near, g1_far)
    g1, dh0_inner, *grads = call(
        functools.partial(middle_kernel, rows), (g, edges, hid1, dh1, x1, hid0, x, weights, *near_grads),
        (shape(rows), shape(rows - 2)) + (grad,) * 4,
        [vmem(rows - 4), vmem(rows + 2), vmem(rows), vmem(rows - 2)],
        36 * row_flops, "middle",
    )
    dh0_near, dh0_far, part, send = call(
        functools.partial(backward0_kernel, rows, scale),
        (g1, g1near, g1far, hid0, x, xnear, xfar, weights, *grads),
        (shape(1), shape(1), jax.ShapeDtypeStruct(half, F32),
         jax.ShapeDtypeStruct(half, BF16)),
        [plain(2), vmem(6), vmem(2), plain(6),
         pltpu.VMEM((2, *half), F32)],
        8 * row_flops, "backward0",
    )

    quarter = (CHAN // 2, 18 * CHAN)
    part, send = call(
        halved_kernel, (part, exchange(send, 1, count)),
        (jax.ShapeDtypeStruct(quarter, F32), jax.ShapeDtypeStruct(quarter, BF16)), [], 0, "halved",
    )
    arrived = exchange(send, 2, count)
    dh0_near, dh0_far, _ = lax.optimization_barrier((dh0_near, dh0_far, send))
    dh0near, dh0far = neighbours(dh0_near, dh0_far)
    part = part + arrived.astype(F32)
    step = 4
    input_grad = None
    while step < count:
        send = part.astype(BF16)
        masks = [step, 2 * step, 3 * step] if 2 * step < count else [step]
        arrived = [exchange(send, mask, count) for mask in masks]
        if input_grad is None:
            (input_grad,) = call(
                functools.partial(input_grad_kernel, rows), (dh0_inner, dh0_near, dh0_far, dh0near, dh0far, g1, weights),
                (tile,),
                [vmem(rows + 2), wide], 8 * row_flops, "input_grad", after=(send,),
            )
            arrived, input_grad = lax.optimization_barrier((arrived, input_grad))
        own = send.astype(F32)
        arrived = [value.astype(F32) for value in arrived]
        part = own + arrived[0]
        if len(masks) == 3:
            part = part + (arrived[1] + arrived[2])
        step *= len(masks) + 1
    done = part.astype(BF16)
    bit = (place & 2) != 0
    other = exchange(done, 2, count)
    (section_output,) = call(
        functools.partial(output_kernel, rows), (hid1, x1, weights), (tile,),
        [vmem(rows + 2), wide], 8 * row_flops, "output", after=(done,),
    )
    other, section_output = lax.optimization_barrier((other, section_output))
    done = jnp.where(bit, jnp.concatenate([other, done]), jnp.concatenate([done, other]))
    (kernel_grad,) = call(
        gathered_kernel, (done, exchange(done, 1, count)),
        (jax.ShapeDtypeStruct((2, 2, CHAN, 9 * CHAN), F32),), [], 0, "gathered",
    )
    return (section_output, input_grad, kernel_grad)


def solution(mesh):
    return jax.shard_map(
        local,
        mesh=mesh,
        in_specs=(P(None, "space", "groups"), P(None, "space", "groups"), P()),
        out_specs=(
            P(None, "space", "groups"),
            P(None, "space", "groups"),
            P("groups", None, None, None),
        ),
        check_vma=False,
    )
```

```python
import functools
import math

import jax
import jax.numpy as jnp
from jax import lax
from jax.experimental import pallas as pl
from jax.experimental.pallas import tpu as pltpu
from jax.sharding import PartitionSpec as P

CHAN = 64
STACK = 3 * CHAN
F32 = jnp.float32
BF16 = jnp.bfloat16
VMEM = pl.BlockSpec(memory_space=pltpu.VMEM)
ANY = pl.BlockSpec(memory_space=pl.ANY)
HBM = pl.BlockSpec(memory_space=pltpu.HBM)
PIECES = 4


def call(body, operands, outs, scratch, flops, name, after=(), place=VMEM):
    nbytes = sum(v.size * v.dtype.itemsize for v in (*operands, *outs))
    held = sum(math.prod(v.shape) * v.dtype.itemsize for v in scratch if v.dtype in (F32, BF16))

    def kernel(*refs):
        body(*refs[len(after) :])

    return pl.pallas_call(
        kernel,
        out_shape=outs,
        in_specs=[ANY] * len(after) + [place] + [VMEM] * (len(operands) - 1),
        out_specs=[VMEM] * len(outs),
        scratch_shapes=scratch,
        compiler_params=pltpu.CompilerParams(vmem_limit_bytes=nbytes + held + (6 << 20)),
        cost_estimate=pl.CostEstimate(flops=flops, bytes_accessed=nbytes, transcendentals=0),
        name=name,
    )(*after, *operands)


def stacked(field):
    width = field.shape[1]
    lane = lax.broadcasted_iota(jnp.int32, field.shape, 1)
    zero = jnp.zeros_like(field)
    left = jnp.where(lane == 0, zero, pltpu.roll(field, 1, 1))
    right = jnp.where(lane == width - 1, zero, pltpu.roll(field, width - 1, 1))
    return jnp.concatenate([left, field, right], axis=0)


def put(ref, row, field):
    ref[row * STACK : (row + 1) * STACK, :] = stacked(field)


def middle(ref, row):
    return ref[row * STACK + CHAN : row * STACK + 2 * CHAN, :]


def one(ref, row):
    return ref[row * CHAN : (row + 1) * CHAN, :]


def stack_rows(ref, rows, target, at):
    for row in rows:
        put(target, row + at, one(ref, row))


def g_entry_kernel(
    edge, tile_ref, w_ref, rows_ref, near_ref, far_ref, inner_ref, held, g3, arrived
):
    entry_kernel(edge, tile_ref, rows_ref, near_ref, far_ref, held, arrived)
    rows = tile_ref.shape[1]
    stack_rows(rows_ref, range(rows), g3, 0)

    def keep(row, total):
        inner_ref[row * CHAN : (row + 1) * CHAN, :] = total

    conv_rows(w_ref[7], g3, 0, rows - 2, keep)


def copy_rows(ref, count, target, at):
    target[at * CHAN : (at + count) * CHAN, :] = ref[: count * CHAN, :]


def two_rows(target, index, column, value):
    width = value.shape[1]
    target[index, :CHAN, column : column + width] = value
    target[index, CHAN:, STACK + column : STACK + column + width] = value


def weights_kernel(kernels_ref, target):
    target[...] = jnp.zeros_like(target)
    line = lax.broadcasted_iota(jnp.int32, (CHAN, CHAN), 0)
    same = line == lax.broadcasted_iota(jnp.int32, (CHAN, CHAN), 1)
    unit = jnp.where(same, 1.0, 0.0).astype(BF16)
    for section in range(2):
        for which in range(2):
            index = 2 * (2 * section + which)
            two_rows(target, index, 0, kernels_ref[section, which])
            for tap in range(9):
                at = (8 - tap) * CHAN
                block = kernels_ref[section, which, :, at : at + CHAN]
                turned = lax.dot_general(
                    unit, block, (((1,), (1,)), ((), ())), preferred_element_type=F32
                )
                two_rows(target, index + 1, tap * CHAN, turned.astype(BF16))


def conv_rows(weight, source, first, count, finish):
    for row in range(first, first + count, 2):
        total = jnp.dot(
            weight,
            source[row * STACK : (row + 4) * STACK, :],
            preferred_element_type=F32,
        )
        finish(row, total[:CHAN])
        finish(row + 1, total[CHAN:])


def grad_rows(upper, upper_row, lower, lower_row, count):
    total = None
    for row in range(0, count, 2):
        left = upper[(row + upper_row) * STACK : (row + upper_row + 2) * STACK, :]
        right = lower[(row + lower_row) * CHAN : (row + lower_row + 4) * CHAN, :]
        term = lax.dot_general(
            left, right, (((1,), (1,)), ((), ())), preferred_element_type=F32
        )
        total = term if total is None else total + term
    return total[:STACK, :STACK] + total[STACK:, CHAN:]


def channels_first(wide, target):
    target[...] = jnp.swapaxes(wide[...], 0, 1).astype(BF16)


def odd_place():
    return lax.rem(lax.axis_index("space"), 2) == 1


def put_at(ref, row, field):
    ref[pl.ds(pl.multiple_of(row * STACK, CHAN), STACK), :] = stacked(field)


def halo_rows(near_ref, far_ref, count, rows, target):
    odd = odd_place()
    above, below = 0, rows + count
    near_at = jnp.where(odd, above, below)
    far_at = jnp.where(odd, below, above)
    for row in range(count):
        put_at(target, near_at + row, one(near_ref, row))
        put_at(target, far_at + row, one(far_ref, row))


def send_edges(rows_ref, edge, near_ref, far_ref):
    odd = odd_place()
    last = rows_ref.shape[0] - edge * CHAN
    near_at = jnp.where(odd, 0, last)
    far_at = jnp.where(odd, last, 0)
    near_ref[...] = rows_ref[pl.ds(pl.multiple_of(near_at, CHAN), edge * CHAN), :]
    far_ref[...] = rows_ref[pl.ds(pl.multiple_of(far_at, CHAN), edge * CHAN), :]


def entry_kernel(edge, tile_ref, rows_ref, near_ref, far_ref, held, arrived):
    piece = CHAN // PIECES
    copies = [
        pltpu.make_async_copy(
            tile_ref.at[i * piece : (i + 1) * piece],
            held.at[i * piece : (i + 1) * piece],
            arrived.at[i],
        )
        for i in range(PIECES)
    ]
    for copy in copies:
        copy.start()
    for i, copy in enumerate(copies):
        copy.wait()
        part = held[i * piece : (i + 1) * piece].astype(F32)
        turned = jnp.swapaxes(part, 0, 1).astype(BF16)
        for row in range(turned.shape[0]):
            at = row * CHAN + i * piece
            rows_ref[at : at + piece, :] = turned[row]
    send_edges(rows_ref, edge, near_ref, far_ref)


def channels_first(wide, target):
    target[...] = jnp.swapaxes(wide[...], 0, 1).astype(BF16)


def inner_kernel(rows, x_ref, w_ref, hid0_ref, x1_ref, hid1_ref, x3, h3, y3):
    stack_rows(x_ref, range(rows), x3, 0)

    def hidden0(row, total):
        value = jnp.maximum(total, 0.0).astype(BF16)
        put(h3, row, value)
        hid0_ref[row * CHAN : (row + 1) * CHAN, :] = value

    conv_rows(w_ref[0], x3, 0, rows - 2, hidden0)

    def next_x(row, total):
        value = (one(x_ref, row + 2).astype(F32) + total).astype(BF16)
        put(y3, row, value)
        x1_ref[row * CHAN : (row + 1) * CHAN, :] = value

    conv_rows(w_ref[2], h3, 0, rows - 4, next_x)

    def hidden1(row, total):
        hid1_ref[row * CHAN : (row + 1) * CHAN, :] = jnp.maximum(total, 0.0).astype(BF16)

    conv_rows(w_ref[4], y3, 0, rows - 6, hidden1)


def side_rows(rows, height, top, x_ref, halo_ref, w_ref, hid0_in, x1_in, hid0, x1, hid1, x3, h3, y3):
    first = lax.axis_index("space") * rows
    own, rest = (0, 4) if top else (2, 0)

    def inside(row, value):
        if 0 <= row < rows:
            return value
        keep = jnp.logical_and(first + row >= 0, first + row < height)
        return jnp.where(keep, value, 0.0)

    for i in range(4):
        put(x3, own + i, one(halo_ref, i))
    for i in range(2):
        put(x3, rest + i, one(x_ref, (0 if top else rows - 2) + i))
        put(h3, rest + i, one(hid0_in, (0 if top else rows - 4) + i))
        put(y3, rest + i, one(x1_in, (0 if top else rows - 6) + i))

    def hidden0(row, total):
        at = (-3 if top else rows - 1) + row
        value = inside(at, jnp.maximum(total, 0.0)).astype(BF16)
        hid0[row * CHAN : (row + 1) * CHAN, :] = value
        put(h3, own + row, value)

    conv_rows(w_ref[0], x3, 0, 4, hidden0)

    def next_x(row, total):
        at = (-2 if top else rows - 2) + row
        value = middle(x3, (2 if top else 0) + row).astype(F32) + total
        value = inside(at, value).astype(BF16)
        x1[row * CHAN : (row + 1) * CHAN, :] = value
        put(y3, own + row, value)

    conv_rows(w_ref[2], h3, 0, 4, next_x)

    def hidden1(row, total):
        at = (-1 if top else rows - 3) + row
        value = inside(at, jnp.maximum(total, 0.0)).astype(BF16)
        hid1[row * CHAN : (row + 1) * CHAN, :] = value

    conv_rows(w_ref[4], y3, 0, 4, hidden1)


def near_kernel(rows, height, *refs):
    odd = odd_place()
    for top in (True, False):
        pl.when(odd == top)(functools.partial(side_rows, rows, height, top, *refs))


def far_kernel(
    rows, height, x_ref, far_ref, w_ref, hid0_in, x1_in, hid1_in, near0, near1, near2,
    hid0_ref, x1_ref, hid1_ref, far0, far1, far2, *scratch,
):
    def far_side(top):
        side_rows(
            rows, height, top, x_ref, far_ref, w_ref, hid0_in, x1_in, far0, far1, far2, *scratch
        )
        for edge, hid0, x1, hid1 in ((top, far0, far1, far2), (not top, near0, near1, near2)):
            for target, source, count in ((hid0_ref, hid0, 2), (x1_ref, x1, 3), (hid1_ref, hid1, 4)):
                to = 0 if edge else rows + 2 - count
                at = 4 - count if edge else 0
                target[to * CHAN : (to + count) * CHAN, :] = source[at * CHAN : (at + count) * CHAN, :]

    copy_rows(hid0_in, rows - 2, hid0_ref, 2)
    copy_rows(x1_in, rows - 4, x1_ref, 3)
    copy_rows(hid1_in, rows - 6, hid1_ref, 4)
    odd = odd_place()
    for top in (True, False):
        pl.when(odd != top)(functools.partial(far_side, top))


def backward_side(
    rows, top, g_ref, halo_ref, hid1_row, inner_ref, w_ref, inner_rows, keep_dh1, keep_edge, g3, d3
):
    start = 0 if top else rows - 2
    for i in range(2):
        put(g3, (0 if top else 2) + i, one(halo_ref, i))
        put(g3, (2 if top else 0) + i, one(g_ref, start + i))

    def dhidden1(row, total):
        value = jnp.where(hid1_row(row) > 0, total, 0.0).astype(BF16)
        keep_dh1(row, value)
        at = row + 1 if top else row - (rows - 3)
        if 0 <= at < 4:
            put(d3, at, value)

    for row in inner_rows:
        dhidden1(row, one(inner_ref, row - 1))
    edge = -1 if top else rows - 1
    conv_rows(w_ref[7], g3, 0, 2, lambda row, total: dhidden1(edge + row, total))

    def next_g(row, total):
        keep_edge(row, (one(g_ref, start + row).astype(F32) + total).astype(BF16))

    conv_rows(w_ref[5], d3, 0, 2, next_g)


def backward1_near_kernel(
    rows, g_ref, near_ref, hid1_near, hid1_in, inner_ref, w_ref, dh1_ref, edge_ref, g3, d3
):
    def near_side(top):
        def hid1_row(row):
            if 3 <= row < rows - 3:
                return one(hid1_in, row - 3)
            return one(hid1_near, row + 1 if top else row - (rows - 3))

        def keep_dh1(row, value):
            at = row + 1 if top else row - 3
            dh1_ref[at * CHAN : (at + 1) * CHAN, :] = value

        def keep_edge(row, value):
            edge_ref[row * CHAN : (row + 1) * CHAN, :] = value

        inner_rows = range(1, rows - 3) if top else range(3, rows - 1)
        backward_side(
            rows, top, g_ref, near_ref, hid1_row, inner_ref, w_ref, inner_rows, keep_dh1, keep_edge, g3, d3
        )

    odd = odd_place()
    for top in (True, False):
        pl.when(odd == top)(functools.partial(near_side, top))


def backward1_far_kernel(
    rows, g_ref, far_ref, hid1_ref, inner_ref, w_ref, dh1_near, edge_near,
    next_near, next_far, edges_ref, dh1_ref, g3, d3,
):
    def far_side(top):
        def keep_dh1(row, value):
            dh1_ref[(row + 1) * CHAN : (row + 2) * CHAN, :] = value

        def keep_edge(row, value):
            at = row if top else 2 + row
            edges_ref[at * CHAN : (at + 1) * CHAN, :] = value

        inner_rows = (1, 2) if top else (rows - 3, rows - 2)
        backward_side(
            rows, top, g_ref, far_ref, lambda row: one(hid1_ref, row + 1), inner_ref, w_ref, inner_rows,
            keep_dh1, keep_edge, g3, d3,
        )
        copy_rows(dh1_near, rows - 2, dh1_ref, 4 if top else 0)
        copy_rows(edge_near, 2, edges_ref, 2 if top else 0)

    odd = odd_place()
    for top in (True, False):
        pl.when(odd != top)(functools.partial(far_side, top))
    send_edges(edges_ref, 1, next_near, next_far)


def grads_near_kernel(
    rows, g_ref, hid1_near, hid1_in, dh1_near, x1_near, x1_in, grad11, grad10, s3, t3, hid1, x1
):
    def near_side(top):
        start = 0 if top else rows - 4
        for i in range(4):
            put(s3, i, one(g_ref, start + i))
            put(t3, i, one(dh1_near, start + i + 1 if top else start + i - 3))
        for i in range(6):
            row = start - 1 + i
            if 3 <= row < rows - 3:
                value = one(hid1_in, row - 3)
            else:
                value = one(hid1_near, row + 1 if top else row - (rows - 3))
            hid1[i * CHAN : (i + 1) * CHAN, :] = value
            if 2 <= row < rows - 2:
                value = one(x1_in, row - 2)
            else:
                value = one(x1_near, row + 2 if top else row - (rows - 2))
            x1[i * CHAN : (i + 1) * CHAN, :] = value
        grad11[...] = grad_rows(s3, 0, hid1, 0, 4)
        grad10[...] = grad_rows(t3, 0, x1, 0, 4)

    odd = odd_place()
    for top in (True, False):
        pl.when(odd == top)(functools.partial(near_side, top))


def grad_rows_from(upper, upper_row, lower, lower_row, count):
    total = None
    for row in range(0, count, 2):
        left = pl.ds(pl.multiple_of((row + upper_row) * STACK, CHAN), 2 * STACK)
        right = pl.ds(pl.multiple_of((row + lower_row) * CHAN, CHAN), 4 * CHAN)
        term = lax.dot_general(
            upper[left, :], lower[right, :], (((1,), (1,)), ((), ())), preferred_element_type=F32
        )
        total = term if total is None else total + term
    return total[:STACK, :STACK] + total[STACK:, CHAN:]


def middle_kernel(
    rows, g_ref, edges_ref, hid1_ref, dh1_ref, x1_ref, hid0_ref, x_ref, w_ref, near11, near10,
    g1_ref, dh0_ref, grad00, grad01, grad10, grad11, s3, t3, u3, v3,
):
    stack_rows(dh1_ref, range(1, rows + 1), t3, 0)
    copy_rows(edges_ref, 2, g1_ref, 0)
    g1_ref[(rows - 2) * CHAN :, :] = edges_ref[2 * CHAN :, :]

    def next_g(row, total):
        value = (one(g_ref, row).astype(F32) + total).astype(BF16)
        g1_ref[row * CHAN : (row + 1) * CHAN, :] = value
        put(u3, row, value)

    conv_rows(w_ref[5], t3, 2, rows - 4, next_g)
    stack_rows(g1_ref, (0, 1, rows - 2, rows - 1), u3, 0)

    def dhidden0(row, total):
        value = jnp.where(one(hid0_ref, row + 2) > 0, total, 0.0).astype(BF16)
        dh0_ref[row * CHAN : (row + 1) * CHAN, :] = value
        put(v3, row, value)

    conv_rows(w_ref[3], u3, 0, rows - 2, dhidden0)
    start = jnp.where(odd_place(), 4, 0)
    for row in range(rows - 4):
        source = pl.ds(pl.multiple_of((start + row) * CHAN, CHAN), CHAN)
        put(s3, row, g_ref[source, :])
    grad11[...] = near11[...] + grad_rows_from(s3, 0, hid1_ref, start, rows - 4)
    grad10[...] = near10[...] + grad_rows_from(t3, start + 1, x1_ref, start, rows - 4)
    grad01[...] = grad_rows(u3, 0, hid0_ref, 0, rows)
    grad00[...] = grad_rows(v3, 0, x_ref, 0, rows - 2)


def output_kernel(rows, hid1_ref, x1_ref, w_ref, out_ref, k3, wide):
    stack_rows(hid1_ref, range(rows + 2), k3, 0)

    def last_x(row, total):
        wide[row] = one(x1_ref, row + 1).astype(F32) + total

    conv_rows(w_ref[6], k3, 0, rows, last_x)
    channels_first(wide, out_ref)


def backward0_kernel(
    rows, scale, g1_ref, near_ref, far_ref, hid0_ref, x_ref, xnear_ref, xfar_ref, w_ref, inner00,
    grad01, grad10, grad11, next_near, next_far, keep_ref, send_ref,
    d0, g3, d3, xs, both,
):
    odd = odd_place()
    near_at, far_at = jnp.where(odd, 0, 5), jnp.where(odd, 5, 0)
    put_at(g3, near_at, one(near_ref, 0))
    put_at(g3, far_at, one(far_ref, 0))
    stack_rows(g1_ref, (0, 1), g3, 1)
    stack_rows(g1_ref, (rows - 2, rows - 1), g3, 5 - rows)
    copy_rows(x_ref, 2, xs, 1)
    xs[3 * CHAN : 5 * CHAN, :] = x_ref[(rows - 2) * CHAN :, :]
    near_row, far_row = jnp.where(odd, 3, 0), jnp.where(odd, 0, 3)
    for ref, at, row in ((xnear_ref, near_at, near_row), (xfar_ref, far_at, far_row)):
        source = pl.ds(pl.multiple_of(row * CHAN, CHAN), CHAN)
        xs[pl.ds(pl.multiple_of(at * CHAN, CHAN), CHAN), :] = ref[source, :]
    grad00 = inner00[...]
    for end, row in ((0, 0), (1, rows - 1)):
        total = jnp.dot(
            w_ref[3, :CHAN, : 3 * STACK],
            g3[3 * end * STACK : 3 * (end + 1) * STACK, :],
            preferred_element_type=F32,
        )
        value = jnp.where(one(hid0_ref, row + 1) > 0, total, 0.0).astype(BF16)
        d0[end * CHAN : (end + 1) * CHAN, :] = value
        put(d3, end, value)
    for end in range(2):
        grad00 = grad00 + lax.dot_general(
            d3[end * STACK : (end + 1) * STACK, :],
            xs[end * STACK : (end + 1) * STACK, :],
            (((1,), (1,)), ((), ())),
            preferred_element_type=F32,
        )
    send_edges(d0, 1, next_near, next_far)
    pairs = ((grad00, grad01[...]), (grad10[...], grad11[...]))
    for section, pair in enumerate(pairs):
        for which, value in enumerate(pair):
            for a in range(3):
                for b in range(3):
                    block = value[(2 - b) * CHAN : (3 - b) * CHAN, a * CHAN : (a + 1) * CHAN]
                    at = which * 9 * CHAN + (3 * a + b) * CHAN
                    both[section, :, at : at + CHAN] = block * scale
    mine = lax.rem(lax.axis_index("space"), 2)
    keep_ref[...] = both[mine]
    send_ref[...] = both[1 - mine].astype(BF16)


def input_grad_kernel(rows, dh0_in, own_near, own_far, near_ref, far_ref, g1_ref, w_ref, out_ref, d3, wide):
    halo_rows(near_ref, far_ref, 1, rows, d3)
    stack_rows(dh0_in, range(rows - 2), d3, 2)
    odd = odd_place()
    put_at(d3, jnp.where(odd, 1, rows), one(own_near, 0))
    put_at(d3, jnp.where(odd, rows, 1), one(own_far, 0))

    def last_g(row, total):
        wide[row] = one(g1_ref, row).astype(F32) + total

    conv_rows(w_ref[1], d3, 0, rows, last_g)
    channels_first(wide, out_ref)


def halved_kernel(part_ref, other_ref, keep_ref, send_ref):
    low, high = (
        part_ref[at : at + CHAN // 2, :] + other_ref[at : at + CHAN // 2, :].astype(F32)
        for at in (0, CHAN // 2)
    )
    bit = lax.rem(lax.axis_index("space"), 4) >= 2
    keep_ref[...] = jnp.where(bit, high, low)
    send_ref[...] = jnp.where(bit, low, high).astype(BF16)


def gathered_kernel(own_ref, other_ref, out_ref):
    mine = lax.rem(lax.axis_index("space"), 2)
    for section, ref in ((mine, own_ref), (1 - mine, other_ref)):
        for which in range(2):
            piece = ref[:, which * 9 * CHAN : (which + 1) * 9 * CHAN]
            out_ref[section, which] = piece.astype(F32)

def exchange(value, mask, count):
    return lax.ppermute(value, "space", [(d, d ^ mask) for d in range(count)])


def local(features, cotangent, kernels):
    rows, width = features.shape[1], features.shape[2]
    count = lax.axis_size("space")
    height = rows * count
    scale = 1.0 / math.sqrt(height * width)
    place = lax.axis_index("space")
    beyond = [(i, i + 1) for i in range(1, count - 1, 2)]
    beyond += [(target, source) for source, target in beyond]

    def shape(n, dtype=BF16):
        return jax.ShapeDtypeStruct((n * CHAN, width), dtype)

    def vmem(n):
        return pltpu.VMEM((n * STACK, width), BF16)

    def plain(n):
        return pltpu.VMEM((n * CHAN, width), BF16)

    def neighbours(near, far):
        from_far = lax.ppermute(far, "space", beyond)
        return exchange(near, 1, count), from_far

    row_flops = 2 * CHAN * 9 * CHAN * width * 4
    grad = jax.ShapeDtypeStruct((STACK, STACK), F32)
    tile = jax.ShapeDtypeStruct((CHAN, rows, width), BF16)
    wide = pltpu.VMEM((rows, CHAN, width), F32)
    half = (CHAN, 18 * CHAN)
    entry = [pltpu.VMEM((CHAN, rows, width), BF16), pltpu.SemaphoreType.DMA((PIECES,))]

    x, x_near, x_far = call(
        functools.partial(entry_kernel, 4), (features,), (shape(rows), shape(4), shape(4)),
        entry, 0, "x_rows", place=HBM,
    )
    xnear, xfar = neighbours(x_near, x_far)
    (weights,) = call(
        weights_kernel, (kernels,), (jax.ShapeDtypeStruct((8, 2 * CHAN, 4 * STACK), BF16),), [],
        row_flops, "weights", after=(x_far,),
    )
    inner = call(
        functools.partial(inner_kernel, rows), (x, weights),
        (shape(rows - 2), shape(rows - 4), shape(rows - 6)),
        [vmem(rows), vmem(rows - 2), vmem(rows - 4)], 12 * row_flops, "inner",
    )
    g, g_near, g_far, g_inner = call(
        functools.partial(g_entry_kernel, 2), (cotangent, weights),
        (shape(rows), shape(2), shape(2), shape(rows - 2, F32)),
        [entry[0], vmem(rows), entry[1]], 6 * row_flops, "g_rows", after=(inner[2],), place=HBM,
    )
    gnear, gfar = neighbours(g_near, g_far)
    near = call(
        functools.partial(near_kernel, rows, height), (x, xnear, weights, inner[0], inner[1]),
        (shape(4),) * 3, [vmem(6)] * 3, 12 * row_flops, "forward_near", after=(g_near,),
    )
    dh1_near, edge_near = call(
        functools.partial(backward1_near_kernel, rows),
        (g, gnear, near[2], inner[2], g_inner, weights), (shape(rows - 2), shape(2)),
        [vmem(4)] * 2, 4 * row_flops, "backward1_near",
    )
    near_grads = call(
        functools.partial(grads_near_kernel, rows),
        (g, near[2], inner[2], dh1_near, near[1], inner[1]), (grad, grad),
        [vmem(4), vmem(4), plain(6), plain(6)], 8 * row_flops, "grads_near", after=(edge_near,),
    )
    hid0, x1, hid1 = call(
        functools.partial(far_kernel, rows, height), (x, xfar, weights, *inner, *near),
        (shape(rows + 2),) * 3, [plain(4)] * 3 + [vmem(6)] * 3, 12 * row_flops, "forward_far",
        after=(near_grads[1],),
    )
    g1_near, g1_far, edges, dh1 = call(
        functools.partial(backward1_far_kernel, rows),
        (g, gfar, hid1, g_inner, weights, dh1_near, edge_near),
        (shape(1), shape(1), shape(4), shape(rows + 2)), [vmem(4)] * 2, 4 * row_flops, "backward1_far",
    )
    g1near, g1far = neighbours(g1_near, g1_far)
    g1, dh0_inner, *grads = call(
        functools.partial(middle_kernel, rows), (g, edges, hid1, dh1, x1, hid0, x, weights, *near_grads),
        (shape(rows), shape(rows - 2)) + (grad,) * 4,
        [vmem(rows - 4), vmem(rows + 2), vmem(rows), vmem(rows - 2)],
        36 * row_flops, "middle",
    )
    dh0_near, dh0_far, part, send = call(
        functools.partial(backward0_kernel, rows, scale),
        (g1, g1near, g1far, hid0, x, xnear, xfar, weights, *grads),
        (shape(1), shape(1), jax.ShapeDtypeStruct(half, F32),
         jax.ShapeDtypeStruct(half, BF16)),
        [plain(2), vmem(6), vmem(2), plain(6),
         pltpu.VMEM((2, *half), F32)],
        8 * row_flops, "backward0",
    )

    quarter = (CHAN // 2, 18 * CHAN)
    part, send = call(
        halved_kernel, (part, exchange(send, 1, count)),
        (jax.ShapeDtypeStruct(quarter, F32), jax.ShapeDtypeStruct(quarter, BF16)), [], 0, "halved",
    )
    arrived = exchange(send, 2, count)
    dh0_near, dh0_far, _ = lax.optimization_barrier((dh0_near, dh0_far, send))
    dh0near, dh0far = neighbours(dh0_near, dh0_far)
    part = part + arrived.astype(F32)
    step = 4
    section_output = None
    while step < count:
        send = part.astype(BF16)
        masks = [step, 2 * step, 3 * step] if 2 * step < count else [step]
        arrived = [exchange(send, mask, count) for mask in masks]
        if section_output is None:
            (section_output,) = call(
                functools.partial(output_kernel, rows), (hid1, x1, weights), (tile,),
                [vmem(rows + 2), wide], 8 * row_flops, "output", after=(send,),
            )
            arrived, section_output = lax.optimization_barrier((arrived, section_output))
        own = send.astype(F32)
        arrived = [value.astype(F32) for value in arrived]
        part = own + arrived[0]
        if len(masks) == 3:
            part = part + (arrived[1] + arrived[2])
        step *= len(masks) + 1
    done = part.astype(BF16)
    bit = (place & 2) != 0
    other = exchange(done, 2, count)
    (input_grad,) = call(
        functools.partial(input_grad_kernel, rows), (dh0_inner, dh0_near, dh0_far, dh0near, dh0far, g1, weights),
        (tile,),
        [vmem(rows + 2), wide], 8 * row_flops, "input_grad", after=(done,),
    )
    other, input_grad = lax.optimization_barrier((other, input_grad))
    done = jnp.where(bit, jnp.concatenate([other, done]), jnp.concatenate([done, other]))
    (kernel_grad,) = call(
        gathered_kernel, (done, exchange(done, 1, count)),
        (jax.ShapeDtypeStruct((2, 2, CHAN, 9 * CHAN), F32),), [], 0, "gathered",
    )
    return (section_output, input_grad, kernel_grad)


def solution(mesh):
    return jax.shard_map(
        local,
        mesh=mesh,
        in_specs=(P(None, "space", "groups"), P(None, "space", "groups"), P()),
        out_specs=(
            P(None, "space", "groups"),
            P(None, "space", "groups"),
            P("groups", None, None, None),
        ),
        check_vma=False,
    )
```

```python
import functools
import math

import jax
import jax.numpy as jnp
from jax import lax
from jax.experimental import pallas as pl
from jax.experimental.pallas import tpu as pltpu
from jax.sharding import PartitionSpec as P

CHAN = 64
STACK = 3 * CHAN
F32 = jnp.float32
BF16 = jnp.bfloat16
VMEM = pl.BlockSpec(memory_space=pltpu.VMEM)
ANY = pl.BlockSpec(memory_space=pl.ANY)
HBM = pl.BlockSpec(memory_space=pltpu.HBM)
PIECES = 4


def call(body, operands, outs, scratch, flops, name, after=(), place=VMEM):
    nbytes = sum(v.size * v.dtype.itemsize for v in (*operands, *outs))
    held = sum(math.prod(v.shape) * v.dtype.itemsize for v in scratch if v.dtype in (F32, BF16))

    def kernel(*refs):
        body(*refs[len(after) :])

    return pl.pallas_call(
        kernel,
        out_shape=outs,
        in_specs=[ANY] * len(after) + [place] + [VMEM] * (len(operands) - 1),
        out_specs=[VMEM] * len(outs),
        scratch_shapes=scratch,
        compiler_params=pltpu.CompilerParams(vmem_limit_bytes=nbytes + held + (6 << 20)),
        cost_estimate=pl.CostEstimate(flops=flops, bytes_accessed=nbytes, transcendentals=0),
        name=name,
    )(*after, *operands)


def stacked(field):
    width = field.shape[1]
    lane = lax.broadcasted_iota(jnp.int32, field.shape, 1)
    zero = jnp.zeros_like(field)
    left = jnp.where(lane == 0, zero, pltpu.roll(field, 1, 1))
    right = jnp.where(lane == width - 1, zero, pltpu.roll(field, width - 1, 1))
    return jnp.concatenate([left, field, right], axis=0)


def put(ref, row, field):
    ref[row * STACK : (row + 1) * STACK, :] = stacked(field)


def middle(ref, row):
    return ref[row * STACK + CHAN : row * STACK + 2 * CHAN, :]


def one(ref, row):
    return ref[row * CHAN : (row + 1) * CHAN, :]


def stack_rows(ref, rows, target, at):
    for row in rows:
        put(target, row + at, one(ref, row))


def g_entry_kernel(
    edge, tile_ref, w_ref, rows_ref, near_ref, far_ref, inner_ref, g3
):
    entry_kernel(edge, tile_ref, rows_ref, near_ref, far_ref)
    rows = tile_ref.shape[1]
    stack_rows(rows_ref, range(rows), g3, 0)

    def keep(row, total):
        inner_ref[row * CHAN : (row + 1) * CHAN, :] = total

    conv_rows(w_ref[7], g3, 0, rows - 2, keep)


def copy_rows(ref, count, target, at):
    target[at * CHAN : (at + count) * CHAN, :] = ref[: count * CHAN, :]


def two_rows(target, index, column, value):
    width = value.shape[1]
    target[index, :CHAN, column : column + width] = value
    target[index, CHAN:, STACK + column : STACK + column + width] = value


def weights_kernel(kernels_ref, target):
    target[...] = jnp.zeros_like(target)
    line = lax.broadcasted_iota(jnp.int32, (CHAN, CHAN), 0)
    same = line == lax.broadcasted_iota(jnp.int32, (CHAN, CHAN), 1)
    unit = jnp.where(same, 1.0, 0.0).astype(BF16)
    for section in range(2):
        for which in range(2):
            index = 2 * (2 * section + which)
            two_rows(target, index, 0, kernels_ref[section, which])
            for tap in range(9):
                at = (8 - tap) * CHAN
                block = kernels_ref[section, which, :, at : at + CHAN]
                turned = lax.dot_general(
                    unit, block, (((1,), (1,)), ((), ())), preferred_element_type=F32
                )
                two_rows(target, index + 1, tap * CHAN, turned.astype(BF16))


def conv_rows(weight, source, first, count, finish):
    for row in range(first, first + count, 2):
        total = jnp.dot(
            weight,
            source[row * STACK : (row + 4) * STACK, :],
            preferred_element_type=F32,
        )
        finish(row, total[:CHAN])
        finish(row + 1, total[CHAN:])


def grad_rows(upper, upper_row, lower, lower_row, count):
    total = None
    for row in range(0, count, 2):
        left = upper[(row + upper_row) * STACK : (row + upper_row + 2) * STACK, :]
        right = lower[(row + lower_row) * CHAN : (row + lower_row + 4) * CHAN, :]
        term = lax.dot_general(
            left, right, (((1,), (1,)), ((), ())), preferred_element_type=F32
        )
        total = term if total is None else total + term
    return total[:STACK, :STACK] + total[STACK:, CHAN:]


def channels_first(wide, target):
    target[...] = jnp.swapaxes(wide[...], 0, 1).astype(BF16)


def odd_place():
    return lax.rem(lax.axis_index("space"), 2) == 1


def put_at(ref, row, field):
    ref[pl.ds(pl.multiple_of(row * STACK, CHAN), STACK), :] = stacked(field)


def halo_rows(near_ref, far_ref, count, rows, target):
    odd = odd_place()
    above, below = 0, rows + count
    near_at = jnp.where(odd, above, below)
    far_at = jnp.where(odd, below, above)
    for row in range(count):
        put_at(target, near_at + row, one(near_ref, row))
        put_at(target, far_at + row, one(far_ref, row))


def send_edges(rows_ref, edge, near_ref, far_ref):
    odd = odd_place()
    last = rows_ref.shape[0] - edge * CHAN
    near_at = jnp.where(odd, 0, last)
    far_at = jnp.where(odd, last, 0)
    near_ref[...] = rows_ref[pl.ds(pl.multiple_of(near_at, CHAN), edge * CHAN), :]
    far_ref[...] = rows_ref[pl.ds(pl.multiple_of(far_at, CHAN), edge * CHAN), :]


def entry_kernel(edge, tile_ref, rows_ref, near_ref, far_ref):
    piece = CHAN // PIECES
    for i in range(PIECES):
        part = tile_ref[i * piece : (i + 1) * piece].astype(F32)
        turned = jnp.swapaxes(part, 0, 1).astype(BF16)
        for row in range(turned.shape[0]):
            at = row * CHAN + i * piece
            rows_ref[at : at + piece, :] = turned[row]
    send_edges(rows_ref, edge, near_ref, far_ref)


def channels_first(wide, target):
    target[...] = jnp.swapaxes(wide[...], 0, 1).astype(BF16)


def inner_kernel(rows, x_ref, w_ref, hid0_ref, x1_ref, hid1_ref, x3, h3, y3):
    stack_rows(x_ref, range(rows), x3, 0)

    def hidden0(row, total):
        value = jnp.maximum(total, 0.0).astype(BF16)
        put(h3, row, value)
        hid0_ref[row * CHAN : (row + 1) * CHAN, :] = value

    conv_rows(w_ref[0], x3, 0, rows - 2, hidden0)

    def next_x(row, total):
        value = (one(x_ref, row + 2).astype(F32) + total).astype(BF16)
        put(y3, row, value)
        x1_ref[row * CHAN : (row + 1) * CHAN, :] = value

    conv_rows(w_ref[2], h3, 0, rows - 4, next_x)

    def hidden1(row, total):
        hid1_ref[row * CHAN : (row + 1) * CHAN, :] = jnp.maximum(total, 0.0).astype(BF16)

    conv_rows(w_ref[4], y3, 0, rows - 6, hidden1)


def side_rows(rows, height, top, x_ref, halo_ref, w_ref, hid0_in, x1_in, hid0, x1, hid1, x3, h3, y3):
    first = lax.axis_index("space") * rows
    own, rest = (0, 4) if top else (2, 0)

    def inside(row, value):
        if 0 <= row < rows:
            return value
        keep = jnp.logical_and(first + row >= 0, first + row < height)
        return jnp.where(keep, value, 0.0)

    for i in range(4):
        put(x3, own + i, one(halo_ref, i))
    for i in range(2):
        put(x3, rest + i, one(x_ref, (0 if top else rows - 2) + i))
        put(h3, rest + i, one(hid0_in, (0 if top else rows - 4) + i))
        put(y3, rest + i, one(x1_in, (0 if top else rows - 6) + i))

    def hidden0(row, total):
        at = (-3 if top else rows - 1) + row
        value = inside(at, jnp.maximum(total, 0.0)).astype(BF16)
        hid0[row * CHAN : (row + 1) * CHAN, :] = value
        put(h3, own + row, value)

    conv_rows(w_ref[0], x3, 0, 4, hidden0)

    def next_x(row, total):
        at = (-2 if top else rows - 2) + row
        value = middle(x3, (2 if top else 0) + row).astype(F32) + total
        value = inside(at, value).astype(BF16)
        x1[row * CHAN : (row + 1) * CHAN, :] = value
        put(y3, own + row, value)

    conv_rows(w_ref[2], h3, 0, 4, next_x)

    def hidden1(row, total):
        at = (-1 if top else rows - 3) + row
        value = inside(at, jnp.maximum(total, 0.0)).astype(BF16)
        hid1[row * CHAN : (row + 1) * CHAN, :] = value

    conv_rows(w_ref[4], y3, 0, 4, hidden1)


def near_kernel(rows, height, *refs):
    odd = odd_place()
    for top in (True, False):
        pl.when(odd == top)(functools.partial(side_rows, rows, height, top, *refs))


def far_kernel(
    rows, height, x_ref, far_ref, w_ref, hid0_in, x1_in, hid1_in, near0, near1, near2,
    hid0_ref, x1_ref, hid1_ref, far0, far1, far2, *scratch,
):
    def far_side(top):
        side_rows(
            rows, height, top, x_ref, far_ref, w_ref, hid0_in, x1_in, far0, far1, far2, *scratch
        )
        for edge, hid0, x1, hid1 in ((top, far0, far1, far2), (not top, near0, near1, near2)):
            for target, source, count in ((hid0_ref, hid0, 2), (x1_ref, x1, 3), (hid1_ref, hid1, 4)):
                to = 0 if edge else rows + 2 - count
                at = 4 - count if edge else 0
                target[to * CHAN : (to + count) * CHAN, :] = source[at * CHAN : (at + count) * CHAN, :]

    copy_rows(hid0_in, rows - 2, hid0_ref, 2)
    copy_rows(x1_in, rows - 4, x1_ref, 3)
    copy_rows(hid1_in, rows - 6, hid1_ref, 4)
    odd = odd_place()
    for top in (True, False):
        pl.when(odd != top)(functools.partial(far_side, top))


def backward_side(
    rows, top, g_ref, halo_ref, hid1_row, inner_ref, w_ref, inner_rows, keep_dh1, keep_edge, g3, d3
):
    start = 0 if top else rows - 2
    for i in range(2):
        put(g3, (0 if top else 2) + i, one(halo_ref, i))
        put(g3, (2 if top else 0) + i, one(g_ref, start + i))

    def dhidden1(row, total):
        value = jnp.where(hid1_row(row) > 0, total, 0.0).astype(BF16)
        keep_dh1(row, value)
        at = row + 1 if top else row - (rows - 3)
        if 0 <= at < 4:
            put(d3, at, value)

    for row in inner_rows:
        dhidden1(row, one(inner_ref, row - 1))
    edge = -1 if top else rows - 1
    conv_rows(w_ref[7], g3, 0, 2, lambda row, total: dhidden1(edge + row, total))

    def next_g(row, total):
        keep_edge(row, (one(g_ref, start + row).astype(F32) + total).astype(BF16))

    conv_rows(w_ref[5], d3, 0, 2, next_g)


def backward1_near_kernel(
    rows, g_ref, near_ref, hid1_near, hid1_in, inner_ref, w_ref, dh1_ref, edge_ref, g3, d3
):
    def near_side(top):
        def hid1_row(row):
            if 3 <= row < rows - 3:
                return one(hid1_in, row - 3)
            return one(hid1_near, row + 1 if top else row - (rows - 3))

        def keep_dh1(row, value):
            at = row + 1 if top else row - 3
            dh1_ref[at * CHAN : (at + 1) * CHAN, :] = value

        def keep_edge(row, value):
            edge_ref[row * CHAN : (row + 1) * CHAN, :] = value

        inner_rows = range(1, rows - 3) if top else range(3, rows - 1)
        backward_side(
            rows, top, g_ref, near_ref, hid1_row, inner_ref, w_ref, inner_rows, keep_dh1, keep_edge, g3, d3
        )

    odd = odd_place()
    for top in (True, False):
        pl.when(odd == top)(functools.partial(near_side, top))


def backward1_far_kernel(
    rows, g_ref, far_ref, hid1_ref, inner_ref, w_ref, dh1_near, edge_near,
    next_near, next_far, edges_ref, dh1_ref, g3, d3,
):
    def far_side(top):
        def keep_dh1(row, value):
            dh1_ref[(row + 1) * CHAN : (row + 2) * CHAN, :] = value

        def keep_edge(row, value):
            at = row if top else 2 + row
            edges_ref[at * CHAN : (at + 1) * CHAN, :] = value

        inner_rows = (1, 2) if top else (rows - 3, rows - 2)
        backward_side(
            rows, top, g_ref, far_ref, lambda row: one(hid1_ref, row + 1), inner_ref, w_ref, inner_rows,
            keep_dh1, keep_edge, g3, d3,
        )
        copy_rows(dh1_near, rows - 2, dh1_ref, 4 if top else 0)
        copy_rows(edge_near, 2, edges_ref, 2 if top else 0)

    odd = odd_place()
    for top in (True, False):
        pl.when(odd != top)(functools.partial(far_side, top))
    send_edges(edges_ref, 1, next_near, next_far)


def grads_near_kernel(
    rows, g_ref, hid1_near, hid1_in, dh1_near, x1_near, x1_in, grad11, grad10, s3, t3, hid1, x1
):
    def near_side(top):
        start = 0 if top else rows - 4
        for i in range(4):
            put(s3, i, one(g_ref, start + i))
            put(t3, i, one(dh1_near, start + i + 1 if top else start + i - 3))
        for i in range(6):
            row = start - 1 + i
            if 3 <= row < rows - 3:
                value = one(hid1_in, row - 3)
            else:
                value = one(hid1_near, row + 1 if top else row - (rows - 3))
            hid1[i * CHAN : (i + 1) * CHAN, :] = value
            if 2 <= row < rows - 2:
                value = one(x1_in, row - 2)
            else:
                value = one(x1_near, row + 2 if top else row - (rows - 2))
            x1[i * CHAN : (i + 1) * CHAN, :] = value
        grad11[...] = grad_rows(s3, 0, hid1, 0, 4)
        grad10[...] = grad_rows(t3, 0, x1, 0, 4)

    odd = odd_place()
    for top in (True, False):
        pl.when(odd == top)(functools.partial(near_side, top))


def grad_rows_from(upper, upper_row, lower, lower_row, count):
    total = None
    for row in range(0, count, 2):
        left = pl.ds(pl.multiple_of((row + upper_row) * STACK, CHAN), 2 * STACK)
        right = pl.ds(pl.multiple_of((row + lower_row) * CHAN, CHAN), 4 * CHAN)
        term = lax.dot_general(
            upper[left, :], lower[right, :], (((1,), (1,)), ((), ())), preferred_element_type=F32
        )
        total = term if total is None else total + term
    return total[:STACK, :STACK] + total[STACK:, CHAN:]


def middle_kernel(
    rows, g_ref, edges_ref, hid1_ref, dh1_ref, x1_ref, hid0_ref, x_ref, w_ref, near11, near10,
    g1_ref, dh0_ref, grad00, grad01, grad10, grad11, s3, t3, u3, v3,
):
    stack_rows(dh1_ref, range(1, rows + 1), t3, 0)
    copy_rows(edges_ref, 2, g1_ref, 0)
    g1_ref[(rows - 2) * CHAN :, :] = edges_ref[2 * CHAN :, :]

    def next_g(row, total):
        value = (one(g_ref, row).astype(F32) + total).astype(BF16)
        g1_ref[row * CHAN : (row + 1) * CHAN, :] = value
        put(u3, row, value)

    conv_rows(w_ref[5], t3, 2, rows - 4, next_g)
    stack_rows(g1_ref, (0, 1, rows - 2, rows - 1), u3, 0)

    def dhidden0(row, total):
        value = jnp.where(one(hid0_ref, row + 2) > 0, total, 0.0).astype(BF16)
        dh0_ref[row * CHAN : (row + 1) * CHAN, :] = value
        put(v3, row, value)

    conv_rows(w_ref[3], u3, 0, rows - 2, dhidden0)
    start = jnp.where(odd_place(), 4, 0)
    for row in range(rows - 4):
        source = pl.ds(pl.multiple_of((start + row) * CHAN, CHAN), CHAN)
        put(s3, row, g_ref[source, :])
    grad11[...] = near11[...] + grad_rows_from(s3, 0, hid1_ref, start, rows - 4)
    grad10[...] = near10[...] + grad_rows_from(t3, start + 1, x1_ref, start, rows - 4)
    grad01[...] = grad_rows(u3, 0, hid0_ref, 0, rows)
    grad00[...] = grad_rows(v3, 0, x_ref, 0, rows - 2)


def output_kernel(rows, hid1_ref, x1_ref, w_ref, out_ref, k3, wide):
    stack_rows(hid1_ref, range(rows + 2), k3, 0)

    def last_x(row, total):
        wide[row] = one(x1_ref, row + 1).astype(F32) + total

    conv_rows(w_ref[6], k3, 0, rows, last_x)
    channels_first(wide, out_ref)


def backward0_kernel(
    rows, scale, g1_ref, near_ref, far_ref, hid0_ref, x_ref, xnear_ref, xfar_ref, w_ref, inner00,
    grad01, grad10, grad11, next_near, next_far, keep_ref, send_ref,
    d0, g3, d3, xs, both,
):
    odd = odd_place()
    near_at, far_at = jnp.where(odd, 0, 5), jnp.where(odd, 5, 0)
    put_at(g3, near_at, one(near_ref, 0))
    put_at(g3, far_at, one(far_ref, 0))
    stack_rows(g1_ref, (0, 1), g3, 1)
    stack_rows(g1_ref, (rows - 2, rows - 1), g3, 5 - rows)
    copy_rows(x_ref, 2, xs, 1)
    xs[3 * CHAN : 5 * CHAN, :] = x_ref[(rows - 2) * CHAN :, :]
    near_row, far_row = jnp.where(odd, 3, 0), jnp.where(odd, 0, 3)
    for ref, at, row in ((xnear_ref, near_at, near_row), (xfar_ref, far_at, far_row)):
        source = pl.ds(pl.multiple_of(row * CHAN, CHAN), CHAN)
        xs[pl.ds(pl.multiple_of(at * CHAN, CHAN), CHAN), :] = ref[source, :]
    grad00 = inner00[...]
    for end, row in ((0, 0), (1, rows - 1)):
        total = jnp.dot(
            w_ref[3, :CHAN, : 3 * STACK],
            g3[3 * end * STACK : 3 * (end + 1) * STACK, :],
            preferred_element_type=F32,
        )
        value = jnp.where(one(hid0_ref, row + 1) > 0, total, 0.0).astype(BF16)
        d0[end * CHAN : (end + 1) * CHAN, :] = value
        put(d3, end, value)
    for end in range(2):
        grad00 = grad00 + lax.dot_general(
            d3[end * STACK : (end + 1) * STACK, :],
            xs[end * STACK : (end + 1) * STACK, :],
            (((1,), (1,)), ((), ())),
            preferred_element_type=F32,
        )
    send_edges(d0, 1, next_near, next_far)
    pairs = ((grad00, grad01[...]), (grad10[...], grad11[...]))
    for section, pair in enumerate(pairs):
        for which, value in enumerate(pair):
            for a in range(3):
                for b in range(3):
                    block = value[(2 - b) * CHAN : (3 - b) * CHAN, a * CHAN : (a + 1) * CHAN]
                    at = which * 9 * CHAN + (3 * a + b) * CHAN
                    both[section, :, at : at + CHAN] = block * scale
    mine = lax.rem(lax.axis_index("space"), 2)
    keep_ref[...] = both[mine]
    send_ref[...] = both[1 - mine].astype(BF16)


def input_grad_kernel(rows, dh0_in, own_near, own_far, near_ref, far_ref, g1_ref, w_ref, out_ref, d3, wide):
    halo_rows(near_ref, far_ref, 1, rows, d3)
    stack_rows(dh0_in, range(rows - 2), d3, 2)
    odd = odd_place()
    put_at(d3, jnp.where(odd, 1, rows), one(own_near, 0))
    put_at(d3, jnp.where(odd, rows, 1), one(own_far, 0))

    def last_g(row, total):
        wide[row] = one(g1_ref, row).astype(F32) + total

    conv_rows(w_ref[1], d3, 0, rows, last_g)
    channels_first(wide, out_ref)


def halved_kernel(part_ref, other_ref, keep_ref, send_ref):
    low, high = (
        part_ref[at : at + CHAN // 2, :] + other_ref[at : at + CHAN // 2, :].astype(F32)
        for at in (0, CHAN // 2)
    )
    bit = lax.rem(lax.axis_index("space"), 4) >= 2
    keep_ref[...] = jnp.where(bit, high, low)
    send_ref[...] = jnp.where(bit, low, high).astype(BF16)


def gathered_kernel(own_ref, other_ref, out_ref):
    mine = lax.rem(lax.axis_index("space"), 2)
    for section, ref in ((mine, own_ref), (1 - mine, other_ref)):
        for which in range(2):
            piece = ref[:, which * 9 * CHAN : (which + 1) * 9 * CHAN]
            out_ref[section, which] = piece.astype(F32)

def exchange(value, mask, count):
    return lax.ppermute(value, "space", [(d, d ^ mask) for d in range(count)])


def local(features, cotangent, kernels):
    rows, width = features.shape[1], features.shape[2]
    count = lax.axis_size("space")
    height = rows * count
    scale = 1.0 / math.sqrt(height * width)
    place = lax.axis_index("space")
    beyond = [(i, i + 1) for i in range(1, count - 1, 2)]
    beyond += [(target, source) for source, target in beyond]

    def shape(n, dtype=BF16):
        return jax.ShapeDtypeStruct((n * CHAN, width), dtype)

    def vmem(n):
        return pltpu.VMEM((n * STACK, width), BF16)

    def plain(n):
        return pltpu.VMEM((n * CHAN, width), BF16)

    def neighbours(near, far):
        from_far = lax.ppermute(far, "space", beyond)
        return exchange(near, 1, count), from_far

    row_flops = 2 * CHAN * 9 * CHAN * width * 4
    grad = jax.ShapeDtypeStruct((STACK, STACK), F32)
    tile = jax.ShapeDtypeStruct((CHAN, rows, width), BF16)
    wide = pltpu.VMEM((rows, CHAN, width), F32)
    half = (CHAN, 18 * CHAN)

    x, x_near, x_far = call(
        functools.partial(entry_kernel, 4), (features,), (shape(rows), shape(4), shape(4)),
        [], 0, "x_rows", place=VMEM,
    )
    xnear, xfar = neighbours(x_near, x_far)
    (weights,) = call(
        weights_kernel, (kernels,), (jax.ShapeDtypeStruct((8, 2 * CHAN, 4 * STACK), BF16),), [],
        row_flops, "weights", after=(x_far,),
    )
    inner = call(
        functools.partial(inner_kernel, rows), (x, weights),
        (shape(rows - 2), shape(rows - 4), shape(rows - 6)),
        [vmem(rows), vmem(rows - 2), vmem(rows - 4)], 12 * row_flops, "inner",
    )
    g, g_near, g_far, g_inner = call(
        functools.partial(g_entry_kernel, 2), (cotangent, weights),
        (shape(rows), shape(2), shape(2), shape(rows - 2, F32)),
        [vmem(rows)], 6 * row_flops, "g_rows", after=(inner[2],), place=VMEM,
    )
    gnear, gfar = neighbours(g_near, g_far)
    near = call(
        functools.partial(near_kernel, rows, height), (x, xnear, weights, inner[0], inner[1]),
        (shape(4),) * 3, [vmem(6)] * 3, 12 * row_flops, "forward_near", after=(g_near,),
    )
    dh1_near, edge_near = call(
        functools.partial(backward1_near_kernel, rows),
        (g, gnear, near[2], inner[2], g_inner, weights), (shape(rows - 2), shape(2)),
        [vmem(4)] * 2, 4 * row_flops, "backward1_near",
    )
    near_grads = call(
        functools.partial(grads_near_kernel, rows),
        (g, near[2], inner[2], dh1_near, near[1], inner[1]), (grad, grad),
        [vmem(4), vmem(4), plain(6), plain(6)], 8 * row_flops, "grads_near", after=(edge_near,),
    )
    hid0, x1, hid1 = call(
        functools.partial(far_kernel, rows, height), (x, xfar, weights, *inner, *near),
        (shape(rows + 2),) * 3, [plain(4)] * 3 + [vmem(6)] * 3, 12 * row_flops, "forward_far",
        after=(near_grads[1],),
    )
    g1_near, g1_far, edges, dh1 = call(
        functools.partial(backward1_far_kernel, rows),
        (g, gfar, hid1, g_inner, weights, dh1_near, edge_near),
        (shape(1), shape(1), shape(4), shape(rows + 2)), [vmem(4)] * 2, 4 * row_flops, "backward1_far",
    )
    g1near, g1far = neighbours(g1_near, g1_far)
    g1, dh0_inner, *grads = call(
        functools.partial(middle_kernel, rows), (g, edges, hid1, dh1, x1, hid0, x, weights, *near_grads),
        (shape(rows), shape(rows - 2)) + (grad,) * 4,
        [vmem(rows - 4), vmem(rows + 2), vmem(rows), vmem(rows - 2)],
        36 * row_flops, "middle",
    )
    dh0_near, dh0_far, part, send = call(
        functools.partial(backward0_kernel, rows, scale),
        (g1, g1near, g1far, hid0, x, xnear, xfar, weights, *grads),
        (shape(1), shape(1), jax.ShapeDtypeStruct(half, F32),
         jax.ShapeDtypeStruct(half, BF16)),
        [plain(2), vmem(6), vmem(2), plain(6),
         pltpu.VMEM((2, *half), F32)],
        8 * row_flops, "backward0",
    )

    quarter = (CHAN // 2, 18 * CHAN)
    part, send = call(
        halved_kernel, (part, exchange(send, 1, count)),
        (jax.ShapeDtypeStruct(quarter, F32), jax.ShapeDtypeStruct(quarter, BF16)), [], 0, "halved",
    )
    arrived = exchange(send, 2, count)
    dh0_near, dh0_far, _ = lax.optimization_barrier((dh0_near, dh0_far, send))
    dh0near, dh0far = neighbours(dh0_near, dh0_far)
    part = part + arrived.astype(F32)
    step = 4
    section_output = None
    while step < count:
        send = part.astype(BF16)
        masks = [step, 2 * step, 3 * step] if 2 * step < count else [step]
        arrived = [exchange(send, mask, count) for mask in masks]
        if section_output is None:
            (section_output,) = call(
                functools.partial(output_kernel, rows), (hid1, x1, weights), (tile,),
                [vmem(rows + 2), wide], 8 * row_flops, "output", after=(send,),
            )
            arrived, section_output = lax.optimization_barrier((arrived, section_output))
        own = send.astype(F32)
        arrived = [value.astype(F32) for value in arrived]
        part = own + arrived[0]
        if len(masks) == 3:
            part = part + (arrived[1] + arrived[2])
        step *= len(masks) + 1
    done = part.astype(BF16)
    bit = (place & 2) != 0
    other = exchange(done, 2, count)
    (input_grad,) = call(
        functools.partial(input_grad_kernel, rows), (dh0_inner, dh0_near, dh0_far, dh0near, dh0far, g1, weights),
        (tile,),
        [vmem(rows + 2), wide], 8 * row_flops, "input_grad", after=(done,),
    )
    other, input_grad = lax.optimization_barrier((other, input_grad))
    done = jnp.where(bit, jnp.concatenate([other, done]), jnp.concatenate([done, other]))
    (kernel_grad,) = call(
        gathered_kernel, (done, exchange(done, 1, count)),
        (jax.ShapeDtypeStruct((2, 2, CHAN, 9 * CHAN), F32),), [], 0, "gathered",
    )
    return (section_output, input_grad, kernel_grad)


def solution(mesh):
    return jax.shard_map(
        local,
        mesh=mesh,
        in_specs=(P(None, "space", "groups"), P(None, "space", "groups"), P()),
        out_specs=(
            P(None, "space", "groups"),
            P(None, "space", "groups"),
            P("groups", None, None, None),
        ),
        check_vma=False,
    )
```
